32 devices in a mesh: batch: 8 (over y, x, core), seq: 4 (over z).
Axes of the slice: x: 2, y: 2, z: 4, core: 2. Of those that a mesh axis runs over, the one named last changes fastest.
Arguments:
- tokens: bfloat16 [8, 1024, 2048], P('batch', 'seq'), may hold values from -6 to 6
- segments: int32 [8, 1024], P('batch'), may hold values from 0 to 7, never falling along the last dimension, each value on 1 to 512 neighbouring positions
- valid_count: int32 [8], P('batch'), may hold values from 256 to 1024, as said below
- cotangent: bfloat16 [8, 1024, 2048], P('batch', 'seq'), may hold values from -6 to 6
- w_qkv: bfloat16 [2048, 6144], P(('batch', 'seq')), may hold values from -0.125 to 0.125
- w_out: bfloat16 [2048, 2048], P(None, ('batch', 'seq')), may hold values from -0.125 to 0.125
- w_up: bfloat16 [2048, 8192], P(('batch', 'seq')), may hold values from -0.125 to 0.125
- w_down: bfloat16 [8192, 2048], P(None, ('batch', 'seq')), may hold values from -0.0625 to 0.0625
- gain_attn: bfloat16 [2048], P(('batch', 'seq')), may hold values from 0.5 to 1.5
- bias_attn: bfloat16 [2048], P(('batch', 'seq')), may hold values from -1.1953125 to 1.1953125
- gain_mix: bfloat16 [2048], P(('batch', 'seq')), may hold values from 0.5 to 1.5
- bias_mix: bfloat16 [2048], P(('batch', 'seq')), may hold values from -1.1953125 to 1.1953125
- gain_ffn: bfloat16 [2048], P(('batch', 'seq')), may hold values from 0.5 to 1.5
- bias_ffn: bfloat16 [2048], P(('batch', 'seq')), may hold values from -1.1953125 to 1.1953125
- gain_hidden: bfloat16 [8192], P(('batch', 'seq')), may hold values from 0.5 to 1.5
- bias_hidden: bfloat16 [8192], P(('batch', 'seq')), may hold values from -1.1953125 to 1.1953125
Outputs:
- output: bfloat16 [8, 1024, 2048], P('batch', 'seq')
- grad_tokens: float32 [8, 1024, 2048], P('batch', 'seq')
- grad_w_qkv: float32 [2048, 6144], P(('batch', 'seq'))
- grad_w_out: float32 [2048, 2048], P(None, ('batch', 'seq'))
- grad_w_up: float32 [2048, 8192], P(('batch', 'seq'))
- grad_w_down: float32 [8192, 2048], P(None, ('batch', 'seq'))
- grad_gain_attn: float32 [2048], P(('batch', 'seq'))
- grad_bias_attn: float32 [2048], P(('batch', 'seq'))
- grad_gain_mix: float32 [2048], P(('batch', 'seq'))
- grad_bias_mix: float32 [2048], P(('batch', 'seq'))
- grad_gain_ffn: float32 [2048], P(('batch', 'seq'))
- grad_bias_ffn: float32 [2048], P(('batch', 'seq'))
- grad_gain_hidden: float32 [8192], P(('batch', 'seq'))
- grad_bias_hidden: float32 [8192], P(('batch', 'seq'))
The draws below stay inside these ranges and needn't reach their ends.
Inputs may be any that keep to these rules, and one draw needn't show every extreme that they name: `segments`: in each row the segment id never falls along the slots; each id covers 1 to 512 slots. `valid_count`: in every draw some row has all 1024 slots used.
All inputs are finite; a program needn't handle non-finite values.
Results may differ from the reference program's by a relative error of at most 0.015.
Values may be sent and summed in bfloat16 or wider, within the bound.
No kernel may reach another device: no remote copies, remote signals or barrier semaphores. Data moves between devices by JAX's collectives and lax.ppermute only.
A program may use at most 640 MiB of HBM per device.

```python
import math
import jax
import jax.numpy as jnp
import numpy as np
from jax import lax

D = 2048
FF = 8192
LENGTH = 1024
DOCS = 8
ROWS = 8


def draw_valid_count(key, part):
    first_key, second_key, third_key = jax.random.split(key, 3)
    half = LENGTH // 2
    left = jax.random.randint(first_key, (ROWS,), 0, half + 1)
    right = jax.random.randint(second_key, (ROWS,), 0, half + 1)
    shortfall = left * right // max(half, 1) * 3 // 2
    full_row = jax.random.randint(third_key, (), 0, ROWS)
    return jnp.where(jnp.arange(ROWS) == full_row, LENGTH, LENGTH - shortfall).astype(jnp.int32)


def level_of(key, extent, pieces, least, largest):
    level, own = 1.0, jax.random.fold_in(key, 6)
    for dim, blocks in pieces:
        steps = jnp.exp(jax.random.uniform(jax.random.fold_in(own, dim), (blocks,), jnp.float32, least / len(pieces), largest / len(pieces)))
        level = level * jnp.repeat(steps, extent[dim] // blocks).reshape([-1 if axis == dim else 1 for axis in range(len(extent))])
    return level


def split_up(amount, total, limit, skew):
    loads = [(1 << 20) // math.isqrt(standing ** skew) + 1 for standing in range(2, amount + 1)]
    rest, counts = total - limit - (amount - 1), [1] * (amount - 1)
    while rest > 0:
        free = [i for i in range(amount - 1) if counts[i] < limit]
        whole, budget = sum([loads[i] for i in free]), rest
        for i in free:
            more = min(limit - counts[i], max(1, budget * loads[i] // whole), rest)
            counts[i] = counts[i] + more
            rest = rest - more
    return np.array([limit] + counts)


def uneven(key, number_of, total, bound, slope):
    if number_of == 2:
        one = jax.random.randint(key, (), max(1, total - bound), min(bound, total - 1) + 1)
        return jnp.stack([one, total - one])
    lengths = jnp.asarray(split_up(number_of, total, bound, slope), jnp.int32)
    twos = (number_of - 1) // 2
    giver, taker = lengths[1:1 + 2 * twos:2], lengths[2:2 + 2 * twos:2]
    slack = jnp.minimum(giver - 1, bound - taker)
    shifted = jax.random.randint(jax.random.fold_in(key, 1), (twos,), 0, 1 << 20) % (slack + 1)
    lengths = lengths.at[1:1 + 2 * twos:2].set(giver - shifted).at[2:2 + 2 * twos:2].set(taker + shifted)
    return lengths[jax.random.permutation(jax.random.fold_in(key, 2), number_of)]


def scatter_about(rng, shape, deviation, bound, shards=(), kind=jnp.bfloat16):
    level = level_of(rng, shape, shards, -0.22, 0.18) if shards else 1.0
    values = jax.random.normal(rng, shape, jnp.float32) * deviation * level
    return jnp.minimum(jnp.maximum(values, -bound), bound).astype(kind)


def setup_inputs(seed: int = 0) -> dict:
    key_of = jax.random.split(jax.random.key(seed), 17)
    return {
        "tokens": scatter_about(key_of[0], (ROWS, LENGTH, D), 1.0, 6.0, ((0, 8), (1, 4))),
        "segments": jax.vmap(lambda own: jnp.searchsorted(jnp.cumsum(uneven(own, DOCS, LENGTH, LENGTH // 2, 2)), jnp.arange(LENGTH), side="right"))(jax.random.split(key_of[1], ROWS)).reshape((ROWS, LENGTH)).astype(jnp.int32),
        "valid_count": draw_valid_count(jax.random.fold_in(key_of[16], 71), 0),
        "cotangent": scatter_about(key_of[3], (ROWS, LENGTH, D), 1.0, 6.0, ((0, 8), (1, 4))),
        "w_qkv": scatter_about(key_of[4], (D, 3 * D), D ** -0.5, 0.125, ((0, 32),)),
        "w_out": scatter_about(key_of[5], (D, D), D ** -0.5, 0.125, ((1, 32),)),
        "w_up": scatter_about(key_of[6], (D, FF), D ** -0.5, 0.125, ((0, 32),)),
        "w_down": scatter_about(key_of[7], (FF, D), FF ** -0.5, 0.0625, ((1, 32),)),
        "gain_attn": jnp.clip(1.0 + 0.1 * jax.random.normal(key_of[8], (D,), jnp.float32), 0.5, 1.5).astype(jnp.bfloat16),
        "bias_attn": scatter_about(key_of[9], (D,), 0.3, 1.1953125, ((0, 32),)),
        "gain_mix": jnp.clip(1.0 + 0.1 * jax.random.normal(key_of[10], (D,), jnp.float32), 0.5, 1.5).astype(jnp.bfloat16),
        "bias_mix": scatter_about(key_of[11], (D,), 0.3, 1.1953125, ((0, 32),)),
        "gain_ffn": jnp.clip(1.0 + 0.1 * jax.random.normal(key_of[12], (D,), jnp.float32), 0.5, 1.5).astype(jnp.bfloat16),
        "bias_ffn": scatter_about(key_of[13], (D,), 0.3, 1.1953125, ((0, 32),)),
        "gain_hidden": jnp.clip(1.0 + 0.1 * jax.random.normal(key_of[14], (FF,), jnp.float32), 0.5, 1.5).astype(jnp.bfloat16),
        "bias_hidden": scatter_about(key_of[15], (FF,), 0.3, 1.1953125, ((0, 32),)),
    }


@jax.custom_vjp
def low(v):
    return lax.optimization_barrier(v.astype(jnp.bfloat16)).astype(jnp.float32)

@jax.custom_vjp
def low_back(v):
    return v

def low_keep(v):
    return (low(v), None)

def low_pass(kept, grad):
    return (grad,)

def back_keep(v):
    return (v, None)

def back_low(kept, grad):
    return (low(grad),)
low.defvjp(low_keep, low_pass)
low_back.defvjp(back_keep, back_low)
EPSILON = 1e-05
PRECISE = lax.Precision.HIGHEST

def layer_norm(values, gain, bias):
    center = values - lax.optimization_barrier(jnp.mean(values, axis=-1, keepdims=True))
    spread = lax.optimization_barrier(jnp.mean(center * center, axis=-1, keepdims=True))
    return center * lax.rsqrt(spread + EPSILON) * gain + bias

def xpos_tables(first, count, total):
    slot_pos = (first + jnp.arange(count, dtype=jnp.int32) - total // 2).astype(jnp.float32)
    index = jnp.arange(32, dtype=jnp.int32).astype(jnp.float32)
    angle = slot_pos[:, None] * jnp.exp(index * (-jnp.log(10000.0) / 32.0))[None, :]
    zeta = (index / 32.0 + 0.4) / 1.4
    growth = jnp.exp(slot_pos[:, None] * jnp.log(zeta)[None, :] / 512.0)
    return (jnp.cos(angle), jnp.sin(angle), growth)

def rotate(head_view, cosine, sine, growth):
    lower = head_view[..., :32]
    upper = head_view[..., 32:]
    cosine = cosine[:, None, :]
    sine = sine[:, None, :]
    growth = growth[:, None, :]
    return jnp.concatenate([(lower * cosine - upper * sine) * growth, (upper * cosine + lower * sine) * growth], axis=-1)

def allowed_mask(query_slots, key_slots, seg_query, seg_key, valid_len):
    same = seg_query[:, None] == seg_key[None, :]
    before = key_slots[None, :] <= query_slots[:, None]
    living = (query_slots < valid_len)[:, None]
    return (key_slots[None, :] == query_slots[:, None]) | same & before & living

def row_forward(x_row, seg_row, valid_len, weights):
    w_qkv, w_out, w_up, w_down, gain_attn, bias_attn, gain_mix, bias_mix, gain_ffn, bias_ffn, gain_hidden, bias_hidden = weights
    length = x_row.shape[0]
    heads = D // 64
    normed = low(layer_norm(x_row, gain_attn, bias_attn))
    projected = low_back(jnp.dot(normed, w_qkv, precision=PRECISE))
    cosine, sine, growth = xpos_tables(0, length, length)
    queries = low(rotate(projected[:, :D].reshape(length, heads, 64), cosine, sine, growth))
    key_rows = low(rotate(projected[:, D:2 * D].reshape(length, heads, 64), cosine, sine, 1.0 / growth))
    value_rows = low(projected[:, 2 * D:].reshape(length, heads, 64))
    block = min(512, length)
    slots_all = jnp.arange(length, dtype=jnp.int32)

    def attend(start):
        query_block = lax.dynamic_slice_in_dim(queries, start, block, 0)
        query_slots = start + jnp.arange(block, dtype=jnp.int32)
        seg_query = lax.dynamic_slice_in_dim(seg_row, start, block, 0)
        allowed = allowed_mask(query_slots, slots_all, seg_query, seg_row, valid_len)
        scores = jnp.einsum('qhd,khd->hqk', query_block, key_rows, precision=PRECISE) * 0.125
        scores = jnp.where(allowed[None], scores, -1e+30)
        top = lax.optimization_barrier(jnp.max(scores, axis=-1, keepdims=True))
        weight = jnp.where(allowed[None], jnp.exp(scores - top), 0.0)
        weight = weight / lax.optimization_barrier(jnp.sum(weight, axis=-1, keepdims=True))
        return jnp.einsum('hqk,khd->qhd', weight, value_rows, precision=PRECISE)
    starts = jnp.arange(length // block, dtype=jnp.int32) * block
    attended = lax.map(jax.checkpoint(attend), starts).reshape(length, D)
    mixed = low(layer_norm(attended, gain_mix, bias_mix))
    resid_mid = x_row + low_back(jnp.dot(mixed, w_out, precision=PRECISE))
    ffn_in = low(layer_norm(resid_mid, gain_ffn, bias_ffn))
    hidden = low_back(jnp.dot(ffn_in, w_up, precision=PRECISE))
    hidden_normed = low(layer_norm(jax.nn.gelu(hidden, approximate=False), gain_hidden, bias_hidden))
    return resid_mid + low_back(jnp.dot(hidden_normed, w_down, precision=PRECISE))

def reference(tokens, segments, valid_count, cotangent, w_qkv, w_out, w_up, w_down, gain_attn, bias_attn, gain_mix, bias_mix, gain_ffn, bias_ffn, gain_hidden, bias_hidden):
    weights = tuple((weight.astype(jnp.float32) for weight in (w_qkv, w_out, w_up, w_down, gain_attn, bias_attn, gain_mix, bias_mix, gain_ffn, bias_ffn, gain_hidden, bias_hidden)))
    living = (jnp.arange(LENGTH, dtype=jnp.int32)[None, :] < valid_count[:, None]).astype(jnp.float32)
    grad_out = cotangent.astype(jnp.float32) * living[:, :, None]

    def forward(inputs, params):

        def one_row(packed):
            x_row, seg_row, valid_len = packed
            return row_forward(x_row, seg_row, valid_len, params)
        return lax.map(jax.checkpoint(one_row), (inputs, segments, valid_count))
    result, pull = jax.vjp(forward, tokens.astype(jnp.float32), weights)
    grad_inputs, grads = pull(grad_out)
    return (result.astype(jnp.bfloat16), grad_inputs, grads[0], grads[1], grads[2], grads[3], grads[4], grads[5], grads[6], grads[7], grads[8], grads[9], grads[10], grads[11])
```

```python
import functools

import jax
import jax.numpy as jnp
import numpy as np
from jax import lax
from jax.experimental import pallas as pl
from jax.experimental.pallas import tpu as pltpu
from jax.sharding import PartitionSpec as P

EPSILON = 1e-05
HEAD = 64
STRIPE = 256
LOW = jnp.bfloat16
WIDE = jnp.float32
BOTH = ("batch", "seq")

LAYER = (2, 0, 1, 2, 1, 3, 3, 0)
PLACE = (1, 1, 1, 0, 0, 1, 0, 0)
TURN = ((1, 1), (3, 2), (0, 2), (3, 1))


class Plan:
    def __init__(self, nb, ns):
        self.nb, self.ns = nb, ns
        self.rows = nb // ns
        self.fast = nb == 8 and ns == 4
        if self.fast:
            layer, place, turn = LAYER, PLACE, TURN
        else:
            layer = [b // self.rows for b in range(nb)]
            place = [b % self.rows for b in range(nb)]
            turn = [[0] * self.rows for _ in range(ns)]
        self.there = []
        for b in range(nb):
            for s in range(ns):
                k, p = layer[b], place[b]
                target = ((s ^ turn[k][p]) * self.rows + p) * ns + k
                self.there.append((b * ns + s, target))
        self.back = [(d, s) for s, d in self.there]
        row_of = {(layer[b], place[b]): b for b in range(nb)}
        table = []
        for b in range(nb):
            for k in range(ns):
                c, t = b % self.rows, b // self.rows
                order = [c, 1 - c] if self.fast else list(range(self.rows))
                entry = [t ^ turn[k][c]] + [row_of[k, p] for p in order]
                for p in order:
                    for q in range(ns):
                        entry.append(q ^ t ^ turn[k][p] if self.fast else q ^ turn[k][p])
                table.append(entry)
        self.table = np.array(table, np.int32)


def swap_over(value, axis, step, size):
    return lax.ppermute(value, axis, [(i, i ^ step) for i in range(size)])


def bits(size):
    return [1 << i for i in range(size.bit_length() - 1)]


def sum_over(value, axis, size):
    for step in bits(size):
        value = value + swap_over(value, axis, step, size)
    return value


def aligned(plan, value, step):
    if not plan.fast:
        return value
    shape = value.shape
    axis = {1: 1, 4: 2, 2: 3}[step]
    return jnp.flip(value.reshape(shape[0], 2, 2, 2, shape[1] // 8), axis).reshape(shape)


def gather_over(value, axis, size):
    index = lax.axis_index(axis)
    value = value[None]
    for step in bits(size):
        other = swap_over(value, axis, step, size)
        upper = (index & step) != 0
        value = jnp.concatenate(
            [jnp.where(upper, other, value), jnp.where(upper, value, other)], axis=0
        )
    return value


def gather_blocks(plan, block):
    if not plan.fast:
        slots, width = block.shape
        full = lax.all_gather(block, "batch", axis=0, tiled=False)
        full = full.reshape(plan.nb // plan.rows, plan.rows, slots, width)
        return full.transpose(1, 0, 2, 3).reshape(plan.nb * slots, width)
    half = block.shape[1] // 2
    from_x = swap_over(block, "batch", 2, 8)
    from_y = swap_over(block, "batch", 4, 8)
    far_a = swap_over(from_x[:, :half], "batch", 4, 8)
    far_b = swap_over(from_y[:, half:], "batch", 2, 8)
    far = jnp.concatenate([far_a, far_b], axis=1)
    own = [block, from_x, from_y, far]
    other = [swap_over(piece, "batch", 1, 8) for piece in own]
    return jnp.concatenate(own + other, axis=0)


def reduce_blocks(plan, product, left):
    count = left.shape[0]
    if not plan.fast:
        part = product(left).astype(LOW)
        width = part.shape[1]
        slots = count // plan.nb
        part = part.reshape(plan.rows, plan.nb // plan.rows, slots, width).transpose(1, 0, 2, 3)
        return lax.psum_scatter(
            part.reshape(count, width), "batch", scatter_dimension=0, tiled=True
        ).astype(WIDE)
    other = swap_over(product(left[count // 2 :]).astype(LOW), "batch", 1, 8)
    mine = product(left[: count // 2]) + other.astype(WIDE)
    slots, width = count // 8, mine.shape[1]
    half = width // 2
    mine = mine.reshape(4, slots, width)
    near, at_x, at_y, far = mine[0], mine[1], mine[2], mine[3]
    to_y = swap_over(far[:, :half].astype(LOW), "batch", 2, 8).astype(WIDE)
    to_x = swap_over(far[:, half:].astype(LOW), "batch", 4, 8).astype(WIDE)
    x_a = swap_over(at_x[:, :half].astype(LOW), "batch", 2, 8).astype(WIDE)
    y_b = swap_over(at_y[:, half:].astype(LOW), "batch", 4, 8).astype(WIDE)
    x_b = swap_over((at_x[:, half:] + to_x).astype(LOW), "batch", 2, 8).astype(WIDE)
    y_a = swap_over((at_y[:, :half] + to_y).astype(LOW), "batch", 4, 8).astype(WIDE)
    return jnp.concatenate([near[:, :half] + x_a + y_a, near[:, half:] + x_b + y_b], axis=1)


def gather_weight(plan, shard):
    rows, width = shard.shape
    part = width // plan.nb
    pieces = shard.reshape(rows, plan.nb, part).transpose(1, 0, 2)
    pieces = lax.all_to_all(pieces, "batch", 0, 0, tiled=True)
    full = lax.all_gather(pieces, "seq", axis=1, tiled=True)
    return full.reshape(plan.nb * plan.ns * rows, part)


def scatter_weight(plan, part):
    total, width = part.shape
    rows = total // (plan.nb * plan.ns)
    own = lax.psum_scatter(
        part.astype(LOW).reshape(plan.nb, plan.ns * rows, width),
        "seq",
        scatter_dimension=1,
        tiled=True,
    )
    pieces = lax.all_to_all(own, "batch", 0, 0, tiled=True)
    return pieces.transpose(1, 0, 2).reshape(rows, plan.nb * width)


def norm_stats(values):
    mean = jnp.mean(values, axis=-1, keepdims=True)
    center = values - mean
    return mean, lax.rsqrt(jnp.mean(center * center, axis=-1, keepdims=True) + EPSILON)


def spread_stats(plan, values):
    count = values.shape[1]
    mean = jnp.mean(values, axis=-1)
    center = values - mean[:, None]
    square = jnp.sum(center * center, axis=-1)
    for step in bits(plan.nb):
        other = swap_over(jnp.stack([mean, square]), "batch", step, plan.nb)
        other = aligned(plan, other, step)
        gap = other[0] - mean
        mean = 0.5 * (mean + other[0])
        square = square + other[1] + gap * gap * (0.5 * count)
        count = 2 * count
    return mean[:, None], lax.rsqrt(square / count + EPSILON)[:, None]


def norm_back(upstream, gain, unit, scale):
    scaled = upstream * gain
    first = jnp.mean(scaled, axis=-1, keepdims=True)
    second = jnp.mean(scaled * unit, axis=-1, keepdims=True)
    grad = scale * (scaled - first - unit * second)
    return grad, jnp.sum(upstream * unit, axis=0), jnp.sum(upstream, axis=0)


def spread_norm_back(plan, upstream, gain, unit, scale):
    scaled = upstream * gain
    sums = jnp.stack([jnp.sum(scaled, axis=-1), jnp.sum(scaled * unit, axis=-1)])
    for step in bits(plan.nb):
        sums = sums + aligned(plan, swap_over(sums, "batch", step, plan.nb), step)
    sums = sums / (upstream.shape[1] * plan.nb)
    grad = scale * (scaled - sums[0][:, None] - unit * sums[1][:, None])
    return grad, jnp.sum(upstream * unit, axis=0), jnp.sum(upstream, axis=0)


def xpos_tables(length):
    slot_pos = (jnp.arange(length, dtype=jnp.int32) - length // 2).astype(WIDE)
    index = jnp.arange(32, dtype=jnp.int32).astype(WIDE)
    angle = slot_pos[:, None] * jnp.exp(index * (-jnp.log(10000.0) / 32.0))[None, :]
    zeta = (index / 32.0 + 0.4) / 1.4
    growth = jnp.exp(slot_pos[:, None] * jnp.log(zeta)[None, :] / 512.0)
    cosine, sine = jnp.cos(angle), jnp.sin(angle)
    tables = []
    for scale in (growth, 1.0 / growth):
        tables += [cosine * scale] * 4
        tables += [-sine * scale, sine * scale] * 2
    return jnp.concatenate(tables, axis=1)


def swap_halves(values):
    lane = lax.broadcasted_iota(jnp.int32, values.shape, 1)
    return jnp.where(lane % 64 < 32, pltpu.roll(values, 96, 1), pltpu.roll(values, 32, 1))


def matmul(a, b, contract):
    return lax.dot_general(a, b, ((contract[:1], contract[1:]), ((), ())), preferred_element_type=WIDE)


def fill_bias(bias, valid, seg_row, seg_col, length):
    for i in range(length // STRIPE):
        low, high = i * STRIPE, (i + 1) * STRIPE
        shape = (STRIPE, high)
        query = lax.broadcasted_iota(jnp.int32, shape, 0) + low
        key = lax.broadcasted_iota(jnp.int32, shape, 1)
        same = seg_col[low:high] == seg_row[:, :high]
        allowed = (key == query) | (same & (key <= query) & (query < valid))
        bias[low:high, :high] = jnp.where(allowed, 0.0, -1e30)


def attend_kernel(info, proj, tables, seg_row, seg_col, qkv, attended, log_total, bias, *, ns, slots, hd):
    row, head = pl.program_id(0), pl.program_id(1)
    length = ns * slots

    def place(quarter):
        return pl.multiple_of(info[row, quarter] * slots, slots)

    @pl.when(head == 0)
    def _():
        for q in range(ns):
            source, low, high = place(q), q * slots, (q + 1) * slots
            for part in range(2):
                cosine = tables[low:high, 256 * part : 256 * part + 128]
                sine = tables[low:high, 256 * part + 128 : 256 * part + 256]
                for pair in range(hd // 128):
                    at = part * hd + pair * 128
                    values = proj[pl.ds(source, slots), at : at + 128]
                    turned = values * cosine + swap_halves(values) * sine
                    qkv[low:high, at : at + 128] = turned.astype(LOW)
            qkv[low:high, 2 * hd :] = proj[pl.ds(source, slots), 2 * hd :].astype(LOW)
        fill_bias(bias, info[row, ns], seg_row[...], seg_col[...], length)
        log_total[...] = jnp.zeros_like(log_total)

    mine = lax.broadcasted_iota(jnp.int32, (STRIPE, hd), 1) // HEAD == head
    column = lax.broadcasted_iota(jnp.int32, (STRIPE, 128), 1) == head
    for i in range(length // STRIPE):
        low, high = i * STRIPE, (i + 1) * STRIPE
        queries = jnp.where(mine, qkv[low:high, :hd], jnp.zeros((), LOW))
        scores = matmul(queries, qkv[:high, hd : 2 * hd], (1, 1)) * 0.125 + bias[low:high, :high]
        top = jnp.max(scores, axis=-1, keepdims=True)
        weight = jnp.exp(scores - top)
        total = jnp.sum(weight, axis=-1, keepdims=True)
        summed = matmul(weight.astype(LOW), qkv[:high, 2 * hd :], (1, 0)) / total
        log_total[low:high] = jnp.where(column, top + jnp.log(total), log_total[low:high])
        for u in range(STRIPE // slots):
            to = place(i * (STRIPE // slots) + u)
            rows = slice(u * slots, (u + 1) * slots)
            attended[pl.ds(to, slots), :] = jnp.where(
                mine[rows], summed[rows], attended[pl.ds(to, slots), :]
            )


def attend_back_kernel(
    info, qkv, attended, grad, log_total, tables, seg_row, seg_col, out,
    bias, grad_low, product, grad_q, grad_k, grad_v, *, ns, slots, hd
):
    row, head = pl.program_id(0), pl.program_id(1)
    length = ns * slots

    def place(quarter):
        return pl.multiple_of(info[row, quarter] * slots, slots)

    @pl.when(head == 0)
    def _():
        for q in range(ns):
            source, low, high = place(q), q * slots, (q + 1) * slots
            values = grad[pl.ds(source, slots), :]
            grad_low[low:high] = values.astype(LOW)
            product[low:high] = values * attended[pl.ds(source, slots), :]
        fill_bias(bias, info[row, ns], seg_row[...], seg_col[...], length)
        for total in (grad_q, grad_k, grad_v):
            total[...] = jnp.zeros_like(total)

    mine = lax.broadcasted_iota(jnp.int32, (STRIPE, hd), 1) // HEAD == head
    column = lax.broadcasted_iota(jnp.int32, (STRIPE, 128), 1) == head
    nothing = jnp.zeros((), LOW)
    mine_all = lax.broadcasted_iota(jnp.int32, (length, hd), 1) // HEAD == head
    keys_mine = jnp.where(mine_all, qkv[:, hd : 2 * hd], nothing)
    for i in range(length // STRIPE):
        low, high = i * STRIPE, (i + 1) * STRIPE
        queries = jnp.where(mine, qkv[low:high, :hd], nothing)
        upstream = jnp.where(mine, grad_low[low:high], nothing)
        delta = jnp.sum(jnp.where(mine, product[low:high], 0.0), axis=-1, keepdims=True)
        log_sum = jnp.sum(jnp.where(column, log_total[low:high], 0.0), axis=-1, keepdims=True)
        scores = matmul(queries, qkv[:high, hd : 2 * hd], (1, 1)) * 0.125 + bias[low:high, :high]
        prob = jnp.exp(scores - log_sum)
        grad_prob = matmul(upstream, qkv[:high, 2 * hd :], (1, 1))
        grad_s = (prob * (grad_prob - delta) * 0.125).astype(LOW)
        grad_q[low:high] += matmul(grad_s, keys_mine[:high], (1, 0))
        grad_k[:high] += matmul(grad_s, queries, (0, 0))
        grad_v[:high] += matmul(prob.astype(LOW), upstream, (0, 0))

    @pl.when(head == pl.num_programs(1) - 1)
    def _():
        for q in range(ns):
            target, low, high = place(q), q * slots, (q + 1) * slots
            for part, total in enumerate((grad_q, grad_k)):
                cosine = tables[low:high, 256 * part : 256 * part + 128]
                sine = tables[low:high, 256 * part + 128 : 256 * part + 256]
                for pair in range(hd // 128):
                    values = total[low:high, pair * 128 : pair * 128 + 128]
                    turned = values * cosine - swap_halves(values) * sine
                    at = part * hd + pair * 128
                    out[pl.ds(target, slots), at : at + 128] = turned.astype(LOW)
            out[pl.ds(target, slots), 2 * hd :] = grad_v[low:high].astype(LOW)


def row_block(length, width):
    return pl.BlockSpec((length, width), lambda r, h, info: (r, 0))


def shared_block(length, width):
    return pl.BlockSpec((length, width), lambda r, h, info: (0, 0))


def attend(plan, info, proj, tables, segments):
    count, width = proj.shape
    length, hd = count // plan.rows, width // 3
    slots = length // plan.ns
    return pl.pallas_call(
        functools.partial(attend_kernel, ns=plan.ns, slots=slots, hd=hd),
        grid_spec=pltpu.PrefetchScalarGridSpec(
            num_scalar_prefetch=1,
            grid=(plan.rows, hd // HEAD),
            in_specs=[
                row_block(length, width),
                shared_block(length, 512),
                pl.BlockSpec((None, 1, length), lambda r, h, info: (r, 0, 0)),
                pl.BlockSpec((None, length, 1), lambda r, h, info: (r, 0, 0)),
            ],
            out_specs=[row_block(length, width), row_block(length, hd), row_block(length, 128)],
            scratch_shapes=[pltpu.VMEM((length, length), WIDE)],
        ),
        out_shape=[
            jax.ShapeDtypeStruct((count, width), LOW),
            jax.ShapeDtypeStruct((count, hd), WIDE),
            jax.ShapeDtypeStruct((count, 128), WIDE),
        ],
        compiler_params=pltpu.CompilerParams(vmem_limit_bytes=48 << 20),
        name="attend",
    )(info, proj, tables, segments[:, None, :], segments[:, :, None])


def attend_back(plan, info, qkv, attended, grad, log_total, tables, segments):
    count, width = qkv.shape
    length, hd = count // plan.rows, width // 3
    slots = length // plan.ns
    return pl.pallas_call(
        functools.partial(attend_back_kernel, ns=plan.ns, slots=slots, hd=hd),
        grid_spec=pltpu.PrefetchScalarGridSpec(
            num_scalar_prefetch=1,
            grid=(plan.rows, hd // HEAD),
            in_specs=[
                row_block(length, width),
                row_block(length, hd),
                row_block(length, hd),
                row_block(length, 128),
                shared_block(length, 512),
                pl.BlockSpec((None, 1, length), lambda r, h, info: (r, 0, 0)),
                pl.BlockSpec((None, length, 1), lambda r, h, info: (r, 0, 0)),
            ],
            out_specs=row_block(length, width),
            scratch_shapes=[
                pltpu.VMEM((length, length), WIDE),
                pltpu.VMEM((length, hd), LOW),
                pltpu.VMEM((length, hd), WIDE),
                pltpu.VMEM((length, hd), WIDE),
                pltpu.VMEM((length, hd), WIDE),
                pltpu.VMEM((length, hd), WIDE),
            ],
        ),
        out_shape=jax.ShapeDtypeStruct((count, width), LOW),
        compiler_params=pltpu.CompilerParams(vmem_limit_bytes=48 << 20),
        name="attend_back",
    )(info, qkv, attended, grad, log_total, tables, segments[:, None, :], segments[:, :, None])


def shards(
    plan,
    tokens,
    segments,
    valid_count,
    cotangent,
    w_qkv,
    w_out,
    w_up,
    w_down,
    gain_attn,
    bias_attn,
    gain_mix,
    bias_mix,
    gain_ffn,
    bias_ffn,
    gain_hidden,
    bias_hidden,
):
    nb, ns = plan.nb, plan.ns
    width, slots, length = tokens.shape[2], tokens.shape[1], segments.shape[1]
    hd, hidden_part = width // nb, w_up.shape[1] // nb
    batch_index, seq_index = lax.axis_index("batch"), lax.axis_index("seq")
    entry = lax.dynamic_index_in_dim(
        jnp.asarray(plan.table), batch_index * ns + seq_index, 0, keepdims=False
    )

    tokens_low = lax.ppermute(tokens[0], BOTH, plan.there)
    slot = seq_index * slots + jnp.arange(slots, dtype=jnp.int32)
    living = (slot < valid_count[0])[:, None]
    grad_low = lax.ppermute(
        jnp.where(living, cotangent[0], jnp.zeros((), LOW)), BOTH, plan.there
    )

    group = w_qkv.reshape(w_qkv.shape[0], 3, nb, hd).transpose(0, 2, 1, 3)
    qkv_w = gather_weight(plan, group.reshape(w_qkv.shape))
    out_wt = gather_weight(plan, w_out.T)
    up_w = gather_weight(plan, w_up)
    down_wt = gather_weight(plan, w_down.T)

    own_params = (gain_attn, bias_attn, gain_mix, bias_mix, gain_ffn, bias_ffn, gain_hidden, bias_hidden)
    params = gather_over(jnp.concatenate([p.astype(WIDE) for p in own_params]), "seq", ns)
    packed = jnp.concatenate(
        [params.reshape(-1), segments[0].astype(WIDE), valid_count.astype(WIDE)]
    )
    packed = gather_over(packed, "batch", nb)
    spread = packed[:, : params.size].reshape(nb, ns, -1)
    vectors, at = [], 0
    for index, p in enumerate(own_params):
        piece = spread[:, :, at : at + p.shape[0]]
        at += p.shape[0]
        if index in (0, 1, 4, 5):
            vectors.append(piece.reshape(-1))
        else:
            vectors.append(lax.dynamic_index_in_dim(piece, batch_index, 0, False).reshape(-1))
    ga, ba, gm, bm, gf, bf, gh, bh = vectors
    layer_rows = packed[entry[1 : 1 + plan.rows], params.size :].astype(jnp.int32)
    seg_rows = layer_rows[:, :length]
    info = jnp.concatenate(
        [entry[1 + plan.rows :].reshape(plan.rows, ns), layer_rows[:, length:]], axis=1
    )
    tables = xpos_tables(length)

    resid = tokens_low.astype(WIDE)
    mean_attn, scale_attn = norm_stats(resid)
    unit_attn = (resid - mean_attn) * scale_attn
    normed = gather_blocks(plan, (unit_attn * ga + ba).astype(LOW))
    projected = matmul(normed, qkv_w, (1, 0))
    qkv, attended, log_total = attend(plan, info, projected, tables, seg_rows)
    mean_mix, scale_mix = spread_stats(plan, attended)
    unit_mix = (attended - mean_mix) * scale_mix
    mixed = (unit_mix * gm + bm).astype(LOW)
    resid_mid = resid + reduce_blocks(plan, lambda left: matmul(left, out_wt, (1, 1)), mixed)
    mean_ffn, scale_ffn = norm_stats(resid_mid)
    unit_ffn = (resid_mid - mean_ffn) * scale_ffn
    ffn_in = gather_blocks(plan, (unit_ffn * gf + bf).astype(LOW))
    hidden = matmul(ffn_in, up_w, (1, 0))
    phi = 0.5 * lax.erfc(hidden * (-(0.5**0.5)))
    active = hidden * phi
    slope = phi + hidden * (jnp.exp(-0.5 * hidden * hidden) * ((2.0 * np.pi) ** -0.5))
    mean_hid, scale_hid = spread_stats(plan, active)
    unit_hid = (active - mean_hid) * scale_hid
    hidden_low = (unit_hid * gh + bh).astype(LOW)
    output = resid_mid + reduce_blocks(
        plan, lambda left: matmul(left, down_wt, (1, 1)), hidden_low
    )
    output = lax.ppermute(output.astype(LOW), BOTH, plan.back)

    grad_all = gather_blocks(plan, grad_low)
    grad_hn = matmul(grad_all, down_wt, (1, 0))
    grad_down = scatter_weight(plan, matmul(grad_all, hidden_low, (0, 0)))
    grad_active, gain_hidden_part, bias_hidden_part = spread_norm_back(
        plan, grad_hn, gh, unit_hid, scale_hid
    )
    grad_hidden = (grad_active * slope).astype(LOW)
    grad_ffn_in = reduce_blocks(plan, lambda left: matmul(left, up_w, (1, 1)), grad_hidden)
    grad_up = scatter_weight(plan, matmul(ffn_in, grad_hidden, (0, 0)))
    grad_mid, gain_ffn_part, bias_ffn_part = norm_back(grad_ffn_in, gf, unit_ffn, scale_ffn)
    grad_mid = grad_mid + grad_low.astype(WIDE)
    mid_all = gather_blocks(plan, grad_mid.astype(LOW))
    grad_mixed = matmul(mid_all, out_wt, (1, 0))
    grad_out = scatter_weight(plan, matmul(mid_all, mixed, (0, 0)))
    grad_attended, gain_mix_part, bias_mix_part = spread_norm_back(
        plan, grad_mixed, gm, unit_mix, scale_mix
    )
    grad_proj = attend_back(plan, info, qkv, attended, grad_attended, log_total, tables, seg_rows)
    grad_normed = reduce_blocks(plan, lambda left: matmul(left, qkv_w, (1, 1)), grad_proj)
    grad_qkv = scatter_weight(plan, matmul(normed, grad_proj, (0, 0)))
    grad_resid, gain_attn_part, bias_attn_part = norm_back(
        grad_normed, ga, unit_attn, scale_attn
    )
    grad_tokens = lax.ppermute((grad_mid + grad_resid).astype(LOW), BOTH, plan.back)

    whole = (gain_ffn_part, bias_ffn_part, gain_attn_part, bias_attn_part)
    parts = (gain_mix_part, bias_mix_part, gain_hidden_part, bias_hidden_part)
    whole_sum = sum_over(sum_over(jnp.stack(whole), "seq", ns), "batch", nb)
    whole_sum = whole_sum.reshape(4, nb * ns, -1)
    own = lax.dynamic_index_in_dim(whole_sum, batch_index * ns + seq_index, 1, False)
    part_sum = sum_over(jnp.concatenate(parts), "seq", ns)
    mixes = part_sum[: 2 * hd].reshape(2, ns, -1)
    hiddens = part_sum[2 * hd :].reshape(2, ns, -1)
    mixes = lax.dynamic_index_in_dim(mixes, seq_index, 1, False)
    hiddens = lax.dynamic_index_in_dim(hiddens, seq_index, 1, False)

    grad_qkv = grad_qkv.reshape(-1, nb, 3, hd).transpose(0, 2, 1, 3).reshape(w_qkv.shape)
    return (
        output[None],
        grad_tokens.astype(WIDE)[None],
        grad_qkv.astype(WIDE),
        grad_out.astype(WIDE).T,
        grad_up.astype(WIDE),
        grad_down.astype(WIDE).T,
        own[2],
        own[3],
        mixes[0],
        mixes[1],
        own[0],
        own[1],
        hiddens[0],
        hiddens[1],
    )


def solution(mesh):
    plan = Plan(mesh.shape["batch"], mesh.shape["seq"])
    rows = P("batch", "seq", None)
    over_rows, over_columns, vector = P(BOTH, None), P(None, BOTH), P(BOTH)
    return jax.shard_map(
        functools.partial(shards, plan),
        mesh=mesh,
        in_specs=(rows, P("batch", None), P("batch"), rows)
        + (over_rows, over_columns, over_rows, over_columns)
        + (vector,) * 8,
        out_specs=(rows, rows, over_rows, over_columns, over_rows, over_columns) + (vector,) * 8,
        check_vma=False,
    )
```

```python
import functools

import jax
import jax.numpy as jnp
import numpy as np
from jax import lax
from jax.experimental import pallas as pl
from jax.experimental.pallas import tpu as pltpu
from jax.sharding import PartitionSpec as P

EPSILON = 1e-05
HEAD = 64
STRIPE = 256
ROWS_AT_ONCE = 256
LOW = jnp.bfloat16
WIDE = jnp.float32
BOTH = ("batch", "seq")

LAYER = (2, 0, 1, 2, 1, 3, 3, 0)
PLACE = (1, 1, 1, 0, 0, 1, 0, 0)
TURN = ((1, 1), (3, 2), (0, 2), (3, 1))


class Plan:
    def __init__(self, nb, ns):
        self.nb, self.ns = nb, ns
        self.rows = nb // ns
        self.fast = nb == 8 and ns == 4
        if self.fast:
            layer, place, turn = LAYER, PLACE, TURN
        else:
            layer = [b // self.rows for b in range(nb)]
            place = [b % self.rows for b in range(nb)]
            turn = [[0] * self.rows for _ in range(ns)]
        self.there = []
        for b in range(nb):
            for s in range(ns):
                k, p = layer[b], place[b]
                target = ((s ^ turn[k][p]) * self.rows + p) * ns + k
                self.there.append((b * ns + s, target))
        self.back = [(d, s) for s, d in self.there]
        row_of = {(layer[b], place[b]): b for b in range(nb)}
        table = []
        for b in range(nb):
            for k in range(ns):
                c, t = b % self.rows, b // self.rows
                order = [c, 1 - c] if self.fast else list(range(self.rows))
                entry = [row_of[k, p] for p in order]
                for p in order:
                    for q in range(ns):
                        entry.append(q ^ t ^ turn[k][p] if self.fast else q ^ turn[k][p])
                table.append(entry)
        self.table = np.array(table, np.int32)


def swap_over(value, axis, step, size):
    return lax.ppermute(value, axis, [(i, i ^ step) for i in range(size)])


def bits(size):
    return [1 << i for i in range(size.bit_length() - 1)]


def sum_over(value, axis, size):
    for step in bits(size):
        value = value + swap_over(value, axis, step, size)
    return value


def aligned(plan, value, step):
    if not plan.fast:
        return value
    shape = value.shape
    axis = {1: 1, 4: 2, 2: 3}[step]
    return jnp.flip(value.reshape(shape[0], 2, 2, 2, shape[1] // 8), axis).reshape(shape)


def gather_over(value, axis, size):
    index = lax.axis_index(axis)
    value = value[None]
    for step in bits(size):
        other = swap_over(value, axis, step, size)
        upper = (index & step) != 0
        value = jnp.concatenate(
            [jnp.where(upper, other, value), jnp.where(upper, value, other)], axis=0
        )
    return value


def sync(*values):
    return lax.optimization_barrier(values)


def gather_near(plan, block):
    if not plan.fast:
        slots, width = block.shape
        full = lax.all_gather(block, "batch", axis=0, tiled=False)
        full = full.reshape(plan.nb // plan.rows, plan.rows, slots, width)
        return [full.transpose(1, 0, 2, 3).reshape(plan.nb * slots, width)]
    return [block, swap_over(block, "batch", 2, 8), swap_over(block, "batch", 4, 8)]


def gather_far(plan, near):
    if not plan.fast:
        return near
    block, from_x, from_y = near
    half = block.shape[0] // 2
    far = swap_over(from_x[:half], "batch", 4, 8), swap_over(from_y[half:], "batch", 2, 8)
    other = [swap_over(piece, "batch", 1, 8) for piece in near]
    *other, far_a, far_b = sync(*other, *far)
    return [*near, far_a, far_b, *other, swap_over(far_a, "batch", 1, 8), swap_over(far_b, "batch", 1, 8)]


def reduce_first(plan, kept, *others):
    if not plan.fast:
        count, width = kept.shape
        slots = count // plan.nb
        part = kept.reshape(plan.rows, plan.nb // plan.rows, slots, width).transpose(1, 0, 2, 3)
        total = lax.psum_scatter(
            part.reshape(count, width), "batch", scatter_dimension=0, tiled=True
        )
        total, *others = sync(total, *others)
        return total.astype(WIDE), others
    over_x, over_y, near, at_x, at_y = kept
    slots, half = at_x.shape
    over_x, over_y = swap_over(over_x, "batch", 2, 8), swap_over(over_y, "batch", 4, 8)
    over_x, over_y, *others = sync(over_x, over_y, *others)
    to_x = (at_x + over_y[:slots].astype(WIDE)).astype(LOW)
    to_y = (at_y + over_x[:slots].astype(WIDE)).astype(LOW)
    first = near[:, :half] + over_x[slots:].astype(WIDE)
    second = near[:, half:] + over_y[slots:].astype(WIDE)
    return (first, second, to_x, to_y), others


def reduce_last(plan, state):
    if not plan.fast:
        return state
    first, second, to_x, to_y = state
    from_x, from_y = swap_over(to_x, "batch", 2, 8), swap_over(to_y, "batch", 4, 8)
    from_x, from_y = sync(from_x, from_y)
    return jnp.concatenate([first + from_y.astype(WIDE), second + from_x.astype(WIDE)], axis=1)


def split_columns(plan, shard):
    rows, width = shard.shape
    return shard.reshape(rows, plan.nb, width // plan.nb).transpose(1, 0, 2)


def join_columns(plan, pieces):
    nb, rows, part = pieces.shape
    return pieces.transpose(1, 0, 2).reshape(rows, nb * part)


def exchange(pieces):
    return lax.all_to_all(pieces, "batch", 0, 0, tiled=True)


def gather_layers(pieces):
    nb, rows, part = pieces.shape
    return lax.all_gather(pieces.reshape(nb * rows, part), "seq", axis=0, tiled=True)


def scatter_layers(plan, part):
    own = lax.psum_scatter(part, "seq", scatter_dimension=0, tiled=True)
    rows, width = own.shape
    return own.reshape(plan.nb, rows // plan.nb, width)


def to_inner(plan, values):
    count, width = values.shape
    values = values.reshape(count, plan.nb, plan.ns, width // (plan.nb * plan.ns))
    return values.transpose(0, 2, 1, 3).reshape(count, width)


def to_outer(plan, values):
    count, width = values.shape
    values = values.reshape(count, plan.ns, plan.nb, width // (plan.nb * plan.ns))
    return values.transpose(0, 2, 1, 3).reshape(count, width)


def norm_stats(values):
    mean = jnp.mean(values, axis=-1, keepdims=True)
    center = values - mean
    return mean, lax.rsqrt(jnp.mean(center * center, axis=-1, keepdims=True) + EPSILON)


def spread_stats(plan, stats, count):
    mean, square = stats[0], stats[1]
    for step in bits(plan.nb):
        other = swap_over(jnp.stack([mean, square]), "batch", step, plan.nb)
        other = aligned(plan, other, step)
        gap = other[0] - mean
        mean = 0.5 * (mean + other[0])
        square = square + other[1] + gap * gap * (0.5 * count)
        count = 2 * count
    return jnp.stack([mean, lax.rsqrt(square / count + EPSILON)])


def spread_sums(plan, sums, count):
    for step in bits(plan.nb):
        sums = sums + aligned(plan, swap_over(sums, "batch", step, plan.nb), step)
    return sums / (count * plan.nb)


def norm_back(upstream, gain, unit, scale):
    scaled = upstream * gain
    first = jnp.mean(scaled, axis=-1, keepdims=True)
    second = jnp.mean(scaled * unit, axis=-1, keepdims=True)
    grad = scale * (scaled - first - unit * second)
    return grad, jnp.sum(upstream * unit, axis=0), jnp.sum(upstream, axis=0)


def xpos_tables(length):
    slot_pos = (jnp.arange(length, dtype=jnp.int32) - length // 2).astype(WIDE)
    index = jnp.arange(32, dtype=jnp.int32).astype(WIDE)
    angle = slot_pos[:, None] * jnp.exp(index * (-jnp.log(10000.0) / 32.0))[None, :]
    zeta = (index / 32.0 + 0.4) / 1.4
    growth = jnp.exp(slot_pos[:, None] * jnp.log(zeta)[None, :] / 512.0)
    cosine, sine = jnp.cos(angle), jnp.sin(angle)
    tables = []
    for scale in (growth, 1.0 / growth):
        tables += [cosine * scale] * 4
        tables += [-sine * scale, sine * scale] * 2
    return jnp.concatenate(tables, axis=1)


def swap_halves(values):
    lane = lax.broadcasted_iota(jnp.int32, values.shape, 1)
    return jnp.where(lane % 64 < 32, pltpu.roll(values, 96, 1), pltpu.roll(values, 32, 1))


def matmul(a, b, contract):
    return lax.dot_general(a, b, ((contract[:1], contract[1:]), ((), ())), preferred_element_type=WIDE)


def as_column(row):
    return jnp.broadcast_to(row, (128, row.shape[1])).T[:, :1]


def as_row(column):
    return jnp.broadcast_to(column, (column.shape[0], 128)).T[:1]


def stat_rows(values):
    mean = jnp.mean(values, axis=-1, keepdims=True)
    center = values - mean
    square = jnp.sum(center * center, axis=-1, keepdims=True)
    return jnp.concatenate([as_row(mean), as_row(square)], axis=0)


def plain_end(acc, block, out):
    out[...] = acc


def gelu_end(acc, block, active_out, slope_out, stats_out):
    phi = 0.5 + 0.5 * lax.erf(acc * (0.5**0.5))
    active = acc * phi
    active_out[...] = active
    slope_out[...] = phi + acc * (jnp.exp(-0.5 * acc * acc) * ((2.0 * np.pi) ** -0.5))
    stats_out[...] = stat_rows(active)


def norm_back_end(acc, block, normal, stats, gain, bias, out, sums_out, vectors_out, low_out=None):
    out[...] = acc
    unit = (normal[...] - as_column(stats[0:1])) * as_column(stats[1:2])
    if low_out is not None:
        low_out[...] = (unit * gain[...] + bias[...]).astype(LOW)
    scaled = acc * gain[...]
    sums = [jnp.sum(scaled, axis=-1, keepdims=True), jnp.sum(scaled * unit, axis=-1, keepdims=True)]
    sums_out[...] = jnp.concatenate([as_row(sums[0]), as_row(sums[1])], axis=0)
    vectors = jnp.concatenate(
        [jnp.sum(acc * unit, axis=0, keepdims=True), jnp.sum(acc, axis=0, keepdims=True)], axis=0
    )

    @pl.when(block == 0)
    def _():
        vectors_out[...] = vectors

    @pl.when(block != 0)
    def _():
        vectors_out[...] += vectors


def pieces_kernel(*refs, moves, loads, step, n_arrays, n_weights, n_extra, keep, columns, end):
    arrays, weights = refs[:n_arrays], refs[n_arrays : n_arrays + n_weights]
    at = n_arrays + n_weights + n_extra
    extra = refs[n_arrays + n_weights : at]
    full, kept = refs[at], refs[at + 1] if keep else None
    outs = refs[at + 1 + keep : -6]
    rows, weight, arrived, left, loaded, stored = refs[-6:]
    block, count = pl.program_id(0), pl.num_programs(0)

    @pl.when(block == 0)
    def _():
        for index, column, row, n in loads:
            pltpu.make_async_copy(
                weights[index].at[:, pl.ds(column, weight.shape[1])],
                weight.at[pl.ds(row, n), :],
                loaded.at[0],
            ).start()
        for index, first, row, n in moves:
            pltpu.make_async_copy(
                arrays[index].at[pl.ds(first, n), :], rows.at[pl.ds(row, n), :], arrived.at[row // step]
            ).start()
        pltpu.make_async_copy(weight, weight, loaded.at[0]).wait()
        if keep:
            pltpu.make_async_copy(weight, kept, stored.at[0]).start()

    here = pl.ds(pl.multiple_of(block * step, step), step)
    pltpu.make_async_copy(rows.at[here], rows.at[here], arrived.at[block]).wait()
    pltpu.make_async_copy(rows.at[here], full.at[here], left.at[block]).start()
    acc = matmul(rows[here, :], weight[:, :columns], (1, 0))
    end(acc, block, *extra, *outs)

    @pl.when(block == count - 1)
    def _():
        for i in range(rows.shape[0] // step):
            part = pl.ds(i * step, step)
            pltpu.make_async_copy(rows.at[part], full.at[part], left.at[i]).wait()
        if keep:
            pltpu.make_async_copy(weight, kept, stored.at[0]).wait()


def pieces_matmul(arrays, weights, columns, end, extra, outs, name):
    step = ROWS_AT_ONCE
    moves, total = [], 0
    for index, array in enumerate(arrays):
        for first in range(0, array.shape[0], step):
            n = min(step, array.shape[0] - first)
            moves.append((index, first, total, n))
            total += n
    loads, inner = [], 0
    for index, weight in enumerate(weights):
        loads.append((index, columns[0], inner, weight.shape[0]))
        inner += weight.shape[0]
    keep = len(weights) > 1

    def spec(shape, kind):
        if kind == "rows":
            return pl.BlockSpec((step, shape[1]), lambda i: (i, 0))
        if kind == "lanes":
            return pl.BlockSpec((shape[0], step), lambda i: (0, i))
        return pl.BlockSpec(shape, lambda i: (0, 0))

    anywhere = pl.BlockSpec(memory_space=pl.ANY)
    kept = [jax.ShapeDtypeStruct((inner, columns[1]), LOW)] if keep else []
    return pl.pallas_call(
        functools.partial(
            pieces_kernel,
            moves=moves,
            loads=loads,
            step=step,
            n_arrays=len(arrays),
            n_weights=len(weights),
            n_extra=len(extra),
            keep=int(keep),
            columns=columns[2],
            end=end,
        ),
        grid=(total // step,),
        in_specs=[anywhere] * (len(arrays) + len(weights))
        + [spec(array.shape, kind) for array, kind in extra],
        out_specs=[anywhere] * (1 + keep) + [spec(*out[:2]) for out in outs],
        out_shape=[jax.ShapeDtypeStruct((total, inner), LOW)]
        + kept
        + [jax.ShapeDtypeStruct(out[0], out[2] if len(out) > 2 else WIDE) for out in outs],
        scratch_shapes=[
            pltpu.VMEM((total, inner), LOW),
            pltpu.VMEM((inner, columns[1]), LOW),
            pltpu.SemaphoreType.DMA((total // step,)),
            pltpu.SemaphoreType.DMA((total // step,)),
            pltpu.SemaphoreType.DMA((1,)),
            pltpu.SemaphoreType.DMA((1,)),
        ],
        compiler_params=pltpu.CompilerParams(vmem_limit_bytes=56 << 20),
        name=name,
    )(*arrays, *weights, *[array for array, _ in extra])


def mixed_left(values, stats, gain, bias):
    unit = (values[...] - as_column(stats[0:1])) * as_column(stats[1:2])
    return (unit * gain[...] + bias[...]).astype(LOW)


def hidden_left(grad, active, slope, stats, sums, gain):
    scale = as_column(stats[1:2])
    unit = (active[...] - as_column(stats[0:1])) * scale
    back = grad[...] * gain[...] - as_column(sums[0:1]) - unit * as_column(sums[1:2])
    return (scale * back * slope[...]).astype(LOW)


def plain_left(values):
    return values[...]


def part_kernel(*refs, n_in, make_left, keeps, own, split):
    weight = refs[n_in]
    left = make_left(*refs[:n_in])
    acc = matmul(left, weight[...], (1, 1))
    outs = refs[n_in + 1 :]
    others = outs[:4]
    if own:
        outs = outs[5:] if keeps else outs[4:]
    if keeps:
        outs[0][...] = left
        outs = outs[1:]
    block = pl.program_id(0)
    if not own:
        if not split:
            outs[0][...] = acc.astype(LOW)
            return
        for i, out in enumerate(outs):

            @pl.when(block == i)
            def _(out=out):
                out[...] = acc.astype(LOW)

        return
    over_x, over_y, near, at_x, at_y = outs
    slots, half = at_x.shape

    @pl.when(block == 0)
    def _():
        near[...] = acc + others[0][...].astype(WIDE)

    @pl.when(block == 1)
    def _():
        total = acc + others[1][...].astype(WIDE)
        over_x[slots:] = total[:, :half].astype(LOW)
        at_x[...] = total[:, half:]

    @pl.when(block == 2)
    def _():
        total = acc + others[2][...].astype(WIDE)
        over_y[slots:] = total[:, half:].astype(LOW)
        at_y[...] = total[:, :half]

    @pl.when(block == 3)
    def _():
        total = acc + others[3][...].astype(WIDE)
        over_x[:slots] = total[:, :half].astype(LOW)
        over_y[:slots] = total[:, half:].astype(LOW)


def part_call(plan, ins, weight, columns, make_left, keeps, first, blocks, name, others=(), kept=()):
    step = ROWS_AT_ONCE
    total = next(array.shape[0] for array, kind in ins if kind == "rows")
    rows, own = weight.shape[0], len(others) > 0

    def spec(array, kind):
        if kind == "rows":
            return pl.BlockSpec((step, array.shape[1]), lambda i: (first + i, 0))
        if kind == "lanes":
            return pl.BlockSpec((array.shape[0], step), lambda i: (0, first + i))
        return pl.BlockSpec(array.shape, lambda i: (0, 0))

    in_specs = [spec(*item) for item in ins]
    in_specs.append(
        pl.BlockSpec(
            (rows, columns[0]), lambda i: (0, columns[1]), pipeline_mode=pl.Buffered(1)
        )
    )
    operands = [array for array, _ in ins] + [weight, *others]
    in_specs += [
        pl.BlockSpec((step, rows), lambda i: (0, 0), pipeline_mode=pl.Buffered(1)) for _ in others
    ]
    out_specs, out_shape, aliases = [], [], {}
    if keeps:
        if own:
            aliases[len(operands)] = 0
            in_specs.append(pl.BlockSpec(memory_space=pl.ANY))
            operands += kept
        out_specs.append(pl.BlockSpec((step, columns[0]), lambda i: (first + i, 0)))
        out_shape.append(jax.ShapeDtypeStruct((total, columns[0]), LOW))
    whole = []
    if own:
        half = rows // 2
        whole = [((2 * step, half), LOW)] * 2 + [((step, rows), WIDE)] + [((step, half), WIDE)] * 2
    elif plan.fast:
        whole = [((step, rows), LOW)] * blocks
    else:
        out_specs.append(pl.BlockSpec((step, rows), lambda i: (i, 0)))
        out_shape.append(jax.ShapeDtypeStruct((blocks * step, rows), LOW))
    for shape, kind in whole:
        out_specs.append(pl.BlockSpec(shape, lambda i: (0, 0)))
        out_shape.append(jax.ShapeDtypeStruct(shape, kind))
    return pl.pallas_call(
        functools.partial(
            part_kernel, n_in=len(ins), make_left=make_left, keeps=keeps, own=own, split=plan.fast
        ),
        grid=(blocks,),
        in_specs=in_specs,
        out_specs=out_specs,
        out_shape=out_shape,
        input_output_aliases=aliases,
        compiler_params=pltpu.CompilerParams(vmem_limit_bytes=56 << 20),
        name=name,
    )(*operands)


def block_parts(plan, ins, weight, columns, make_left, keeps, name):
    total = next(array.shape[0] for array, kind in ins if kind == "rows")
    blocks = total // ROWS_AT_ONCE
    if not plan.fast:
        *left, part = part_call(plan, ins, weight, columns, make_left, keeps, 0, blocks, name)
        return *left, part
    half = blocks // 2
    outs = part_call(plan, ins, weight, columns, make_left, keeps, half, half, name + "_other")
    left, parts = outs[: int(keeps)], outs[int(keeps) :]
    others = [swap_over(part, "batch", 1, 8) for part in parts]
    outs = part_call(
        plan, ins, weight, columns, make_left, keeps, 0, half, name + "_own", others, left
    )
    return *outs[: int(keeps)], outs[int(keeps) :]


def fill_bias(bias, valid, seg_row, seg_col, length):
    for i in range(length // STRIPE):
        low, high = i * STRIPE, (i + 1) * STRIPE
        shape = (STRIPE, high)
        query = lax.broadcasted_iota(jnp.int32, shape, 0) + low
        key = lax.broadcasted_iota(jnp.int32, shape, 1)
        same = seg_col[low:high] == seg_row[:, :high]
        allowed = (key == query) | (same & (key <= query) & (query < valid))
        bias[low:high, :high] = jnp.where(allowed, 0.0, -1e30)


def attend_kernel(
    info, proj, tables, seg_row, seg_col, qkv, attended, log_total, stats, bias, *, ns, slots, hd
):
    row, head = pl.program_id(0), pl.program_id(1)
    length = ns * slots

    def place(quarter):
        return pl.multiple_of(info[row, quarter] * slots, slots)

    @pl.when(head == 0)
    def _():
        for q in range(ns):
            source, low, high = place(q), q * slots, (q + 1) * slots
            for part in range(2):
                cosine = tables[low:high, 256 * part : 256 * part + 128]
                sine = tables[low:high, 256 * part + 128 : 256 * part + 256]
                for pair in range(hd // 128):
                    at = part * hd + pair * 128
                    values = proj[pl.ds(source, slots), at : at + 128]
                    turned = values * cosine + swap_halves(values) * sine
                    qkv[low:high, at : at + 128] = turned.astype(LOW)
            qkv[low:high, 2 * hd :] = proj[pl.ds(source, slots), 2 * hd :].astype(LOW)
        fill_bias(bias, info[row, ns], seg_row[...], seg_col[...], length)
        log_total[...] = jnp.zeros_like(log_total)

    mine = lax.broadcasted_iota(jnp.int32, (STRIPE, hd), 1) // HEAD == head
    column = lax.broadcasted_iota(jnp.int32, (STRIPE, 128), 1) == head
    for i in range(length // STRIPE):
        low, high = i * STRIPE, (i + 1) * STRIPE
        queries = jnp.where(mine, qkv[low:high, :hd], jnp.zeros((), LOW))
        scores = matmul(queries, qkv[:high, hd : 2 * hd], (1, 1)) * 0.125 + bias[low:high, :high]
        top = jnp.max(scores, axis=-1, keepdims=True)
        weight = jnp.exp(scores - top)
        total = jnp.sum(weight, axis=-1, keepdims=True)
        summed = matmul(weight.astype(LOW), qkv[:high, 2 * hd :], (1, 0)) / total
        log_total[low:high] = jnp.where(column, top + jnp.log(total), log_total[low:high])
        for u in range(STRIPE // slots):
            to = place(i * (STRIPE // slots) + u)
            rows = slice(u * slots, (u + 1) * slots)
            attended[pl.ds(to, slots), :] = jnp.where(
                mine[rows], summed[rows], attended[pl.ds(to, slots), :]
            )

    @pl.when(head == pl.num_programs(1) - 1)
    def _():
        for q in range(ns):
            here = slice(q * slots, (q + 1) * slots)
            stats[:, here] = stat_rows(attended[here])


def attend_back_kernel(
    info, qkv, attended, grad, stats, sums, gain, log_total, tables, seg_row, seg_col, out,
    bias, grad_low, product, grad_q, grad_k, grad_v, *, ns, slots, hd
):
    row, head = pl.program_id(0), pl.program_id(1)
    length = ns * slots

    def place(quarter):
        return pl.multiple_of(info[row, quarter] * slots, slots)

    @pl.when(head == 0)
    def _():
        for q in range(ns):
            to, low, high = place(q), q * slots, (q + 1) * slots
            values = attended[low:high]
            scale = as_column(stats[1:2, low:high])
            unit = (values - as_column(stats[0:1, low:high])) * scale
            back = grad[low:high] * gain[...] - as_column(sums[0:1, low:high])
            back = scale * (back - unit * as_column(sums[1:2, low:high]))
            grad_low[pl.ds(to, slots), :] = back.astype(LOW)
            product[pl.ds(to, slots), :] = back * values
        fill_bias(bias, info[row, ns], seg_row[...], seg_col[...], length)
        for total in (grad_q, grad_k, grad_v):
            total[...] = jnp.zeros_like(total)

    mine = lax.broadcasted_iota(jnp.int32, (STRIPE, hd), 1) // HEAD == head
    column = lax.broadcasted_iota(jnp.int32, (STRIPE, 128), 1) == head
    nothing = jnp.zeros((), LOW)
    mine_all = lax.broadcasted_iota(jnp.int32, (length, hd), 1) // HEAD == head
    keys_mine = jnp.where(mine_all, qkv[:, hd : 2 * hd], nothing)
    for i in range(length // STRIPE):
        low, high = i * STRIPE, (i + 1) * STRIPE
        queries = jnp.where(mine, qkv[low:high, :hd], nothing)
        upstream = jnp.where(mine, grad_low[low:high], nothing)
        delta = jnp.sum(jnp.where(mine, product[low:high], 0.0), axis=-1, keepdims=True)
        log_sum = jnp.sum(jnp.where(column, log_total[low:high], 0.0), axis=-1, keepdims=True)
        scores = matmul(queries, qkv[:high, hd : 2 * hd], (1, 1)) * 0.125 + bias[low:high, :high]
        prob = jnp.exp(scores - log_sum)
        grad_prob = matmul(upstream, qkv[:high, 2 * hd :], (1, 1))
        grad_s = (prob * (grad_prob - delta) * 0.125).astype(LOW)
        grad_q[low:high] += matmul(grad_s, keys_mine[:high], (1, 0))
        grad_k[:high] += matmul(grad_s, queries, (0, 0))
        grad_v[:high] += matmul(prob.astype(LOW), upstream, (0, 0))

    @pl.when(head == pl.num_programs(1) - 1)
    def _():
        for q in range(ns):
            target, low, high = place(q), q * slots, (q + 1) * slots
            for part, total in enumerate((grad_q, grad_k)):
                cosine = tables[low:high, 256 * part : 256 * part + 128]
                sine = tables[low:high, 256 * part + 128 : 256 * part + 256]
                for pair in range(hd // 128):
                    values = total[low:high, pair * 128 : pair * 128 + 128]
                    turned = values * cosine - swap_halves(values) * sine
                    at = part * hd + pair * 128
                    out[pl.ds(target, slots), at : at + 128] = turned.astype(LOW)
            out[pl.ds(target, slots), 2 * hd :] = grad_v[low:high].astype(LOW)


def row_block(length, width):
    return pl.BlockSpec((length, width), lambda r, h, info: (r, 0))


def shared_block(length, width):
    return pl.BlockSpec((length, width), lambda r, h, info: (0, 0))


def attend(plan, info, proj, tables, segments):
    count, width = proj.shape
    length, hd = count // plan.rows, width // 3
    slots = length // plan.ns
    return pl.pallas_call(
        functools.partial(attend_kernel, ns=plan.ns, slots=slots, hd=hd),
        grid_spec=pltpu.PrefetchScalarGridSpec(
            num_scalar_prefetch=1,
            grid=(plan.rows, hd // HEAD),
            in_specs=[
                row_block(length, width),
                shared_block(length, 512),
                pl.BlockSpec((None, 1, length), lambda r, h, info: (r, 0, 0)),
                pl.BlockSpec((None, length, 1), lambda r, h, info: (r, 0, 0)),
            ],
            out_specs=[
                row_block(length, width),
                row_block(length, hd),
                row_block(length, 128),
                pl.BlockSpec((2, length), lambda r, h, info: (0, r)),
            ],
            scratch_shapes=[pltpu.VMEM((length, length), WIDE)],
        ),
        out_shape=[
            jax.ShapeDtypeStruct((count, width), LOW),
            jax.ShapeDtypeStruct((count, hd), WIDE),
            jax.ShapeDtypeStruct((count, 128), WIDE),
            jax.ShapeDtypeStruct((2, count), WIDE),
        ],
        compiler_params=pltpu.CompilerParams(vmem_limit_bytes=48 << 20),
        name="attend",
    )(info, proj, tables, segments[:, None, :], segments[:, :, None])


def attend_back(plan, info, qkv, attended, grad, stats, sums, gain, log_total, tables, segments):
    count, width = qkv.shape
    length, hd = count // plan.rows, width // 3
    slots = length // plan.ns
    return pl.pallas_call(
        functools.partial(attend_back_kernel, ns=plan.ns, slots=slots, hd=hd),
        grid_spec=pltpu.PrefetchScalarGridSpec(
            num_scalar_prefetch=1,
            grid=(plan.rows, hd // HEAD),
            in_specs=[
                row_block(length, width),
                row_block(length, hd),
                row_block(length, hd),
                pl.BlockSpec((2, length), lambda r, h, info: (0, r)),
                pl.BlockSpec((2, length), lambda r, h, info: (0, r)),
                shared_block(1, hd),
                row_block(length, 128),
                shared_block(length, 512),
                pl.BlockSpec((None, 1, length), lambda r, h, info: (r, 0, 0)),
                pl.BlockSpec((None, length, 1), lambda r, h, info: (r, 0, 0)),
            ],
            out_specs=row_block(length, width),
            scratch_shapes=[
                pltpu.VMEM((length, length), WIDE),
                pltpu.VMEM((length, hd), LOW),
                pltpu.VMEM((length, hd), WIDE),
                pltpu.VMEM((length, hd), WIDE),
                pltpu.VMEM((length, hd), WIDE),
                pltpu.VMEM((length, hd), WIDE),
            ],
        ),
        out_shape=jax.ShapeDtypeStruct((count, width), LOW),
        compiler_params=pltpu.CompilerParams(vmem_limit_bytes=48 << 20),
        name="attend_back",
    )(
        info, qkv, attended, grad, stats, sums, gain, log_total, tables,
        segments[:, None, :], segments[:, :, None],
    )


def shards(
    plan,
    tokens,
    segments,
    valid_count,
    cotangent,
    w_qkv,
    w_out,
    w_up,
    w_down,
    gain_attn,
    bias_attn,
    gain_mix,
    bias_mix,
    gain_ffn,
    bias_ffn,
    gain_hidden,
    bias_hidden,
):
    nb, ns = plan.nb, plan.ns
    width, slots, length = tokens.shape[2], tokens.shape[1], segments.shape[1]
    hd, hidden_part = width // nb, w_up.shape[1] // nb
    batch_index, seq_index = lax.axis_index("batch"), lax.axis_index("seq")
    entry = lax.dynamic_index_in_dim(
        jnp.asarray(plan.table), batch_index * ns + seq_index, 0, keepdims=False
    )

    slot = seq_index * slots + jnp.arange(slots, dtype=jnp.int32)
    living = (slot < valid_count[0])[:, None]
    grad_low = to_inner(plan, jnp.where(living, cotangent[0], jnp.zeros((), LOW)))
    tokens_low = lax.ppermute(to_inner(plan, tokens[0]), BOTH, plan.there)
    group = w_qkv.reshape(w_qkv.shape[0], 3, nb, hd).transpose(2, 0, 1, 3)
    group = group.reshape(nb, -1, 3 * hd)
    attn_own = exchange(jnp.concatenate([group, split_columns(plan, w_out.T)], axis=2))
    ffn_own = jnp.concatenate([split_columns(plan, w) for w in (w_up, w_down.T)], axis=2)

    own_params = (gain_attn, bias_attn, gain_mix, bias_mix, gain_ffn, bias_ffn, gain_hidden, bias_hidden)
    params = gather_over(jnp.concatenate([p.astype(WIDE) for p in own_params]), "seq", ns)
    tables = xpos_tables(length)
    tokens_low, attn_own, ffn_own, grad_low, params, tables = sync(
        tokens_low, attn_own, ffn_own, grad_low, params, tables
    )
    attn_w = gather_layers(attn_own)
    ffn_own = exchange(ffn_own)
    packed = jnp.concatenate(
        [params.reshape(-1), segments[0].astype(WIDE), valid_count.astype(WIDE)]
    )
    packed = gather_over(packed, "batch", nb)
    spread = packed[:, : params.size].reshape(nb, ns, -1)
    vectors, at = [], 0
    for index, p in enumerate(own_params):
        piece = spread[:, :, at : at + p.shape[0]]
        at += p.shape[0]
        if index in (0, 1, 4, 5):
            vectors.append(piece.transpose(1, 0, 2).reshape(1, -1))
        else:
            vectors.append(lax.dynamic_index_in_dim(piece, batch_index, 0, False).reshape(1, -1))
    ga, ba, gm, bm, gf, bf, gh, bh = vectors
    layer_rows = jnp.concatenate(
        [
            lax.dynamic_slice_in_dim(packed[:, params.size :], entry[r], 1, 0)
            for r in range(plan.rows)
        ]
    ).astype(jnp.int32)
    seg_rows = layer_rows[:, :length]
    info = jnp.concatenate(
        [entry[plan.rows :].reshape(plan.rows, ns), layer_rows[:, length:]], axis=1
    )
    count = plan.rows * length
    resid = tokens_low.astype(WIDE)
    mean_attn, scale_attn = norm_stats(resid)
    unit_attn = (resid - mean_attn) * scale_attn
    normed_low = (unit_attn * ga + ba).astype(LOW)
    normed_low, ffn_own, gm, bm, gf, bf, gh, bh = sync(
        normed_low, ffn_own, gm, bm, gf, bf, gh, bh
    )
    up_w = gather_layers(ffn_own[:, :, :hidden_part])
    down_wt = gather_layers(ffn_own[:, :, hidden_part:])

    near = sync(*gather_near(plan, normed_low))
    grad_low, *arrays = sync(grad_low, *gather_far(plan, near))
    grad_low = lax.ppermute(grad_low, BOTH, plan.there)
    normed, projected = pieces_matmul(
        arrays,
        [attn_w],
        (0, 3 * hd, 3 * hd),
        plain_end,
        [],
        [((count, 3 * hd), "rows")],
        "project",
    )
    qkv, attended, log_total, stats_mix = attend(plan, info, projected, tables, seg_rows)
    stats_mix, grad_low = sync(stats_mix, grad_low)
    stats_mix = spread_stats(plan, stats_mix, hd)
    mixed, kept = block_parts(
        plan,
        [(attended, "rows"), (stats_mix, "lanes"), (gm, "whole"), (bm, "whole")],
        attn_w,
        (hd, 3),
        mixed_left,
        True,
        "out",
    )
    state, _ = reduce_first(plan, kept)
    resid_mid = resid + reduce_last(plan, state)

    mean_ffn, scale_ffn = norm_stats(resid_mid)
    unit_ffn = (resid_mid - mean_ffn) * scale_ffn
    near = sync(*gather_near(plan, (unit_ffn * gf + bf).astype(LOW)))
    grad_later, *arrays = sync(grad_low, *gather_far(plan, near))
    grad_near = gather_near(plan, grad_later)
    ffn_in, active, slope, stats_hid = pieces_matmul(
        arrays,
        [up_w],
        (0, hidden_part, hidden_part),
        gelu_end,
        [],
        [((count, hidden_part), "rows"), ((count, hidden_part), "rows"), ((2, count), "lanes")],
        "up",
    )
    stats_hid, *grad_near = sync(stats_hid, *grad_near)
    grad_arrays = gather_far(plan, grad_near)
    stats_hid = spread_stats(plan, stats_hid, hidden_part)

    grad_all, grad_hn, sums_hid, vectors_hid, hidden_low = pieces_matmul(
        grad_arrays,
        [down_wt],
        (0, hidden_part, hidden_part),
        norm_back_end,
        [(active, "rows"), (stats_hid, "lanes"), (gh, "whole"), (bh, "whole")],
        [
            ((count, hidden_part), "rows"),
            ((2, count), "lanes"),
            ((2, hidden_part), "whole"),
            ((count, hidden_part), "rows", LOW),
        ],
        "down_back",
    )
    grad_down = matmul(grad_all, hidden_low, (0, 0)).astype(LOW)
    sums_hid = spread_sums(plan, sums_hid, hidden_part)
    sums_hid, grad_down = sync(sums_hid, grad_down)
    grad_down = scatter_layers(plan, grad_down)
    grad_hidden, kept = block_parts(
        plan,
        [
            (grad_hn, "rows"), (active, "rows"), (slope, "rows"),
            (stats_hid, "lanes"), (sums_hid, "lanes"), (gh, "whole"),
        ],
        up_w,
        (hidden_part, 0),
        hidden_left,
        True,
        "up_back",
    )
    grad_up = matmul(ffn_in, grad_hidden, (0, 0)).astype(LOW)
    state, (grad_up, hidden_low) = reduce_first(plan, kept, grad_up, hidden_low)
    grad_up = scatter_layers(plan, grad_up)
    grad_ffn_in = reduce_last(plan, state)
    grad_mid, gain_ffn_part, bias_ffn_part = norm_back(grad_ffn_in, gf, unit_ffn, scale_ffn)
    grad_mid = grad_mid + grad_low.astype(WIDE)
    (kept,) = block_parts(
        plan, [(hidden_low, "rows")], down_wt, (hidden_part, 0), plain_left, False, "down"
    )
    kept, near, grad_down = sync(kept, gather_near(plan, grad_mid.astype(LOW)), grad_down)
    arrays = sync(*gather_far(plan, near))
    grad_down, arrays = sync(grad_down, arrays)
    grad_down = exchange(grad_down)
    mid_all, grad_mixed, sums_mix, vectors_mix = pieces_matmul(
        arrays,
        [attn_w],
        (3 * hd, hd, hd),
        norm_back_end,
        [(attended, "rows"), (stats_mix, "lanes"), (gm, "whole"), (bm, "whole")],
        [((count, hd), "rows"), ((2, count), "lanes"), ((2, hd), "whole")],
        "out_back",
    )
    sums_mix, grad_down = sync(sums_mix, grad_down)
    grad_out = matmul(mid_all, mixed, (0, 0)).astype(LOW)
    sums_mix = spread_sums(plan, sums_mix, hd)
    sums_mix, grad_out, kept = sync(sums_mix, grad_out, kept)
    grad_out = scatter_layers(plan, grad_out)
    grad_proj = attend_back(
        plan, info, qkv, attended, grad_mixed, stats_mix, sums_mix, gm, log_total, tables, seg_rows
    )
    state, (grad_proj, grad_up) = reduce_first(plan, kept, grad_proj, grad_up)
    grad_up = exchange(grad_up)
    output = (resid_mid + reduce_last(plan, state)).astype(LOW)
    grad_qkv = matmul(normed, grad_proj, (0, 0)).astype(LOW)
    grad_proj, grad_qkv, output, grad_up = sync(grad_proj, grad_qkv, output, grad_up)
    grad_qkv = scatter_layers(plan, grad_qkv)
    output = lax.ppermute(output, BOTH, plan.back)
    (kept,) = block_parts(
        plan, [(grad_proj, "rows")], attn_w, (3 * hd, 0), plain_left, False, "project_back"
    )
    state, _ = reduce_first(plan, kept)
    grad_normed = reduce_last(plan, state)
    grad_resid, gain_attn_part, bias_attn_part = norm_back(
        grad_normed, ga, unit_attn, scale_attn
    )
    grad_tokens = (grad_mid + grad_resid).astype(LOW)
    grad_tokens, grad_qkv, grad_out = sync(grad_tokens, grad_qkv, grad_out)
    grad_tokens = lax.ppermute(grad_tokens, BOTH, plan.back)
    grad_qkv, grad_out = exchange(grad_qkv), exchange(grad_out)

    whole = jnp.stack([gain_ffn_part, bias_ffn_part, gain_attn_part, bias_attn_part])
    whole_sum = sum_over(sum_over(whole, "seq", ns), "batch", nb)
    whole_sum = whole_sum.reshape(4, nb * ns, -1)
    own = lax.dynamic_index_in_dim(whole_sum, seq_index * nb + batch_index, 1, False)
    part_sum = sum_over(jnp.concatenate([vectors_mix, vectors_hid], axis=1), "seq", ns)
    mixes = lax.dynamic_index_in_dim(part_sum[:, :hd].reshape(2, ns, -1), seq_index, 1, False)
    hiddens = lax.dynamic_index_in_dim(part_sum[:, hd:].reshape(2, ns, -1), seq_index, 1, False)

    grad_qkv = grad_qkv.reshape(nb, -1, 3, hd).transpose(1, 2, 0, 3)
    grad_out, grad_up, grad_down = [join_columns(plan, g) for g in (grad_out, grad_up, grad_down)]
    return (
        to_outer(plan, output)[None],
        to_outer(plan, grad_tokens).astype(WIDE)[None],
        grad_qkv.reshape(w_qkv.shape).astype(WIDE),
        grad_out.astype(WIDE).T,
        grad_up.astype(WIDE),
        grad_down.astype(WIDE).T,
        own[2],
        own[3],
        mixes[0],
        mixes[1],
        own[0],
        own[1],
        hiddens[0],
        hiddens[1],
    )


def solution(mesh):
    plan = Plan(mesh.shape["batch"], mesh.shape["seq"])
    rows = P("batch", "seq", None)
    over_rows, over_columns, vector = P(BOTH, None), P(None, BOTH), P(BOTH)
    return jax.shard_map(
        functools.partial(shards, plan),
        mesh=mesh,
        in_specs=(rows, P("batch", None), P("batch"), rows)
        + (over_rows, over_columns, over_rows, over_columns)
        + (vector,) * 8,
        out_specs=(rows, rows, over_rows, over_columns, over_rows, over_columns) + (vector,) * 8,
        check_vma=False,
    )
```

```python
import functools

import jax
import jax.numpy as jnp
import numpy as np
from jax import lax
from jax.experimental import pallas as pl
from jax.experimental.pallas import tpu as pltpu
from jax.sharding import PartitionSpec as P

EPSILON = 1e-05
HEAD = 64
STRIPE = 256
ROWS_AT_ONCE = 256
LOW = jnp.bfloat16
WIDE = jnp.float32
BOTH = ("batch", "seq")

LAYER = (2, 0, 1, 2, 1, 3, 3, 0)
PLACE = (1, 1, 1, 0, 0, 1, 0, 0)
TURN = ((1, 1), (3, 2), (0, 2), (3, 1))


class Plan:
    def __init__(self, nb, ns):
        self.nb, self.ns = nb, ns
        self.rows = nb // ns
        self.fast = nb == 8 and ns == 4
        if self.fast:
            layer, place, turn = LAYER, PLACE, TURN
        else:
            layer = [b // self.rows for b in range(nb)]
            place = [b % self.rows for b in range(nb)]
            turn = [[0] * self.rows for _ in range(ns)]
        self.there = []
        for b in range(nb):
            for s in range(ns):
                k, p = layer[b], place[b]
                target = ((s ^ turn[k][p]) * self.rows + p) * ns + k
                self.there.append((b * ns + s, target))
        self.back = [(d, s) for s, d in self.there]
        row_of = {(layer[b], place[b]): b for b in range(nb)}
        table = []
        for b in range(nb):
            for k in range(ns):
                c, t = b % self.rows, b // self.rows
                order = [c, 1 - c] if self.fast else list(range(self.rows))
                entry = [row_of[k, p] for p in order]
                for p in order:
                    for q in range(ns):
                        entry.append(q ^ t ^ turn[k][p] if self.fast else q ^ turn[k][p])
                table.append(entry)
        self.table = np.array(table, np.int32)


def swap_over(value, axis, step, size):
    return lax.ppermute(value, axis, [(i, i ^ step) for i in range(size)])


def bits(size):
    return [1 << i for i in range(size.bit_length() - 1)]


def sum_over(value, axis, size):
    for step in bits(size):
        value = value + swap_over(value, axis, step, size)
    return value


def aligned(plan, value, step):
    if not plan.fast:
        return value
    shape = value.shape
    axis = {1: 1, 4: 2, 2: 3}[step]
    return jnp.flip(value.reshape(shape[0], 2, 2, 2, shape[1] // 8), axis).reshape(shape)


def gather_over(value, axis, size):
    index = lax.axis_index(axis)
    value = value[None]
    for step in bits(size):
        other = swap_over(value, axis, step, size)
        upper = (index & step) != 0
        value = jnp.concatenate(
            [jnp.where(upper, other, value), jnp.where(upper, value, other)], axis=0
        )
    return value


def sync(*values):
    return lax.optimization_barrier(values)


def gather_near(plan, block):
    if not plan.fast:
        slots, width = block.shape
        full = lax.all_gather(block, "batch", axis=0, tiled=False)
        full = full.reshape(plan.nb // plan.rows, plan.rows, slots, width)
        return [full.transpose(1, 0, 2, 3).reshape(plan.nb * slots, width)]
    return [block, swap_over(block, "batch", 2, 8), swap_over(block, "batch", 4, 8)]


def gather_far(plan, near):
    if not plan.fast:
        return near
    block, from_x, from_y = near
    half = block.shape[0] // 2
    far = swap_over(from_x[:half], "batch", 4, 8), swap_over(from_y[half:], "batch", 2, 8)
    other = [swap_over(piece, "batch", 1, 8) for piece in near]
    *other, far_a, far_b = sync(*other, *far)
    return [*near, far_a, far_b, *other, swap_over(far_a, "batch", 1, 8), swap_over(far_b, "batch", 1, 8)]


def reduce_first(plan, kept, *others):
    if not plan.fast:
        count, width = kept.shape
        slots = count // plan.nb
        part = kept.reshape(plan.rows, plan.nb // plan.rows, slots, width).transpose(1, 0, 2, 3)
        total = lax.psum_scatter(
            part.reshape(count, width), "batch", scatter_dimension=0, tiled=True
        )
        total, *others = sync(total, *others)
        return total.astype(WIDE), others
    over_x, far_y, over_y, near, at_x, at_y = kept
    slots, half = at_x.shape
    over_x, far_y = swap_over(over_x, "batch", 2, 8), swap_over(far_y, "batch", 4, 8)
    over_y = swap_over(over_y, "batch", 4, 8)
    over_x, far_y, over_y, *others = sync(over_x, far_y, over_y, *others)
    to_x = (at_x + far_y.astype(WIDE)).astype(LOW)
    to_y = (at_y + over_x[:slots].astype(WIDE)).astype(LOW)
    first = near[:, :half] + over_x[slots:].astype(WIDE)
    second = near[:, half:] + over_y.astype(WIDE)
    return (first, second, to_x, to_y), others


def reduce_last(plan, state):
    if not plan.fast:
        return state
    first, second, to_x, to_y = state
    from_x, from_y = swap_over(to_x, "batch", 2, 8), swap_over(to_y, "batch", 4, 8)
    from_x, from_y = sync(from_x, from_y)
    return jnp.concatenate([first + from_y.astype(WIDE), second + from_x.astype(WIDE)], axis=1)


def split_columns(plan, shard):
    rows, width = shard.shape
    return shard.reshape(rows, plan.nb, width // plan.nb).transpose(1, 0, 2)


def join_columns(plan, pieces):
    nb, rows, part = pieces.shape
    return pieces.transpose(1, 0, 2).reshape(rows, nb * part)


def exchange(pieces):
    return lax.all_to_all(pieces, "batch", 0, 0, tiled=True)


def gather_layers(pieces):
    nb, rows, part = pieces.shape
    return lax.all_gather(pieces.reshape(nb * rows, part), "seq", axis=0, tiled=True)


def scatter_layers(plan, part):
    own = lax.psum_scatter(part, "seq", scatter_dimension=0, tiled=True)
    rows, width = own.shape
    return own.reshape(plan.nb, rows // plan.nb, width)


def reorder_kernel(values, out, *, sources):
    low = lax.broadcasted_iota(jnp.int32, (values.shape[0], 128), 1) < 64
    for at, (first, second, half) in enumerate(sources):
        a = values[:, first * 128 : first * 128 + 128].astype(WIDE)
        b = values[:, second * 128 : second * 128 + 128].astype(WIDE)
        if half:
            a = pltpu.roll(a, 64, 1)
        else:
            b = pltpu.roll(b, 64, 1)
        out[:, at * 128 : at * 128 + 128] = jnp.where(low, a, b).astype(out.dtype)


def reorder(plan, values, outward, dtype):
    count, width = values.shape
    sizes = (plan.ns, plan.nb) if outward else (plan.nb, plan.ns)
    if width != plan.nb * plan.ns * 64 or sizes[0] % 2 or sizes[1] % 2:
        values = values.reshape(count, *sizes, width // (plan.nb * plan.ns))
        return values.transpose(0, 2, 1, 3).reshape(count, width).astype(dtype)
    sources = []
    for inner in range(sizes[1]):
        for outer in range(0, sizes[0], 2):
            at = outer * sizes[1] + inner
            sources.append((at // 2, (at + sizes[1]) // 2, at % 2))
    return pl.pallas_call(
        functools.partial(reorder_kernel, sources=sources),
        out_shape=jax.ShapeDtypeStruct(values.shape, dtype),
        compiler_params=pltpu.CompilerParams(vmem_limit_bytes=48 << 20),
        name="reorder",
    )(values)


def norm_stats(values):
    mean = jnp.mean(values, axis=-1, keepdims=True)
    center = values - mean
    return mean, lax.rsqrt(jnp.mean(center * center, axis=-1, keepdims=True) + EPSILON)


def spread_stats(plan, stats, count):
    mean, square = stats[0], stats[1]
    for step in bits(plan.nb):
        other = swap_over(jnp.stack([mean, square]), "batch", step, plan.nb)
        other = aligned(plan, other, step)
        gap = other[0] - mean
        mean = 0.5 * (mean + other[0])
        square = square + other[1] + gap * gap * (0.5 * count)
        count = 2 * count
    return jnp.stack([mean, lax.rsqrt(square / count + EPSILON)])


def spread_sums(plan, sums, count):
    for step in bits(plan.nb):
        sums = sums + aligned(plan, swap_over(sums, "batch", step, plan.nb), step)
    return sums / (count * plan.nb)


def norm_back(upstream, gain, unit, scale):
    scaled = upstream * gain
    first = jnp.mean(scaled, axis=-1, keepdims=True)
    second = jnp.mean(scaled * unit, axis=-1, keepdims=True)
    grad = scale * (scaled - first - unit * second)
    return grad, jnp.sum(upstream * unit, axis=0), jnp.sum(upstream, axis=0)


def xpos_tables(length):
    slot_pos = (jnp.arange(length, dtype=jnp.int32) - length // 2).astype(WIDE)
    lane = jnp.arange(128, dtype=jnp.int32)
    index = (lane % 32).astype(WIDE)
    angle = slot_pos[:, None] * jnp.exp(index * (-jnp.log(10000.0) / 32.0))[None, :]
    zeta = (index / 32.0 + 0.4) / 1.4
    growth = jnp.exp(slot_pos[:, None] * jnp.log(zeta)[None, :] / 512.0)
    cosine, sine = jnp.cos(angle), jnp.sin(angle)
    sine = jnp.where(lane % 64 < 32, -sine, sine)
    return cosine * growth, sine * growth, cosine / growth, sine / growth


def swap_halves(values):
    lane = lax.broadcasted_iota(jnp.int32, values.shape, 1)
    return jnp.where(lane % 64 < 32, pltpu.roll(values, 96, 1), pltpu.roll(values, 32, 1))


def matmul(a, b, contract):
    return lax.dot_general(a, b, ((contract[:1], contract[1:]), ((), ())), preferred_element_type=WIDE)


def as_column(row):
    return jnp.broadcast_to(row, (128, row.shape[1])).T[:, :1]


def as_row(column):
    return jnp.broadcast_to(column, (column.shape[0], 128)).T[:1]


def stat_rows(values):
    mean = jnp.mean(values, axis=-1, keepdims=True)
    center = values - mean
    square = jnp.sum(center * center, axis=-1, keepdims=True)
    return jnp.concatenate([as_row(mean), as_row(square)], axis=0)


def plain_end(acc, block, out):
    out[...] = acc


def gelu_end(acc, block, active_out, slope_out, stats_out):
    phi = 0.5 + 0.5 * lax.erf(acc * (0.5**0.5))
    active = acc * phi
    active_out[...] = active
    slope_out[...] = phi + acc * (jnp.exp(-0.5 * acc * acc) * ((2.0 * np.pi) ** -0.5))
    stats_out[...] = stat_rows(active)


def norm_back_end(acc, block, normal, stats, gain, bias, out, sums_out, vectors_out, low_out=None):
    out[...] = acc
    unit = (normal[...] - as_column(stats[0:1])) * as_column(stats[1:2])
    if low_out is not None:
        low_out[...] = (unit * gain[...] + bias[...]).astype(LOW)
    scaled = acc * gain[...]
    sums = [jnp.sum(scaled, axis=-1, keepdims=True), jnp.sum(scaled * unit, axis=-1, keepdims=True)]
    sums_out[...] = jnp.concatenate([as_row(sums[0]), as_row(sums[1])], axis=0)
    vectors = jnp.concatenate(
        [jnp.sum(acc * unit, axis=0, keepdims=True), jnp.sum(acc, axis=0, keepdims=True)], axis=0
    )

    @pl.when(block == 0)
    def _():
        vectors_out[...] = vectors

    @pl.when(block != 0)
    def _():
        vectors_out[...] += vectors


def pieces_kernel(*refs, moves, loads, step, n_arrays, n_weights, n_extra, keep, columns, end):
    arrays, weights = refs[:n_arrays], refs[n_arrays : n_arrays + n_weights]
    at = n_arrays + n_weights + n_extra
    extra = refs[n_arrays + n_weights : at]
    full, kept = refs[at], refs[at + 1] if keep else None
    outs = refs[at + 1 + keep : -6]
    rows, weight, arrived, left, loaded, stored = refs[-6:]
    block, count = pl.program_id(0), pl.num_programs(0)

    @pl.when(block == 0)
    def _():
        for index, column, row, n in loads:
            pltpu.make_async_copy(
                weights[index].at[:, pl.ds(column, weight.shape[1])],
                weight.at[pl.ds(row, n), :],
                loaded.at[0],
            ).start()
        for index, first, row, n in moves:
            pltpu.make_async_copy(
                arrays[index].at[pl.ds(first, n), :], rows.at[pl.ds(row, n), :], arrived.at[row // step]
            ).start()
        pltpu.make_async_copy(weight, weight, loaded.at[0]).wait()
        if keep:
            pltpu.make_async_copy(weight, kept, stored.at[0]).start()

    here = pl.ds(pl.multiple_of(block * step, step), step)
    pltpu.make_async_copy(rows.at[here], rows.at[here], arrived.at[block]).wait()
    pltpu.make_async_copy(rows.at[here], full.at[here], left.at[block]).start()
    acc = matmul(rows[here, :], weight[:, :columns], (1, 0))
    end(acc, block, *extra, *outs)

    @pl.when(block == count - 1)
    def _():
        for i in range(rows.shape[0] // step):
            part = pl.ds(i * step, step)
            pltpu.make_async_copy(rows.at[part], full.at[part], left.at[i]).wait()
        if keep:
            pltpu.make_async_copy(weight, kept, stored.at[0]).wait()


def moves_of(arrays, step):
    moves, total = [], 0
    for index, array in enumerate(arrays):
        for first in range(0, array.shape[0], step):
            n = min(step, array.shape[0] - first)
            moves.append((index, first, total, n))
            total += n
    return moves, total


def pieces_matmul(arrays, weights, columns, end, extra, outs, name):
    step = ROWS_AT_ONCE
    moves, total = moves_of(arrays, step)
    loads, inner = [], 0
    for index, weight in enumerate(weights):
        loads.append((index, columns[0], inner, weight.shape[0]))
        inner += weight.shape[0]
    keep = len(weights) > 1

    def spec(shape, kind):
        if kind == "rows":
            return pl.BlockSpec((step, shape[1]), lambda i: (i, 0))
        if kind == "lanes":
            return pl.BlockSpec((shape[0], step), lambda i: (0, i))
        return pl.BlockSpec(shape, lambda i: (0, 0))

    anywhere = pl.BlockSpec(memory_space=pl.ANY)
    kept = [jax.ShapeDtypeStruct((inner, columns[1]), LOW)] if keep else []
    return pl.pallas_call(
        functools.partial(
            pieces_kernel,
            moves=moves,
            loads=loads,
            step=step,
            n_arrays=len(arrays),
            n_weights=len(weights),
            n_extra=len(extra),
            keep=int(keep),
            columns=columns[2],
            end=end,
        ),
        grid=(total // step,),
        in_specs=[anywhere] * (len(arrays) + len(weights))
        + [spec(array.shape, kind) for array, kind in extra],
        out_specs=[anywhere] * (1 + keep) + [spec(*out[:2]) for out in outs],
        out_shape=[jax.ShapeDtypeStruct((total, inner), LOW)]
        + kept
        + [jax.ShapeDtypeStruct(out[0], out[2] if len(out) > 2 else WIDE) for out in outs],
        scratch_shapes=[
            pltpu.VMEM((total, inner), LOW),
            pltpu.VMEM((inner, columns[1]), LOW),
            pltpu.SemaphoreType.DMA((total // step,)),
            pltpu.SemaphoreType.DMA((total // step,)),
            pltpu.SemaphoreType.DMA((1,)),
            pltpu.SemaphoreType.DMA((1,)),
        ],
        compiler_params=pltpu.CompilerParams(vmem_limit_bytes=56 << 20),
        name=name,
    )(*arrays, *weights, *[array for array, _ in extra])


def mixed_left(values, stats, gain, bias):
    unit = (values[...] - as_column(stats[0:1])) * as_column(stats[1:2])
    return (unit * gain[...] + bias[...]).astype(LOW)


def hidden_left(grad, active, slope, stats, sums, gain):
    scale = as_column(stats[1:2])
    unit = (active[...] - as_column(stats[0:1])) * scale
    back = grad[...] * gain[...] - as_column(sums[0:1]) - unit * as_column(sums[1:2])
    return (scale * back * slope[...]).astype(LOW)


def plain_left(values):
    return values[...]


def part_kernel(*refs, n_in, make_left, keeps, ends):
    n_more = len(ends[1])
    left = make_left(*refs[:n_in])
    acc = matmul(left, refs[n_in][...], (1, 1))
    more, outs = refs[n_in + 1 : n_in + 1 + n_more], refs[n_in + 1 + n_more :]
    if keeps:
        outs[0 if ends[2] else 1][...] = left
        outs = outs[1:] if ends[2] else outs[2:]
    ends[0](acc, pl.program_id(0), *more, *outs)


def other_end(acc, block, *outs):
    if len(outs) == 1:
        outs[0][...] = acc.astype(LOW)
        return
    for i, out in enumerate(outs):

        @pl.when(block == i)
        def _(out=out):
            out[...] = acc.astype(LOW)


def own_x_end(acc, block, from_x, from_far, over_x, far_y, at_x):
    slots, half = at_x.shape

    @pl.when(block == 0)
    def _():
        total = acc + from_x[...].astype(WIDE)
        over_x[slots:] = total[:, :half].astype(LOW)
        at_x[...] = total[:, half:]

    @pl.when(block == 1)
    def _():
        total = acc + from_far[...].astype(WIDE)
        over_x[:slots] = total[:, :half].astype(LOW)
        far_y[...] = total[:, half:].astype(LOW)


def own_y_end(acc, block, from_near, from_y, over_y, near, at_y):
    half = at_y.shape[1]

    @pl.when(block == 0)
    def _():
        near[...] = acc + from_near[...].astype(WIDE)

    @pl.when(block == 1)
    def _():
        total = acc + from_y[...].astype(WIDE)
        over_y[...] = total[:, half:].astype(LOW)
        at_y[...] = total[:, :half]


def part_call(ins, weight, columns, make_left, kept, at, blocks, end, more, outs, name):
    step = ROWS_AT_ONCE
    total = next(array.shape[0] for array, kind in ins if kind == "rows")
    rows = weight.shape[0]

    def spec(array, kind):
        if kind == "rows":
            return pl.BlockSpec((step, array.shape[1]), lambda i: (at(i), 0))
        if kind == "lanes":
            return pl.BlockSpec((array.shape[0], step), lambda i: (0, at(i)))
        return pl.BlockSpec(array.shape, lambda i: (0, 0))

    once = pl.Buffered(1)
    in_specs = [spec(*item) for item in ins]
    in_specs.append(
        pl.BlockSpec((rows, columns[0]), lambda i: (0, columns[1]), pipeline_mode=once)
    )
    in_specs += [pl.BlockSpec(m.shape, lambda i: (0, 0), pipeline_mode=once) for m in more]
    operands = [array for array, _ in ins] + [weight, *more]
    out_specs, out_shape, aliases = [], [], {}
    if kept is not None:
        if kept:
            aliases[len(operands)] = 0
            in_specs.append(pl.BlockSpec(memory_space=pl.ANY))
            operands += kept
        out_specs.append(pl.BlockSpec((step, columns[0]), lambda i: (at(i), 0)))
        out_shape.append(jax.ShapeDtypeStruct((total, columns[0]), LOW))
    for shape, dtype, moves in outs:
        out_specs.append(pl.BlockSpec((step if moves else shape[0], shape[1]), lambda i, m=moves: (i if m else 0, 0)))
        out_shape.append(jax.ShapeDtypeStruct(shape, dtype))
    return pl.pallas_call(
        functools.partial(
            part_kernel,
            n_in=len(ins),
            make_left=make_left,
            keeps=kept is not None,
            ends=(end, more, not kept),
        ),
        grid=(blocks,),
        in_specs=in_specs,
        out_specs=out_specs,
        out_shape=out_shape,
        input_output_aliases=aliases,
        compiler_params=pltpu.CompilerParams(vmem_limit_bytes=56 << 20),
        name=name,
    )(*operands)


def block_parts(plan, ins, weight, columns, make_left, keeps, name):
    step, rows = ROWS_AT_ONCE, weight.shape[0]
    left = [] if keeps else None

    def call(at, blocks, end, more, outs, name):
        return part_call(ins, weight, columns, make_left, left, at, blocks, end, more, outs, name)

    if not plan.fast:
        total = next(array.shape[0] for array, kind in ins if kind == "rows")
        outs = [((total, rows), LOW, True)]
        return call(lambda i: i, total // step, other_end, [], outs, name)
    half = rows // 2
    outs = [((step, rows), LOW, False)] * 4
    outs = call(lambda i: 4 + i, 4, other_end, [], outs, name + "_other")
    if keeps:
        left = [outs[0]]
    near, at_x, at_y, far = outs[int(keeps) :]
    others = [swap_over(part, "batch", 1, 8) for part in (at_x, far, near, at_y)]
    outs = [((2 * step, half), LOW, False), ((step, half), LOW, False), ((step, half), WIDE, False)]
    outs = call(lambda i: 1 + 2 * i, 2, own_x_end, others[:2], outs, name + "_own_x")
    if keeps:
        left = [outs[0]]
    over_x, far_y, at_x = outs[int(keeps) :]
    outs = [((step, half), LOW, False), ((step, rows), WIDE, False), ((step, half), WIDE, False)]
    outs = call(lambda i: 2 * i, 2, own_y_end, others[2:], outs, name + "_own_y")
    if keeps:
        left = [outs[0]]
    over_y, near, at_y = outs[int(keeps) :]
    return *(left or []), (over_x, far_y, over_y, near, at_x, at_y)


def fill_bias(bias, valid, seg_row, seg_col, length):
    for i in range(length // STRIPE):
        low, high = i * STRIPE, (i + 1) * STRIPE
        shape = (STRIPE, high)
        query = lax.broadcasted_iota(jnp.int32, shape, 0) + low
        key = lax.broadcasted_iota(jnp.int32, shape, 1)
        same = seg_col[low:high] == seg_row[:, :high]
        allowed = (key == query) | (same & (key <= query) & (query < valid))
        bias[low:high, :high] = jnp.where(allowed, 0.0, -1e30)


def attend_kernel(
    info, proj, cos_q, sin_q, cos_k, sin_k, seg_row, seg_col, qkv, attended, log_total, stats, bias,
    *, ns, slots, hd
):
    row, head = pl.program_id(0), pl.program_id(1)
    length = ns * slots

    def place(quarter):
        return pl.multiple_of(info[row, quarter] * slots, slots)

    @pl.when(head == 0)
    def _():
        for q in range(ns):
            source, low, high = place(q), q * slots, (q + 1) * slots
            for part, (cosine, sine) in enumerate(((cos_q, sin_q), (cos_k, sin_k))):
                cosine, sine = cosine[low:high], sine[low:high]
                for pair in range(hd // 128):
                    at = part * hd + pair * 128
                    values = proj[pl.ds(source, slots), at : at + 128]
                    turned = values * cosine + swap_halves(values) * sine
                    qkv[low:high, at : at + 128] = turned.astype(LOW)
            qkv[low:high, 2 * hd :] = proj[pl.ds(source, slots), 2 * hd :].astype(LOW)
        fill_bias(bias, info[row, ns], seg_row[...], seg_col[...], length)
        log_total[...] = jnp.zeros_like(log_total)

    mine = lax.broadcasted_iota(jnp.int32, (STRIPE, hd), 1) // HEAD == head
    column = lax.broadcasted_iota(jnp.int32, (STRIPE, 128), 1) == head
    for i in range(length // STRIPE):
        low, high = i * STRIPE, (i + 1) * STRIPE
        queries = jnp.where(mine, qkv[low:high, :hd], jnp.zeros((), LOW))
        scores = matmul(queries, qkv[:high, hd : 2 * hd], (1, 1)) * 0.125 + bias[low:high, :high]
        top = jnp.max(scores, axis=-1, keepdims=True)
        weight = jnp.exp(scores - top)
        total = jnp.sum(weight, axis=-1, keepdims=True)
        summed = matmul(weight.astype(LOW), qkv[:high, 2 * hd :], (1, 0)) / total
        log_total[low:high] = jnp.where(column, top + jnp.log(total), log_total[low:high])
        for u in range(STRIPE // slots):
            to = place(i * (STRIPE // slots) + u)
            rows = slice(u * slots, (u + 1) * slots)
            attended[pl.ds(to, slots), :] = jnp.where(
                mine[rows], summed[rows], attended[pl.ds(to, slots), :]
            )

    @pl.when(head == pl.num_programs(1) - 1)
    def _():
        for q in range(ns):
            here = slice(q * slots, (q + 1) * slots)
            stats[:, here] = stat_rows(attended[here])


def attend_back_kernel(
    info, qkv, attended, grad, stats, sums, gain, log_total, cos_q, sin_q, cos_k, sin_k, seg_row, seg_col, out,
    bias, grad_low, product, grad_q, grad_k, grad_v, *, ns, slots, hd
):
    row, head = pl.program_id(0), pl.program_id(1)
    length = ns * slots

    def place(quarter):
        return pl.multiple_of(info[row, quarter] * slots, slots)

    @pl.when(head == 0)
    def _():
        for q in range(ns):
            to, low, high = place(q), q * slots, (q + 1) * slots
            values = attended[low:high]
            scale = as_column(stats[1:2, low:high])
            unit = (values - as_column(stats[0:1, low:high])) * scale
            back = grad[low:high] * gain[...] - as_column(sums[0:1, low:high])
            back = scale * (back - unit * as_column(sums[1:2, low:high]))
            grad_low[pl.ds(to, slots), :] = back.astype(LOW)
            product[pl.ds(to, slots), :] = back * values
        fill_bias(bias, info[row, ns], seg_row[...], seg_col[...], length)
        for total in (grad_q, grad_k, grad_v):
            total[...] = jnp.zeros_like(total)

    mine = lax.broadcasted_iota(jnp.int32, (STRIPE, hd), 1) // HEAD == head
    column = lax.broadcasted_iota(jnp.int32, (STRIPE, 128), 1) == head
    nothing = jnp.zeros((), LOW)
    mine_all = lax.broadcasted_iota(jnp.int32, (length, hd), 1) // HEAD == head
    keys_mine = jnp.where(mine_all, qkv[:, hd : 2 * hd], nothing)
    for i in range(length // STRIPE):
        low, high = i * STRIPE, (i + 1) * STRIPE
        queries = jnp.where(mine, qkv[low:high, :hd], nothing)
        upstream = jnp.where(mine, grad_low[low:high], nothing)
        delta = jnp.sum(jnp.where(mine, product[low:high], 0.0), axis=-1, keepdims=True)
        log_sum = jnp.sum(jnp.where(column, log_total[low:high], 0.0), axis=-1, keepdims=True)
        scores = matmul(queries, qkv[:high, hd : 2 * hd], (1, 1)) * 0.125 + bias[low:high, :high]
        prob = jnp.exp(scores - log_sum)
        grad_prob = matmul(upstream, qkv[:high, 2 * hd :], (1, 1))
        grad_s = (prob * (grad_prob - delta) * 0.125).astype(LOW)
        grad_q[low:high] += matmul(grad_s, keys_mine[:high], (1, 0))
        grad_k[:high] += matmul(grad_s, queries, (0, 0))
        grad_v[:high] += matmul(prob.astype(LOW), upstream, (0, 0))

    @pl.when(head == pl.num_programs(1) - 1)
    def _():
        for q in range(ns):
            target, low, high = place(q), q * slots, (q + 1) * slots
            tables = (cos_q, sin_q, grad_q), (cos_k, sin_k, grad_k)
            for part, (cosine, sine, total) in enumerate(tables):
                cosine, sine = cosine[low:high], sine[low:high]
                for pair in range(hd // 128):
                    values = total[low:high, pair * 128 : pair * 128 + 128]
                    turned = values * cosine - swap_halves(values) * sine
                    at = part * hd + pair * 128
                    out[pl.ds(target, slots), at : at + 128] = turned.astype(LOW)
            out[pl.ds(target, slots), 2 * hd :] = grad_v[low:high].astype(LOW)


def row_block(length, width):
    return pl.BlockSpec((length, width), lambda r, h, info: (r, 0))


def shared_block(length, width):
    return pl.BlockSpec((length, width), lambda r, h, info: (0, 0))


def attend(plan, info, proj, tables, segments):
    count, width = proj.shape
    length, hd = count // plan.rows, width // 3
    slots = length // plan.ns
    return pl.pallas_call(
        functools.partial(attend_kernel, ns=plan.ns, slots=slots, hd=hd),
        grid_spec=pltpu.PrefetchScalarGridSpec(
            num_scalar_prefetch=1,
            grid=(plan.rows, hd // HEAD),
            in_specs=[
                row_block(length, width),
                *[shared_block(length, 128)] * 4,
                pl.BlockSpec((None, 1, length), lambda r, h, info: (r, 0, 0)),
                pl.BlockSpec((None, length, 1), lambda r, h, info: (r, 0, 0)),
            ],
            out_specs=[
                row_block(length, width),
                row_block(length, hd),
                row_block(length, 128),
                pl.BlockSpec((2, length), lambda r, h, info: (0, r)),
            ],
            scratch_shapes=[pltpu.VMEM((length, length), WIDE)],
        ),
        out_shape=[
            jax.ShapeDtypeStruct((count, width), LOW),
            jax.ShapeDtypeStruct((count, hd), WIDE),
            jax.ShapeDtypeStruct((count, 128), WIDE),
            jax.ShapeDtypeStruct((2, count), WIDE),
        ],
        compiler_params=pltpu.CompilerParams(vmem_limit_bytes=48 << 20),
        name="attend",
    )(info, proj, *tables, segments[:, None, :], segments[:, :, None])


def attend_back(plan, info, qkv, attended, grad, stats, sums, gain, log_total, tables, segments):
    count, width = qkv.shape
    length, hd = count // plan.rows, width // 3
    slots = length // plan.ns
    return pl.pallas_call(
        functools.partial(attend_back_kernel, ns=plan.ns, slots=slots, hd=hd),
        grid_spec=pltpu.PrefetchScalarGridSpec(
            num_scalar_prefetch=1,
            grid=(plan.rows, hd // HEAD),
            in_specs=[
                row_block(length, width),
                row_block(length, hd),
                row_block(length, hd),
                pl.BlockSpec((2, length), lambda r, h, info: (0, r)),
                pl.BlockSpec((2, length), lambda r, h, info: (0, r)),
                shared_block(1, hd),
                row_block(length, 128),
                *[shared_block(length, 128)] * 4,
                pl.BlockSpec((None, 1, length), lambda r, h, info: (r, 0, 0)),
                pl.BlockSpec((None, length, 1), lambda r, h, info: (r, 0, 0)),
            ],
            out_specs=row_block(length, width),
            scratch_shapes=[
                pltpu.VMEM((length, length), WIDE),
                pltpu.VMEM((length, hd), LOW),
                pltpu.VMEM((length, hd), WIDE),
                pltpu.VMEM((length, hd), WIDE),
                pltpu.VMEM((length, hd), WIDE),
                pltpu.VMEM((length, hd), WIDE),
            ],
        ),
        out_shape=jax.ShapeDtypeStruct((count, width), LOW),
        compiler_params=pltpu.CompilerParams(vmem_limit_bytes=48 << 20),
        name="attend_back",
    )(
        info, qkv, attended, grad, stats, sums, gain, log_total, *tables,
        segments[:, None, :], segments[:, :, None],
    )


def shards(
    plan,
    tokens,
    segments,
    valid_count,
    cotangent,
    w_qkv,
    w_out,
    w_up,
    w_down,
    gain_attn,
    bias_attn,
    gain_mix,
    bias_mix,
    gain_ffn,
    bias_ffn,
    gain_hidden,
    bias_hidden,
):
    nb, ns = plan.nb, plan.ns
    width, slots, length = tokens.shape[2], tokens.shape[1], segments.shape[1]
    hd, hidden_part = width // nb, w_up.shape[1] // nb
    batch_index, seq_index = lax.axis_index("batch"), lax.axis_index("seq")
    entry = lax.dynamic_index_in_dim(
        jnp.asarray(plan.table), batch_index * ns + seq_index, 0, keepdims=False
    )

    tokens_low = reorder(plan, tokens[0], False, LOW)
    group = w_qkv.reshape(w_qkv.shape[0], 3, nb, hd).transpose(2, 0, 1, 3)
    group = group.reshape(nb, -1, 3 * hd)
    attn_own = jnp.concatenate([group, split_columns(plan, w_out.T)], axis=2)
    tokens_low, attn_own = sync(tokens_low, attn_own)
    attn_own = exchange(attn_own)
    qkv_w = gather_layers(attn_own[:, :, : 3 * hd])
    tokens_low = lax.ppermute(tokens_low, BOTH, plan.there)

    own_params = (gain_attn, bias_attn, gain_mix, bias_mix, gain_ffn, bias_ffn, gain_hidden, bias_hidden)
    tokens_low, cotangent, attn_own, *own_params = sync(tokens_low, cotangent, attn_own, *own_params)
    params = gather_over(jnp.concatenate([p.astype(WIDE) for p in own_params]), "seq", ns)
    packed = jnp.concatenate(
        [params.reshape(-1), segments[0].astype(WIDE), valid_count.astype(WIDE)]
    )
    packed = gather_over(packed, "batch", nb)
    spread = packed[:, : params.size].reshape(nb, ns, -1)
    vectors, at = [], 0
    for index, p in enumerate(own_params):
        piece = spread[:, :, at : at + p.shape[0]]
        at += p.shape[0]
        if index in (0, 1, 4, 5):
            vectors.append(piece.transpose(1, 0, 2).reshape(1, -1))
        else:
            vectors.append(lax.dynamic_index_in_dim(piece, batch_index, 0, False).reshape(1, -1))
    ga, ba, gm, bm, gf, bf, gh, bh = vectors
    count = plan.rows * length
    resid = tokens_low.astype(WIDE)
    mean_attn, scale_attn = norm_stats(resid)
    unit_attn = (resid - mean_attn) * scale_attn
    normed_low = (unit_attn * ga + ba).astype(LOW)
    normed_low, packed, cotangent, w_up, w_down, gm, bm, gf, bf, gh, bh = sync(
        normed_low, packed, cotangent, w_up, w_down, gm, bm, gf, bf, gh, bh
    )

    near = gather_near(plan, normed_low)
    ffn_own = jnp.concatenate([split_columns(plan, w) for w in (w_up, w_down.T)], axis=2)
    slot = seq_index * slots + jnp.arange(slots, dtype=jnp.int32)
    living = (slot < valid_count[0])[:, None]
    grad_low = reorder(plan, jnp.where(living, cotangent[0], jnp.zeros((), LOW)), False, LOW)
    layer_rows = jnp.concatenate(
        [
            lax.dynamic_slice_in_dim(packed[:, params.size :], entry[r], 1, 0)
            for r in range(plan.rows)
        ]
    ).astype(jnp.int32)
    seg_rows = layer_rows[:, :length]
    info = jnp.concatenate(
        [entry[plan.rows :].reshape(plan.rows, ns), layer_rows[:, length:]], axis=1
    )
    out_own = attn_own[:, :, 3 * hd :]
    ffn_own, grad_low, seg_rows, info, out_own, near = sync(
        ffn_own, grad_low, seg_rows, info, out_own, near
    )
    out_wt = gather_layers(out_own)
    tables = xpos_tables(length)
    grad_low, ffn_own, tables, arrays = sync(grad_low, ffn_own, tables, gather_far(plan, near))
    ffn_own = exchange(ffn_own)
    grad_low = lax.ppermute(grad_low, BOTH, plan.there)
    normed, projected = pieces_matmul(
        arrays,
        [qkv_w],
        (0, 3 * hd, 3 * hd),
        plain_end,
        [],
        [((count, 3 * hd), "rows")],
        "project",
    )
    qkv, attended, log_total, stats_mix = attend(plan, info, projected, tables, seg_rows)
    stats_mix, grad_low, ffn_own = sync(stats_mix, grad_low, ffn_own)
    up_w = gather_layers(ffn_own[:, :, :hidden_part])
    down_wt = gather_layers(ffn_own[:, :, hidden_part:])
    stats_mix = spread_stats(plan, stats_mix, hd)
    mixed, kept = block_parts(
        plan,
        [(attended, "rows"), (stats_mix, "lanes"), (gm, "whole"), (bm, "whole")],
        out_wt,
        (hd, 0),
        mixed_left,
        True,
        "out",
    )
    state, _ = reduce_first(plan, kept)
    resid_mid = resid + reduce_last(plan, state)

    mean_ffn, scale_ffn = norm_stats(resid_mid)
    unit_ffn = (resid_mid - mean_ffn) * scale_ffn
    near = sync(*gather_near(plan, (unit_ffn * gf + bf).astype(LOW)))
    grad_later, *arrays = sync(grad_low, *gather_far(plan, near))
    grad_near = gather_near(plan, grad_later)
    ffn_in, active, slope, stats_hid = pieces_matmul(
        arrays,
        [up_w],
        (0, hidden_part, hidden_part),
        gelu_end,
        [],
        [((count, hidden_part), "rows"), ((count, hidden_part), "rows"), ((2, count), "lanes")],
        "up",
    )
    stats_hid, *grad_near = sync(stats_hid, *grad_near)
    grad_arrays = gather_far(plan, grad_near)
    stats_hid = spread_stats(plan, stats_hid, hidden_part)

    grad_all, grad_hn, sums_hid, vectors_hid, hidden_low = pieces_matmul(
        grad_arrays,
        [down_wt],
        (0, hidden_part, hidden_part),
        norm_back_end,
        [(active, "rows"), (stats_hid, "lanes"), (gh, "whole"), (bh, "whole")],
        [
            ((count, hidden_part), "rows"),
            ((2, count), "lanes"),
            ((2, hidden_part), "whole"),
            ((count, hidden_part), "rows", LOW),
        ],
        "down_back",
    )
    grad_down = matmul(grad_all, hidden_low, (0, 0)).astype(LOW)
    sums_hid = spread_sums(plan, sums_hid, hidden_part)
    sums_hid, grad_down = sync(sums_hid, grad_down)
    grad_down = scatter_layers(plan, grad_down)
    grad_hidden, kept = block_parts(
        plan,
        [
            (grad_hn, "rows"), (active, "rows"), (slope, "rows"),
            (stats_hid, "lanes"), (sums_hid, "lanes"), (gh, "whole"),
        ],
        up_w,
        (hidden_part, 0),
        hidden_left,
        True,
        "up_back",
    )
    grad_up = matmul(ffn_in, grad_hidden, (0, 0)).astype(LOW)
    state, (grad_up, hidden_low) = reduce_first(plan, kept, grad_up, hidden_low)
    grad_up = scatter_layers(plan, grad_up)
    grad_ffn_in = reduce_last(plan, state)
    grad_mid, gain_ffn_part, bias_ffn_part = norm_back(grad_ffn_in, gf, unit_ffn, scale_ffn)
    grad_mid = grad_mid + grad_low.astype(WIDE)
    (kept,) = block_parts(
        plan,
        [(hidden_low, "rows")],
        down_wt,
        (hidden_part, 0),
        plain_left,
        False,
        "down",
    )
    kept, near = sync(kept, gather_near(plan, grad_mid.astype(LOW)))
    arrays = sync(*gather_far(plan, near))
    grad_down, arrays = sync(grad_down, arrays)
    grad_down = exchange(grad_down)
    mid_all, grad_mixed, sums_mix, vectors_mix = pieces_matmul(
        arrays,
        [out_wt],
        (0, hd, hd),
        norm_back_end,
        [(attended, "rows"), (stats_mix, "lanes"), (gm, "whole"), (bm, "whole")],
        [((count, hd), "rows"), ((2, count), "lanes"), ((2, hd), "whole")],
        "out_back",
    )
    sums_mix, grad_down = sync(sums_mix, grad_down)
    grad_out = matmul(mid_all, mixed, (0, 0)).astype(LOW)
    sums_mix = spread_sums(plan, sums_mix, hd)
    sums_mix, grad_out, grad_up, kept = sync(sums_mix, grad_out, grad_up, kept)
    grad_out = scatter_layers(plan, grad_out)
    grad_proj = attend_back(
        plan, info, qkv, attended, grad_mixed, stats_mix, sums_mix, gm, log_total, tables, seg_rows
    )
    vectors = jnp.concatenate([vectors_mix, vectors_hid], axis=1)
    for step in bits(ns)[:1]:
        vectors = vectors + swap_over(vectors, "seq", step, ns)
    state, (grad_proj, vectors) = reduce_first(plan, kept, grad_proj, vectors)
    grad_qkv = matmul(normed, grad_proj, (0, 0)).astype(LOW)
    grad_proj, grad_qkv, grad_up, grad_out = sync(grad_proj, grad_qkv, exchange(grad_up), grad_out)
    grad_qkv = scatter_layers(plan, grad_qkv)
    output = (resid_mid + reduce_last(plan, state)).astype(LOW)
    (kept,) = block_parts(
        plan, [(grad_proj, "rows")], qkv_w, (3 * hd, 0), plain_left, False, "project_back"
    )
    for step in bits(ns)[1:]:
        vectors = vectors + swap_over(vectors, "seq", step, ns)
    state, (output, vectors) = reduce_first(plan, kept, output, vectors)
    output = lax.ppermute(output, BOTH, plan.back)
    grad_normed = reduce_last(plan, state)
    grad_resid, gain_attn_part, bias_attn_part = norm_back(
        grad_normed, ga, unit_attn, scale_attn
    )
    whole = jnp.stack([gain_ffn_part, bias_ffn_part, gain_attn_part, bias_attn_part])
    whole = whole.reshape(4, ns, nb, -1).transpose(2, 0, 1, 3).reshape(nb, 1, 4 * hd)
    grad_tokens, grad_qkv, output = sync((grad_mid + grad_resid).astype(LOW), grad_qkv, output)
    grad_tokens = lax.ppermute(grad_tokens, BOTH, plan.back)
    attn_grads = jnp.concatenate([grad_qkv, grad_out], axis=2)
    rows = attn_grads.shape[1]
    whole = jnp.broadcast_to(whole.astype(LOW), (nb, 16, 4 * hd))
    attn_grads = exchange(jnp.concatenate([attn_grads, whole], axis=1))
    own = jnp.sum(attn_grads[:, rows].astype(WIDE), axis=0).reshape(4, -1)
    own = sum_over(own, "seq", ns).reshape(4, ns, -1)
    own = lax.dynamic_index_in_dim(own, seq_index, 1, False)
    grad_qkv, grad_out = attn_grads[:, :rows, : 3 * hd], attn_grads[:, :rows, 3 * hd :]
    mixes = lax.dynamic_index_in_dim(vectors[:, :hd].reshape(2, ns, -1), seq_index, 1, False)
    hiddens = lax.dynamic_index_in_dim(vectors[:, hd:].reshape(2, ns, -1), seq_index, 1, False)
    grad_qkv = grad_qkv.reshape(nb, -1, 3, hd).transpose(1, 2, 0, 3).reshape(w_qkv.shape)
    grad_qkv, grad_out = grad_qkv.astype(WIDE), join_columns(plan, grad_out).astype(WIDE).T
    grad_up = join_columns(plan, grad_up).astype(WIDE)
    grad_down = join_columns(plan, grad_down).astype(WIDE).T
    output = reorder(plan, output, True, LOW)
    grad_tokens, own, mixes, hiddens, grad_qkv, grad_out, grad_up, grad_down, output = sync(
        grad_tokens, own, mixes, hiddens, grad_qkv, grad_out, grad_up, grad_down, output
    )
    return (
        output[None],
        reorder(plan, grad_tokens, True, WIDE)[None],
        grad_qkv,
        grad_out,
        grad_up,
        grad_down,
        own[2],
        own[3],
        mixes[0],
        mixes[1],
        own[0],
        own[1],
        hiddens[0],
        hiddens[1],
    )


def solution(mesh):
    plan = Plan(mesh.shape["batch"], mesh.shape["seq"])
    rows = P("batch", "seq", None)
    over_rows, over_columns, vector = P(BOTH, None), P(None, BOTH), P(BOTH)
    return jax.shard_map(
        functools.partial(shards, plan),
        mesh=mesh,
        in_specs=(rows, P("batch", None), P("batch"), rows)
        + (over_rows, over_columns, over_rows, over_columns)
        + (vector,) * 8,
        out_specs=(rows, rows, over_rows, over_columns, over_rows, over_columns) + (vector,) * 8,
        check_vma=False,
    )
```

```python
import functools

import jax
import jax.numpy as jnp
import numpy as np
from jax import lax
from jax.experimental import pallas as pl
from jax.experimental.pallas import tpu as pltpu
from jax.sharding import PartitionSpec as P

EPSILON = 1e-05
HEAD = 64
STRIPE = 256
ROWS_AT_ONCE = 256
LOW = jnp.bfloat16
WIDE = jnp.float32
BOTH = ("batch", "seq")

LAYER = (3, 0, 1, 2, 2, 1, 0, 3)
PLACE = (0, 1, 1, 1, 0, 0, 0, 1)
TURN = ((3, 0), (2, 1), (1, 2), (3, 0))


class Plan:
    def __init__(self, nb, ns):
        self.nb, self.ns = nb, ns
        self.rows = nb // ns
        self.fast = nb == 8 and ns == 4
        if self.fast:
            layer, place, turn = LAYER, PLACE, TURN
        else:
            layer = [b // self.rows for b in range(nb)]
            place = [b % self.rows for b in range(nb)]
            turn = [[0] * self.rows for _ in range(ns)]
        self.there = []
        for b in range(nb):
            for s in range(ns):
                k, p = layer[b], place[b]
                target = ((s ^ turn[k][p]) * self.rows + p) * ns + k
                self.there.append((b * ns + s, target))
        self.back = [(d, s) for s, d in self.there]
        row_of = {(layer[b], place[b]): b for b in range(nb)}
        table = []
        for b in range(nb):
            for k in range(ns):
                c, t = b % self.rows, b // self.rows
                order = [c, 1 - c] if self.fast else list(range(self.rows))
                entry = [row_of[k, p] for p in order]
                for p in order:
                    for q in range(ns):
                        entry.append(q ^ t ^ turn[k][p] if self.fast else q ^ turn[k][p])
                table.append(entry)
        self.table = np.array(table, np.int32)


def swap_over(value, axis, step, size):
    return lax.ppermute(value, axis, [(i, i ^ step) for i in range(size)])


def bits(size):
    return [1 << i for i in range(size.bit_length() - 1)]


def sum_over(value, axis, size):
    for step in bits(size):
        value = value + swap_over(value, axis, step, size)
    return value


def aligned(plan, value, step):
    if not plan.fast:
        return value
    shape = value.shape
    axis = {1: 1, 4: 2, 2: 3}[step]
    return jnp.flip(value.reshape(shape[0], 2, 2, 2, shape[1] // 8), axis).reshape(shape)


def gather_over(value, axis, size):
    index = lax.axis_index(axis)
    value = value[None]
    for step in bits(size):
        other = swap_over(value, axis, step, size)
        upper = (index & step) != 0
        value = jnp.concatenate(
            [jnp.where(upper, other, value), jnp.where(upper, value, other)], axis=0
        )
    return value


def sync(*values):
    return lax.optimization_barrier(values)


def gather_near(plan, block):
    if not plan.fast:
        slots, width = block.shape
        full = lax.all_gather(block, "batch", axis=0, tiled=False)
        full = full.reshape(plan.nb // plan.rows, plan.rows, slots, width)
        return [full.transpose(1, 0, 2, 3).reshape(plan.nb * slots, width)]
    return [block, swap_over(block, "batch", 2, 8), swap_over(block, "batch", 4, 8)]


def gather_far(plan, near):
    if not plan.fast:
        return near
    block, from_x, from_y = near
    half = block.shape[0] // 2
    far = swap_over(from_x[:half], "batch", 4, 8), swap_over(from_y[half:], "batch", 2, 8)
    other = [swap_over(piece, "batch", 1, 8) for piece in near]
    *other, far_a, far_b = sync(*other, *far)
    return [*near, far_a, far_b, *other, swap_over(far_a, "batch", 1, 8), swap_over(far_b, "batch", 1, 8)]


def reduce_first(plan, kept, *others):
    if not plan.fast:
        count, width = kept.shape
        slots = count // plan.nb
        part = kept.reshape(plan.rows, plan.nb // plan.rows, slots, width).transpose(1, 0, 2, 3)
        total = lax.psum_scatter(
            part.reshape(count, width), "batch", scatter_dimension=0, tiled=True
        )
        total, *others = sync(total, *others)
        return total.astype(WIDE), others
    over_x, far_y, over_y, near, at_x, at_y = kept
    slots, half = at_x.shape
    over_x, far_y = swap_over(over_x, "batch", 2, 8), swap_over(far_y, "batch", 4, 8)
    over_y = swap_over(over_y, "batch", 4, 8)
    over_x, far_y, over_y, *others = sync(over_x, far_y, over_y, *others)
    to_x = (at_x + far_y.astype(WIDE)).astype(LOW)
    to_y = (at_y + over_x[:slots].astype(WIDE)).astype(LOW)
    first = near[:, :half] + over_x[slots:].astype(WIDE)
    second = near[:, half:] + over_y.astype(WIDE)
    return (first, second, to_x, to_y), others


def reduce_last(plan, state):
    if not plan.fast:
        return state
    first, second, to_x, to_y = state
    from_x, from_y = swap_over(to_x, "batch", 2, 8), swap_over(to_y, "batch", 4, 8)
    from_x, from_y = sync(from_x, from_y)
    return jnp.concatenate([first + from_y.astype(WIDE), second + from_x.astype(WIDE)], axis=1)


def split_columns(plan, shard):
    rows, width = shard.shape
    return shard.reshape(rows, plan.nb, width // plan.nb).transpose(1, 0, 2)


def join_columns(plan, pieces):
    nb, rows, part = pieces.shape
    return pieces.transpose(1, 0, 2).reshape(rows, nb * part)


def exchange(pieces):
    return lax.all_to_all(pieces, "batch", 0, 0, tiled=True)


def gather_layers(pieces):
    nb, rows, part = pieces.shape
    return lax.all_gather(pieces.reshape(nb * rows, part), "seq", axis=0, tiled=True)


def scatter_layers(plan, part):
    own = lax.psum_scatter(part, "seq", scatter_dimension=0, tiled=True)
    rows, width = own.shape
    return own.reshape(plan.nb, rows // plan.nb, width)


def reorder_kernel(values, out, *, sources):
    low = lax.broadcasted_iota(jnp.int32, (values.shape[0], 128), 1) < 64
    for at, (first, second, half) in enumerate(sources):
        a = values[:, first * 128 : first * 128 + 128].astype(WIDE)
        b = values[:, second * 128 : second * 128 + 128].astype(WIDE)
        if half:
            a = pltpu.roll(a, 64, 1)
        else:
            b = pltpu.roll(b, 64, 1)
        out[:, at * 128 : at * 128 + 128] = jnp.where(low, a, b).astype(out.dtype)


def reorder(plan, values, outward, dtype):
    count, width = values.shape
    sizes = (plan.ns, plan.nb) if outward else (plan.nb, plan.ns)
    if width != plan.nb * plan.ns * 64 or sizes[0] % 2 or sizes[1] % 2:
        values = values.reshape(count, *sizes, width // (plan.nb * plan.ns))
        return values.transpose(0, 2, 1, 3).reshape(count, width).astype(dtype)
    sources = []
    for inner in range(sizes[1]):
        for outer in range(0, sizes[0], 2):
            at = outer * sizes[1] + inner
            sources.append((at // 2, (at + sizes[1]) // 2, at % 2))
    return pl.pallas_call(
        functools.partial(reorder_kernel, sources=sources),
        out_shape=jax.ShapeDtypeStruct(values.shape, dtype),
        compiler_params=pltpu.CompilerParams(vmem_limit_bytes=48 << 20),
        name="reorder",
    )(values)


def norm_stats(values):
    mean = jnp.mean(values, axis=-1, keepdims=True)
    center = values - mean
    return mean, lax.rsqrt(jnp.mean(center * center, axis=-1, keepdims=True) + EPSILON)


def spread_stats(plan, stats, count):
    mean, square = stats[0], stats[1]
    for step in bits(plan.nb):
        other = swap_over(jnp.stack([mean, square]), "batch", step, plan.nb)
        other = aligned(plan, other, step)
        gap = other[0] - mean
        mean = 0.5 * (mean + other[0])
        square = square + other[1] + gap * gap * (0.5 * count)
        count = 2 * count
    return jnp.stack([mean, lax.rsqrt(square / count + EPSILON)])


def spread_sums(plan, sums, count):
    for step in bits(plan.nb):
        sums = sums + aligned(plan, swap_over(sums, "batch", step, plan.nb), step)
    return sums / (count * plan.nb)


def norm_back(upstream, gain, unit, scale):
    scaled = upstream * gain
    first = jnp.mean(scaled, axis=-1, keepdims=True)
    second = jnp.mean(scaled * unit, axis=-1, keepdims=True)
    grad = scale * (scaled - first - unit * second)
    return grad, jnp.sum(upstream * unit, axis=0), jnp.sum(upstream, axis=0)


def xpos_tables(length):
    slot_pos = (jnp.arange(length, dtype=jnp.int32) - length // 2).astype(WIDE)
    lane = jnp.arange(128, dtype=jnp.int32)
    index = (lane % 32).astype(WIDE)
    angle = slot_pos[:, None] * jnp.exp(index * (-jnp.log(10000.0) / 32.0))[None, :]
    zeta = (index / 32.0 + 0.4) / 1.4
    growth = jnp.exp(slot_pos[:, None] * jnp.log(zeta)[None, :] / 512.0)
    cosine, sine = jnp.cos(angle), jnp.sin(angle)
    sine = jnp.where(lane % 64 < 32, -sine, sine)
    return cosine * growth, sine * growth, cosine / growth, sine / growth


def swap_halves(values):
    lane = lax.broadcasted_iota(jnp.int32, values.shape, 1)
    return jnp.where(lane % 64 < 32, pltpu.roll(values, 96, 1), pltpu.roll(values, 32, 1))


def matmul(a, b, contract):
    return lax.dot_general(a, b, ((contract[:1], contract[1:]), ((), ())), preferred_element_type=WIDE)


def as_column(row):
    return jnp.broadcast_to(row, (128, row.shape[1])).T[:, :1]


def as_row(column):
    return jnp.broadcast_to(column, (column.shape[0], 128)).T[:1]


def stat_rows(values):
    mean = jnp.mean(values, axis=-1, keepdims=True)
    center = values - mean
    square = jnp.sum(center * center, axis=-1, keepdims=True)
    return jnp.concatenate([as_row(mean), as_row(square)], axis=0)


def plain_end(acc, block, out):
    out[...] = acc


def gelu_end(acc, block, active_out, slope_out, stats_out):
    phi = 0.5 + 0.5 * lax.erf(acc * (0.5**0.5))
    active = acc * phi
    active_out[...] = active
    slope_out[...] = phi + acc * (jnp.exp(-0.5 * acc * acc) * ((2.0 * np.pi) ** -0.5))
    stats_out[...] = stat_rows(active)


def norm_back_end(acc, block, normal, stats, gain, bias, out, sums_out, vectors_out, low_out=None):
    out[...] = acc
    unit = (normal[...] - as_column(stats[0:1])) * as_column(stats[1:2])
    if low_out is not None:
        low_out[...] = (unit * gain[...] + bias[...]).astype(LOW)
    scaled = acc * gain[...]
    sums = [jnp.sum(scaled, axis=-1, keepdims=True), jnp.sum(scaled * unit, axis=-1, keepdims=True)]
    sums_out[...] = jnp.concatenate([as_row(sums[0]), as_row(sums[1])], axis=0)
    vectors = jnp.concatenate(
        [jnp.sum(acc * unit, axis=0, keepdims=True), jnp.sum(acc, axis=0, keepdims=True)], axis=0
    )

    @pl.when(block == 0)
    def _():
        vectors_out[...] = vectors

    @pl.when(block != 0)
    def _():
        vectors_out[...] += vectors


def pieces_kernel(*refs, moves, loads, step, n_arrays, n_weights, n_extra, keep, columns, end):
    arrays, weights = refs[:n_arrays], refs[n_arrays : n_arrays + n_weights]
    at = n_arrays + n_weights + n_extra
    extra = refs[n_arrays + n_weights : at]
    full, kept = refs[at], refs[at + 1] if keep else None
    outs = refs[at + 1 + keep : -6]
    rows, weight, arrived, left, loaded, stored = refs[-6:]
    block, count = pl.program_id(0), pl.num_programs(0)

    @pl.when(block == 0)
    def _():
        for index, column, row, n in loads:
            pltpu.make_async_copy(
                weights[index].at[:, pl.ds(column, weight.shape[1])],
                weight.at[pl.ds(row, n), :],
                loaded.at[0],
            ).start()
        for index, first, row, n in moves:
            pltpu.make_async_copy(
                arrays[index].at[pl.ds(first, n), :], rows.at[pl.ds(row, n), :], arrived.at[row // step]
            ).start()
        pltpu.make_async_copy(weight, weight, loaded.at[0]).wait()
        if keep:
            pltpu.make_async_copy(weight, kept, stored.at[0]).start()

    here = pl.ds(pl.multiple_of(block * step, step), step)
    pltpu.make_async_copy(rows.at[here], rows.at[here], arrived.at[block]).wait()
    pltpu.make_async_copy(rows.at[here], full.at[here], left.at[block]).start()
    acc = matmul(rows[here, :], weight[:, :columns], (1, 0))
    end(acc, block, *extra, *outs)

    @pl.when(block == count - 1)
    def _():
        for i in range(rows.shape[0] // step):
            part = pl.ds(i * step, step)
            pltpu.make_async_copy(rows.at[part], full.at[part], left.at[i]).wait()
        if keep:
            pltpu.make_async_copy(weight, kept, stored.at[0]).wait()


def moves_of(arrays, step):
    moves, total = [], 0
    for index, array in enumerate(arrays):
        for first in range(0, array.shape[0], step):
            n = min(step, array.shape[0] - first)
            moves.append((index, first, total, n))
            total += n
    return moves, total


def pieces_matmul(arrays, weights, columns, end, extra, outs, name):
    step = ROWS_AT_ONCE
    moves, total = moves_of(arrays, step)
    loads, inner = [], 0
    for index, weight in enumerate(weights):
        loads.append((index, columns[0], inner, weight.shape[0]))
        inner += weight.shape[0]
    keep = len(weights) > 1

    def spec(shape, kind):
        if kind == "rows":
            return pl.BlockSpec((step, shape[1]), lambda i: (i, 0))
        if kind == "lanes":
            return pl.BlockSpec((shape[0], step), lambda i: (0, i))
        return pl.BlockSpec(shape, lambda i: (0, 0))

    anywhere = pl.BlockSpec(memory_space=pl.ANY)
    kept = [jax.ShapeDtypeStruct((inner, columns[1]), LOW)] if keep else []
    return pl.pallas_call(
        functools.partial(
            pieces_kernel,
            moves=moves,
            loads=loads,
            step=step,
            n_arrays=len(arrays),
            n_weights=len(weights),
            n_extra=len(extra),
            keep=int(keep),
            columns=columns[2],
            end=end,
        ),
        grid=(total // step,),
        in_specs=[anywhere] * (len(arrays) + len(weights))
        + [spec(array.shape, kind) for array, kind in extra],
        out_specs=[anywhere] * (1 + keep) + [spec(*out[:2]) for out in outs],
        out_shape=[jax.ShapeDtypeStruct((total, inner), LOW)]
        + kept
        + [jax.ShapeDtypeStruct(out[0], out[2] if len(out) > 2 else WIDE) for out in outs],
        scratch_shapes=[
            pltpu.VMEM((total, inner), LOW),
            pltpu.VMEM((inner, columns[1]), LOW),
            pltpu.SemaphoreType.DMA((total // step,)),
            pltpu.SemaphoreType.DMA((total // step,)),
            pltpu.SemaphoreType.DMA((1,)),
            pltpu.SemaphoreType.DMA((1,)),
        ],
        compiler_params=pltpu.CompilerParams(vmem_limit_bytes=56 << 20),
        name=name,
    )(*arrays, *weights, *[array for array, _ in extra])


def mixed_left(values, stats, gain, bias):
    unit = (values[...] - as_column(stats[0:1])) * as_column(stats[1:2])
    return (unit * gain[...] + bias[...]).astype(LOW)


def hidden_left(grad, active, slope, stats, sums, gain):
    scale = as_column(stats[1:2])
    unit = (active[...] - as_column(stats[0:1])) * scale
    back = grad[...] * gain[...] - as_column(sums[0:1]) - unit * as_column(sums[1:2])
    return (scale * back * slope[...]).astype(LOW)


def plain_left(values):
    return values[...]


def part_kernel(*refs, n_in, make_left, keeps, ends):
    n_more = len(ends[1])
    left = make_left(*refs[:n_in])
    acc = matmul(left, refs[n_in][...], (1, 1))
    more, outs = refs[n_in + 1 : n_in + 1 + n_more], refs[n_in + 1 + n_more :]
    if keeps:
        outs[0 if ends[2] else 1][...] = left
        outs = outs[1:] if ends[2] else outs[2:]
    ends[0](acc, pl.program_id(0), *more, *outs)


def other_end(acc, block, *outs):
    if len(outs) == 1:
        outs[0][...] = acc.astype(LOW)
        return
    for i, out in enumerate(outs):

        @pl.when(block == i)
        def _(out=out):
            out[...] = acc.astype(LOW)


def own_x_end(acc, block, from_x, from_far, over_x, far_y, at_x):
    slots, half = at_x.shape

    @pl.when(block == 0)
    def _():
        total = acc + from_x[...].astype(WIDE)
        over_x[slots:] = total[:, :half].astype(LOW)
        at_x[...] = total[:, half:]

    @pl.when(block == 1)
    def _():
        total = acc + from_far[...].astype(WIDE)
        over_x[:slots] = total[:, :half].astype(LOW)
        far_y[...] = total[:, half:].astype(LOW)


def own_y_end(acc, block, from_near, from_y, over_y, near, at_y):
    half = at_y.shape[1]

    @pl.when(block == 0)
    def _():
        near[...] = acc + from_near[...].astype(WIDE)

    @pl.when(block == 1)
    def _():
        total = acc + from_y[...].astype(WIDE)
        over_y[...] = total[:, half:].astype(LOW)
        at_y[...] = total[:, :half]


def part_call(ins, weight, columns, make_left, kept, at, blocks, end, more, outs, name):
    step = ROWS_AT_ONCE
    total = next(array.shape[0] for array, kind in ins if kind == "rows")
    rows = weight.shape[0]

    def spec(array, kind):
        if kind == "rows":
            return pl.BlockSpec((step, array.shape[1]), lambda i: (at(i), 0))
        if kind == "lanes":
            return pl.BlockSpec((array.shape[0], step), lambda i: (0, at(i)))
        return pl.BlockSpec(array.shape, lambda i: (0, 0))

    once = pl.Buffered(1)
    in_specs = [spec(*item) for item in ins]
    in_specs.append(
        pl.BlockSpec((rows, columns[0]), lambda i: (0, columns[1]), pipeline_mode=once)
    )
    in_specs += [pl.BlockSpec(m.shape, lambda i: (0, 0), pipeline_mode=once) for m in more]
    operands = [array for array, _ in ins] + [weight, *more]
    out_specs, out_shape, aliases = [], [], {}
    if kept is not None:
        if kept:
            aliases[len(operands)] = 0
            in_specs.append(pl.BlockSpec(memory_space=pl.ANY))
            operands += kept
        out_specs.append(pl.BlockSpec((step, columns[0]), lambda i: (at(i), 0)))
        out_shape.append(jax.ShapeDtypeStruct((total, columns[0]), LOW))
    for shape, dtype, moves in outs:
        out_specs.append(pl.BlockSpec((step if moves else shape[0], shape[1]), lambda i, m=moves: (i if m else 0, 0)))
        out_shape.append(jax.ShapeDtypeStruct(shape, dtype))
    return pl.pallas_call(
        functools.partial(
            part_kernel,
            n_in=len(ins),
            make_left=make_left,
            keeps=kept is not None,
            ends=(end, more, not kept),
        ),
        grid=(blocks,),
        in_specs=in_specs,
        out_specs=out_specs,
        out_shape=out_shape,
        input_output_aliases=aliases,
        compiler_params=pltpu.CompilerParams(vmem_limit_bytes=56 << 20),
        name=name,
    )(*operands)


def block_parts(plan, ins, weight, columns, make_left, keeps, name):
    step, rows = ROWS_AT_ONCE, weight.shape[0]
    left = [] if keeps else None

    def call(at, blocks, end, more, outs, name):
        return part_call(ins, weight, columns, make_left, left, at, blocks, end, more, outs, name)

    if not plan.fast:
        total = next(array.shape[0] for array, kind in ins if kind == "rows")
        outs = [((total, rows), LOW, True)]
        return call(lambda i: i, total // step, other_end, [], outs, name)
    half = rows // 2
    outs = [((step, rows), LOW, False)] * 4
    outs = call(lambda i: 4 + i, 4, other_end, [], outs, name + "_other")
    if keeps:
        left = [outs[0]]
    near, at_x, at_y, far = outs[int(keeps) :]
    others = [swap_over(part, "batch", 1, 8) for part in (at_x, far, near, at_y)]
    outs = [((2 * step, half), LOW, False), ((step, half), LOW, False), ((step, half), WIDE, False)]
    outs = call(lambda i: 1 + 2 * i, 2, own_x_end, others[:2], outs, name + "_own_x")
    if keeps:
        left = [outs[0]]
    over_x, far_y, at_x = outs[int(keeps) :]
    outs = [((step, half), LOW, False), ((step, rows), WIDE, False), ((step, half), WIDE, False)]
    outs = call(lambda i: 2 * i, 2, own_y_end, others[2:], outs, name + "_own_y")
    if keeps:
        left = [outs[0]]
    over_y, near, at_y = outs[int(keeps) :]
    return *(left or []), (over_x, far_y, over_y, near, at_x, at_y)


def fill_bias(bias, valid, seg_row, seg_col, length):
    for i in range(length // STRIPE):
        low, high = i * STRIPE, (i + 1) * STRIPE
        shape = (STRIPE, high)
        query = lax.broadcasted_iota(jnp.int32, shape, 0) + low
        key = lax.broadcasted_iota(jnp.int32, shape, 1)
        same = seg_col[low:high] == seg_row[:, :high]
        allowed = (key == query) | (same & (key <= query) & (query < valid))
        bias[low:high, :high] = jnp.where(allowed, 0.0, -1e30)


def attend_kernel(
    info, proj, cos_q, sin_q, cos_k, sin_k, seg_row, seg_col, qkv, attended, log_total, stats, bias,
    *, ns, slots, hd
):
    row, head = pl.program_id(0), pl.program_id(1)
    length = ns * slots

    def place(quarter):
        return pl.multiple_of(info[row, quarter] * slots, slots)

    @pl.when(head == 0)
    def _():
        for q in range(ns):
            source, low, high = place(q), q * slots, (q + 1) * slots
            for part, (cosine, sine) in enumerate(((cos_q, sin_q), (cos_k, sin_k))):
                cosine, sine = cosine[low:high], sine[low:high]
                for pair in range(hd // 128):
                    at = part * hd + pair * 128
                    values = proj[pl.ds(source, slots), at : at + 128]
                    turned = values * cosine + swap_halves(values) * sine
                    qkv[low:high, at : at + 128] = turned.astype(LOW)
            qkv[low:high, 2 * hd :] = proj[pl.ds(source, slots), 2 * hd :].astype(LOW)
        fill_bias(bias, info[row, ns], seg_row[...], seg_col[...], length)
        log_total[...] = jnp.zeros_like(log_total)

    mine = lax.broadcasted_iota(jnp.int32, (STRIPE, hd), 1) // HEAD == head
    column = lax.broadcasted_iota(jnp.int32, (STRIPE, 128), 1) == head
    for i in range(length // STRIPE):
        low, high = i * STRIPE, (i + 1) * STRIPE
        queries = jnp.where(mine, qkv[low:high, :hd] * 0.125, jnp.zeros((), LOW))
        scores = matmul(queries, qkv[:high, hd : 2 * hd], (1, 1)) + bias[low:high, :high]
        top = jnp.max(scores, axis=-1, keepdims=True)
        weight = jnp.exp(scores - top)
        total = jnp.sum(weight, axis=-1, keepdims=True)
        summed = matmul(weight.astype(LOW), qkv[:high, 2 * hd :], (1, 0)) / total
        log_total[low:high] = jnp.where(column, top + jnp.log(total), log_total[low:high])
        for u in range(STRIPE // slots):
            to = place(i * (STRIPE // slots) + u)
            rows = slice(u * slots, (u + 1) * slots)
            attended[pl.ds(to, slots), :] = jnp.where(
                mine[rows], summed[rows], attended[pl.ds(to, slots), :]
            )

    @pl.when(head == pl.num_programs(1) - 1)
    def _():
        for q in range(ns):
            here = slice(q * slots, (q + 1) * slots)
            stats[:, here] = stat_rows(attended[here])


def attend_back_kernel(
    info, qkv, attended, grad, stats, sums, gain, log_total, cos_q, sin_q, cos_k, sin_k, seg_row, seg_col, out,
    bias, grad_low, product, grad_q, grad_k, grad_v, *, ns, slots, hd
):
    row, head = pl.program_id(0), pl.program_id(1)
    length = ns * slots

    def place(quarter):
        return pl.multiple_of(info[row, quarter] * slots, slots)

    @pl.when(head == 0)
    def _():
        for q in range(ns):
            to, low, high = place(q), q * slots, (q + 1) * slots
            values = attended[low:high]
            scale = as_column(stats[1:2, low:high])
            unit = (values - as_column(stats[0:1, low:high])) * scale
            back = grad[low:high] * gain[...] - as_column(sums[0:1, low:high])
            back = scale * (back - unit * as_column(sums[1:2, low:high]))
            grad_low[pl.ds(to, slots), :] = back.astype(LOW)
            product[pl.ds(to, slots), :] = back * values
        fill_bias(bias, info[row, ns], seg_row[...], seg_col[...], length)
        for total in (grad_q, grad_k, grad_v):
            total[...] = jnp.zeros_like(total)

    mine = lax.broadcasted_iota(jnp.int32, (STRIPE, hd), 1) // HEAD == head
    column = lax.broadcasted_iota(jnp.int32, (STRIPE, 128), 1) == head
    nothing = jnp.zeros((), LOW)
    mine_all = lax.broadcasted_iota(jnp.int32, (length, hd), 1) // HEAD == head
    keys_mine = jnp.where(mine_all, qkv[:, hd : 2 * hd], nothing)
    for i in range(length // STRIPE):
        low, high = i * STRIPE, (i + 1) * STRIPE
        queries = jnp.where(mine, qkv[low:high, :hd] * 0.125, nothing)
        upstream = jnp.where(mine, grad_low[low:high], nothing)
        delta = jnp.sum(jnp.where(mine, product[low:high], 0.0), axis=-1, keepdims=True)
        log_sum = jnp.sum(jnp.where(column, log_total[low:high], 0.0), axis=-1, keepdims=True)
        scores = matmul(queries, qkv[:high, hd : 2 * hd], (1, 1)) + bias[low:high, :high]
        prob = jnp.exp(scores - log_sum)
        grad_prob = matmul(upstream, qkv[:high, 2 * hd :], (1, 1))
        grad_s = (prob * (grad_prob - delta)).astype(LOW)
        grad_q[low:high] += matmul(grad_s, keys_mine[:high], (1, 0))
        grad_k[:high] += matmul(grad_s, queries, (0, 0))
        grad_v[:high] += matmul(prob.astype(LOW), upstream, (0, 0))

    @pl.when(head == pl.num_programs(1) - 1)
    def _():
        for q in range(ns):
            target, low, high = place(q), q * slots, (q + 1) * slots
            tables = (cos_q, sin_q, grad_q, 0.125), (cos_k, sin_k, grad_k, 1.0)
            for part, (cosine, sine, total, scale) in enumerate(tables):
                cosine, sine = cosine[low:high] * scale, sine[low:high] * scale
                for pair in range(hd // 128):
                    values = total[low:high, pair * 128 : pair * 128 + 128]
                    turned = values * cosine - swap_halves(values) * sine
                    at = part * hd + pair * 128
                    out[pl.ds(target, slots), at : at + 128] = turned.astype(LOW)
            out[pl.ds(target, slots), 2 * hd :] = grad_v[low:high].astype(LOW)


def row_block(length, width):
    return pl.BlockSpec((length, width), lambda r, h, info: (r, 0))


def shared_block(length, width):
    return pl.BlockSpec((length, width), lambda r, h, info: (0, 0))


def attend(plan, info, proj, tables, segments):
    count, width = proj.shape
    length, hd = count // plan.rows, width // 3
    slots = length // plan.ns
    return pl.pallas_call(
        functools.partial(attend_kernel, ns=plan.ns, slots=slots, hd=hd),
        grid_spec=pltpu.PrefetchScalarGridSpec(
            num_scalar_prefetch=1,
            grid=(plan.rows, hd // HEAD),
            in_specs=[
                row_block(length, width),
                *[shared_block(length, 128)] * 4,
                pl.BlockSpec((None, 1, length), lambda r, h, info: (r, 0, 0)),
                pl.BlockSpec((None, length, 1), lambda r, h, info: (r, 0, 0)),
            ],
            out_specs=[
                row_block(length, width),
                row_block(length, hd),
                row_block(length, 128),
                pl.BlockSpec((2, length), lambda r, h, info: (0, r)),
            ],
            scratch_shapes=[pltpu.VMEM((length, length), WIDE)],
        ),
        out_shape=[
            jax.ShapeDtypeStruct((count, width), LOW),
            jax.ShapeDtypeStruct((count, hd), WIDE),
            jax.ShapeDtypeStruct((count, 128), WIDE),
            jax.ShapeDtypeStruct((2, count), WIDE),
        ],
        compiler_params=pltpu.CompilerParams(vmem_limit_bytes=48 << 20),
        name="attend",
    )(info, proj, *tables, segments[:, None, :], segments[:, :, None])


def attend_back(plan, info, qkv, attended, grad, stats, sums, gain, log_total, tables, segments):
    count, width = qkv.shape
    length, hd = count // plan.rows, width // 3
    slots = length // plan.ns
    return pl.pallas_call(
        functools.partial(attend_back_kernel, ns=plan.ns, slots=slots, hd=hd),
        grid_spec=pltpu.PrefetchScalarGridSpec(
            num_scalar_prefetch=1,
            grid=(plan.rows, hd // HEAD),
            in_specs=[
                row_block(length, width),
                row_block(length, hd),
                row_block(length, hd),
                pl.BlockSpec((2, length), lambda r, h, info: (0, r)),
                pl.BlockSpec((2, length), lambda r, h, info: (0, r)),
                shared_block(1, hd),
                row_block(length, 128),
                *[shared_block(length, 128)] * 4,
                pl.BlockSpec((None, 1, length), lambda r, h, info: (r, 0, 0)),
                pl.BlockSpec((None, length, 1), lambda r, h, info: (r, 0, 0)),
            ],
            out_specs=row_block(length, width),
            scratch_shapes=[
                pltpu.VMEM((length, length), WIDE),
                pltpu.VMEM((length, hd), LOW),
                pltpu.VMEM((length, hd), WIDE),
                pltpu.VMEM((length, hd), WIDE),
                pltpu.VMEM((length, hd), WIDE),
                pltpu.VMEM((length, hd), WIDE),
            ],
        ),
        out_shape=jax.ShapeDtypeStruct((count, width), LOW),
        compiler_params=pltpu.CompilerParams(vmem_limit_bytes=48 << 20),
        name="attend_back",
    )(
        info, qkv, attended, grad, stats, sums, gain, log_total, *tables,
        segments[:, None, :], segments[:, :, None],
    )


def shards(
    plan,
    tokens,
    segments,
    valid_count,
    cotangent,
    w_qkv,
    w_out,
    w_up,
    w_down,
    gain_attn,
    bias_attn,
    gain_mix,
    bias_mix,
    gain_ffn,
    bias_ffn,
    gain_hidden,
    bias_hidden,
):
    nb, ns = plan.nb, plan.ns
    width, slots, length = tokens.shape[2], tokens.shape[1], segments.shape[1]
    hd, hidden_part = width // nb, w_up.shape[1] // nb
    batch_index, seq_index = lax.axis_index("batch"), lax.axis_index("seq")
    entry = lax.dynamic_index_in_dim(
        jnp.asarray(plan.table), batch_index * ns + seq_index, 0, keepdims=False
    )

    tokens_low = reorder(plan, tokens[0], False, LOW)
    group = w_qkv.reshape(w_qkv.shape[0], 3, nb, hd).transpose(2, 0, 1, 3)
    group = group.reshape(nb, -1, 3 * hd)
    attn_own = jnp.concatenate([group, split_columns(plan, w_out.T)], axis=2)
    tokens_low, attn_own = sync(tokens_low, attn_own)
    attn_own = exchange(attn_own)
    qkv_w = gather_layers(attn_own[:, :, : 3 * hd])
    tokens_low = lax.ppermute(tokens_low, BOTH, plan.there)

    own_params = (gain_attn, bias_attn, gain_mix, bias_mix, gain_ffn, bias_ffn, gain_hidden, bias_hidden)
    tokens_low, cotangent, attn_own, *own_params = sync(tokens_low, cotangent, attn_own, *own_params)
    params = gather_over(jnp.concatenate([p.astype(WIDE) for p in own_params]), "seq", ns)
    packed = jnp.concatenate(
        [params.reshape(-1), segments[0].astype(WIDE), valid_count.astype(WIDE)]
    )
    packed = gather_over(packed, "batch", nb)
    spread = packed[:, : params.size].reshape(nb, ns, -1)
    vectors, at = [], 0
    for index, p in enumerate(own_params):
        piece = spread[:, :, at : at + p.shape[0]]
        at += p.shape[0]
        if index in (0, 1, 4, 5):
            vectors.append(piece.transpose(1, 0, 2).reshape(1, -1))
        else:
            vectors.append(lax.dynamic_index_in_dim(piece, batch_index, 0, False).reshape(1, -1))
    ga, ba, gm, bm, gf, bf, gh, bh = vectors
    count = plan.rows * length
    resid = tokens_low.astype(WIDE)
    mean_attn, scale_attn = norm_stats(resid)
    unit_attn = (resid - mean_attn) * scale_attn
    normed_low = (unit_attn * ga + ba).astype(LOW)
    normed_low, packed, cotangent, w_up, w_down, gm, bm, gf, bf, gh, bh = sync(
        normed_low, packed, cotangent, w_up, w_down, gm, bm, gf, bf, gh, bh
    )

    near = gather_near(plan, normed_low)
    ffn_own = jnp.concatenate([split_columns(plan, w) for w in (w_up, w_down.T)], axis=2)
    slot = seq_index * slots + jnp.arange(slots, dtype=jnp.int32)
    living = (slot < valid_count[0])[:, None]
    grad_low = reorder(plan, jnp.where(living, cotangent[0], jnp.zeros((), LOW)), False, LOW)
    layer_rows = jnp.concatenate(
        [
            lax.dynamic_slice_in_dim(packed[:, params.size :], entry[r], 1, 0)
            for r in range(plan.rows)
        ]
    ).astype(jnp.int32)
    seg_rows = layer_rows[:, :length]
    info = jnp.concatenate(
        [entry[plan.rows :].reshape(plan.rows, ns), layer_rows[:, length:]], axis=1
    )
    out_own = attn_own[:, :, 3 * hd :]
    ffn_own, grad_low, seg_rows, info, out_own, near = sync(
        ffn_own, grad_low, seg_rows, info, out_own, near
    )
    out_wt = gather_layers(out_own)
    tables = xpos_tables(length)
    grad_low, ffn_own, tables, arrays = sync(grad_low, ffn_own, tables, gather_far(plan, near))
    ffn_own = exchange(ffn_own)
    grad_low = lax.ppermute(grad_low, BOTH, plan.there)
    normed, projected = pieces_matmul(
        arrays,
        [qkv_w],
        (0, 3 * hd, 3 * hd),
        plain_end,
        [],
        [((count, 3 * hd), "rows")],
        "project",
    )
    qkv, attended, log_total, stats_mix = attend(plan, info, projected, tables, seg_rows)
    stats_mix, grad_low, ffn_own = sync(stats_mix, grad_low, ffn_own)
    up_w = gather_layers(ffn_own[:, :, :hidden_part])
    down_wt = gather_layers(ffn_own[:, :, hidden_part:])
    stats_mix = spread_stats(plan, stats_mix, hd)
    mixed, kept = block_parts(
        plan,
        [(attended, "rows"), (stats_mix, "lanes"), (gm, "whole"), (bm, "whole")],
        out_wt,
        (hd, 0),
        mixed_left,
        True,
        "out",
    )
    state, _ = reduce_first(plan, kept)
    resid_mid = resid + reduce_last(plan, state)

    mean_ffn, scale_ffn = norm_stats(resid_mid)
    unit_ffn = (resid_mid - mean_ffn) * scale_ffn
    near = sync(*gather_near(plan, (unit_ffn * gf + bf).astype(LOW)))
    grad_later, *arrays = sync(grad_low, *gather_far(plan, near))
    grad_near = gather_near(plan, grad_later)
    ffn_in, active, slope, stats_hid = pieces_matmul(
        arrays,
        [up_w],
        (0, hidden_part, hidden_part),
        gelu_end,
        [],
        [((count, hidden_part), "rows"), ((count, hidden_part), "rows"), ((2, count), "lanes")],
        "up",
    )
    stats_hid, *grad_near = sync(stats_hid, *grad_near)
    grad_arrays = gather_far(plan, grad_near)
    stats_hid = spread_stats(plan, stats_hid, hidden_part)

    grad_all, grad_hn, sums_hid, vectors_hid, hidden_low = pieces_matmul(
        grad_arrays,
        [down_wt],
        (0, hidden_part, hidden_part),
        norm_back_end,
        [(active, "rows"), (stats_hid, "lanes"), (gh, "whole"), (bh, "whole")],
        [
            ((count, hidden_part), "rows"),
            ((2, count), "lanes"),
            ((2, hidden_part), "whole"),
            ((count, hidden_part), "rows", LOW),
        ],
        "down_back",
    )
    grad_down = matmul(grad_all, hidden_low, (0, 0)).astype(LOW)
    sums_hid = spread_sums(plan, sums_hid, hidden_part)
    sums_hid, grad_down = sync(sums_hid, grad_down)
    grad_down = scatter_layers(plan, grad_down)
    grad_hidden, kept = block_parts(
        plan,
        [
            (grad_hn, "rows"), (active, "rows"), (slope, "rows"),
            (stats_hid, "lanes"), (sums_hid, "lanes"), (gh, "whole"),
        ],
        up_w,
        (hidden_part, 0),
        hidden_left,
        True,
        "up_back",
    )
    grad_up = matmul(ffn_in, grad_hidden, (0, 0)).astype(LOW)
    state, (grad_up, hidden_low) = reduce_first(plan, kept, grad_up, hidden_low)
    grad_up = scatter_layers(plan, grad_up)
    grad_ffn_in = reduce_last(plan, state)
    grad_mid, gain_ffn_part, bias_ffn_part = norm_back(grad_ffn_in, gf, unit_ffn, scale_ffn)
    grad_mid = grad_mid + grad_low.astype(WIDE)
    (kept,) = block_parts(
        plan,
        [(hidden_low, "rows")],
        down_wt,
        (hidden_part, 0),
        plain_left,
        False,
        "down",
    )
    kept, near = sync(kept, gather_near(plan, grad_mid.astype(LOW)))
    arrays = sync(*gather_far(plan, near))
    grad_down, arrays = sync(grad_down, arrays)
    grad_down = exchange(grad_down)
    mid_all, grad_mixed, sums_mix, vectors_mix = pieces_matmul(
        arrays,
        [out_wt],
        (0, hd, hd),
        norm_back_end,
        [(attended, "rows"), (stats_mix, "lanes"), (gm, "whole"), (bm, "whole")],
        [((count, hd), "rows"), ((2, count), "lanes"), ((2, hd), "whole")],
        "out_back",
    )
    sums_mix, grad_down = sync(sums_mix, grad_down)
    grad_out = matmul(mid_all, mixed, (0, 0)).astype(LOW)
    sums_mix = spread_sums(plan, sums_mix, hd)
    sums_mix, grad_out, grad_up, kept = sync(sums_mix, grad_out, grad_up, kept)
    grad_out = scatter_layers(plan, grad_out)
    grad_proj = attend_back(
        plan, info, qkv, attended, grad_mixed, stats_mix, sums_mix, gm, log_total, tables, seg_rows
    )
    vectors = jnp.concatenate([vectors_mix, vectors_hid], axis=1)
    for step in bits(ns)[:1]:
        vectors = vectors + swap_over(vectors, "seq", step, ns)
    state, (grad_proj, vectors) = reduce_first(plan, kept, grad_proj, vectors)
    grad_qkv = matmul(normed, grad_proj, (0, 0)).astype(LOW)
    grad_proj, grad_qkv, grad_up, grad_out = sync(grad_proj, grad_qkv, exchange(grad_up), grad_out)
    grad_qkv = scatter_layers(plan, grad_qkv)
    output = (resid_mid + reduce_last(plan, state)).astype(LOW)
    (kept,) = block_parts(
        plan, [(grad_proj, "rows")], qkv_w, (3 * hd, 0), plain_left, False, "project_back"
    )
    for step in bits(ns)[1:]:
        vectors = vectors + swap_over(vectors, "seq", step, ns)
    state, (output, vectors) = reduce_first(plan, kept, output, vectors)
    output = lax.ppermute(output, BOTH, plan.back)
    grad_normed = reduce_last(plan, state)
    grad_resid, gain_attn_part, bias_attn_part = norm_back(
        grad_normed, ga, unit_attn, scale_attn
    )
    whole = jnp.stack([gain_ffn_part, bias_ffn_part, gain_attn_part, bias_attn_part])
    whole = sum_over(whole, "seq", ns)
    whole = whole.reshape(4, ns, nb, -1).transpose(2, 0, 1, 3).reshape(nb, 1, 4 * hd)
    grad_tokens, grad_qkv, whole = sync((grad_mid + grad_resid).astype(LOW), grad_qkv, whole)
    grad_tokens = lax.ppermute(grad_tokens, BOTH, plan.back)
    attn_grads = jnp.concatenate([grad_qkv, grad_out], axis=2)
    rows = attn_grads.shape[1]
    whole = jnp.broadcast_to(whole.astype(LOW), (nb, 16, 4 * hd))
    attn_grads = exchange(jnp.concatenate([attn_grads, whole], axis=1))
    own = jnp.sum(attn_grads[:, rows].astype(WIDE), axis=0).reshape(4, ns, -1)
    own = lax.dynamic_index_in_dim(own, seq_index, 1, False)
    grad_qkv, grad_out = attn_grads[:, :rows, : 3 * hd], attn_grads[:, :rows, 3 * hd :]
    mixes = lax.dynamic_index_in_dim(vectors[:, :hd].reshape(2, ns, -1), seq_index, 1, False)
    hiddens = lax.dynamic_index_in_dim(vectors[:, hd:].reshape(2, ns, -1), seq_index, 1, False)
    grad_qkv = grad_qkv.reshape(nb, -1, 3, hd).transpose(1, 2, 0, 3).reshape(w_qkv.shape)
    grad_qkv, grad_out = grad_qkv.astype(WIDE), join_columns(plan, grad_out).astype(WIDE).T
    grad_up = join_columns(plan, grad_up).astype(WIDE)
    grad_down = join_columns(plan, grad_down).astype(WIDE).T
    output = reorder(plan, output, True, LOW)
    grad_tokens, own, mixes, hiddens, grad_qkv, grad_out, grad_up, grad_down, output = sync(
        grad_tokens, own, mixes, hiddens, grad_qkv, grad_out, grad_up, grad_down, output
    )
    return (
        output[None],
        reorder(plan, grad_tokens, True, WIDE)[None],
        grad_qkv,
        grad_out,
        grad_up,
        grad_down,
        own[2],
        own[3],
        mixes[0],
        mixes[1],
        own[0],
        own[1],
        hiddens[0],
        hiddens[1],
    )


def solution(mesh):
    plan = Plan(mesh.shape["batch"], mesh.shape["seq"])
    rows = P("batch", "seq", None)
    over_rows, over_columns, vector = P(BOTH, None), P(None, BOTH), P(BOTH)
    return jax.shard_map(
        functools.partial(shards, plan),
        mesh=mesh,
        in_specs=(rows, P("batch", None), P("batch"), rows)
        + (over_rows, over_columns, over_rows, over_columns)
        + (vector,) * 8,
        out_specs=(rows, rows, over_rows, over_columns, over_rows, over_columns) + (vector,) * 8,
        check_vma=False,
    )
```

```python
import functools

import jax
import jax.numpy as jnp
import numpy as np
from jax import lax
from jax.experimental import pallas as pl
from jax.experimental.pallas import tpu as pltpu
from jax.sharding import PartitionSpec as P

EPSILON = 1e-05
HEAD = 64
STRIPE = 256
ROWS_AT_ONCE = 256
LOW = jnp.bfloat16
WIDE = jnp.float32
BOTH = ("batch", "seq")

LAYER = (3, 0, 1, 2, 2, 1, 0, 3)
PLACE = (0, 1, 1, 1, 0, 0, 0, 1)
TURN = ((3, 0), (2, 1), (1, 2), (3, 0))


class Plan:
    def __init__(self, nb, ns):
        self.nb, self.ns = nb, ns
        self.rows = nb // ns
        self.fast = nb == 8 and ns == 4
        if self.fast:
            layer, place, turn = LAYER, PLACE, TURN
        else:
            layer = [b // self.rows for b in range(nb)]
            place = [b % self.rows for b in range(nb)]
            turn = [[0] * self.rows for _ in range(ns)]
        self.there = []
        for b in range(nb):
            for s in range(ns):
                k, p = layer[b], place[b]
                target = ((s ^ turn[k][p]) * self.rows + p) * ns + k
                self.there.append((b * ns + s, target))
        self.back = [(d, s) for s, d in self.there]
        row_of = {(layer[b], place[b]): b for b in range(nb)}
        table = []
        for b in range(nb):
            for k in range(ns):
                c, t = b % self.rows, b // self.rows
                order = [c, 1 - c] if self.fast else list(range(self.rows))
                entry = [row_of[k, p] for p in order]
                for p in order:
                    for q in range(ns):
                        entry.append(q ^ t ^ turn[k][p] if self.fast else q ^ turn[k][p])
                table.append(entry)
        self.table = np.array(table, np.int32)


def swap_over(value, axis, step, size):
    return lax.ppermute(value, axis, [(i, i ^ step) for i in range(size)])


def bits(size):
    return [1 << i for i in range(size.bit_length() - 1)]


def sum_over(value, axis, size):
    for step in bits(size):
        value = value + swap_over(value, axis, step, size)
    return value


def aligned(plan, value, step):
    if not plan.fast:
        return value
    shape = value.shape
    axis = {1: 1, 4: 2, 2: 3}[step]
    return jnp.flip(value.reshape(shape[0], 2, 2, 2, shape[1] // 8), axis).reshape(shape)


def gather_over(value, axis, size):
    index = lax.axis_index(axis)
    value = value[None]
    for step in bits(size):
        other = swap_over(value, axis, step, size)
        upper = (index & step) != 0
        value = jnp.concatenate(
            [jnp.where(upper, other, value), jnp.where(upper, value, other)], axis=0
        )
    return value


def sync(*values):
    return lax.optimization_barrier(values)


def gather_near(plan, block):
    if not plan.fast:
        slots, width = block.shape
        full = lax.all_gather(block, "batch", axis=0, tiled=False)
        full = full.reshape(plan.nb // plan.rows, plan.rows, slots, width)
        return [full.transpose(1, 0, 2, 3).reshape(plan.nb * slots, width)]
    return [block, swap_over(block, "batch", 2, 8), swap_over(block, "batch", 4, 8)]


def gather_far(plan, near):
    if not plan.fast:
        return near
    block, from_x, from_y = near
    half = block.shape[0] // 2
    far = swap_over(from_x[:half], "batch", 4, 8), swap_over(from_y[half:], "batch", 2, 8)
    other = [swap_over(piece, "batch", 1, 8) for piece in near]
    *other, far_a, far_b = sync(*other, *far)
    return [*near, far_a, far_b, *other, swap_over(far_a, "batch", 1, 8), swap_over(far_b, "batch", 1, 8)]


def reduce_first(plan, kept, *others):
    if not plan.fast:
        count, width = kept.shape
        slots = count // plan.nb
        part = kept.reshape(plan.rows, plan.nb // plan.rows, slots, width).transpose(1, 0, 2, 3)
        total = lax.psum_scatter(
            part.reshape(count, width), "batch", scatter_dimension=0, tiled=True
        )
        total, *others = sync(total, *others)
        return total.astype(WIDE), others
    over_x, far_y, over_y, near, at_x, at_y = kept
    slots, half = at_x.shape
    over_x, far_y = swap_over(over_x, "batch", 2, 8), swap_over(far_y, "batch", 4, 8)
    over_y = swap_over(over_y, "batch", 4, 8)
    over_x, far_y, over_y, *others = sync(over_x, far_y, over_y, *others)
    to_x = (at_x + far_y.astype(WIDE)).astype(LOW)
    to_y = (at_y + over_x[:slots].astype(WIDE)).astype(LOW)
    first = near[:, :half] + over_x[slots:].astype(WIDE)
    second = near[:, half:] + over_y.astype(WIDE)
    return (first, second, to_x, to_y), others


def reduce_last(plan, state, *others):
    if not plan.fast:
        return state, others
    first, second, to_x, to_y = state
    from_x, from_y = swap_over(to_x, "batch", 2, 8), swap_over(to_y, "batch", 4, 8)
    from_x, from_y, *others = sync(from_x, from_y, *others)
    total = jnp.concatenate([first + from_y.astype(WIDE), second + from_x.astype(WIDE)], axis=1)
    return total, others


def split_columns(plan, shard):
    rows, width = shard.shape
    return shard.reshape(rows, plan.nb, width // plan.nb).transpose(1, 0, 2)


def join_columns(plan, pieces):
    nb, rows, part = pieces.shape
    return pieces.transpose(1, 0, 2).reshape(rows, nb * part)


def exchange(pieces):
    return lax.all_to_all(pieces, "batch", 0, 0, tiled=True)


def gather_layers(pieces):
    nb, rows, part = pieces.shape
    return lax.all_gather(pieces.reshape(nb * rows, part), "seq", axis=0, tiled=True)


def scatter_layers(plan, part):
    own = lax.psum_scatter(part, "seq", scatter_dimension=0, tiled=True)
    rows, width = own.shape
    return own.reshape(plan.nb, rows // plan.nb, width)


def reorder_kernel(values, out, *, sources):
    low = lax.broadcasted_iota(jnp.int32, (values.shape[0], 128), 1) < 64
    for at, (first, second, half) in enumerate(sources):
        a = values[:, first * 128 : first * 128 + 128].astype(WIDE)
        b = values[:, second * 128 : second * 128 + 128].astype(WIDE)
        if half:
            a = pltpu.roll(a, 64, 1)
        else:
            b = pltpu.roll(b, 64, 1)
        out[:, at * 128 : at * 128 + 128] = jnp.where(low, a, b).astype(out.dtype)


def reorder(plan, values, outward, dtype):
    count, width = values.shape
    sizes = (plan.ns, plan.nb) if outward else (plan.nb, plan.ns)
    if width != plan.nb * plan.ns * 64 or sizes[0] % 2 or sizes[1] % 2:
        values = values.reshape(count, *sizes, width // (plan.nb * plan.ns))
        return values.transpose(0, 2, 1, 3).reshape(count, width).astype(dtype)
    sources = []
    for inner in range(sizes[1]):
        for outer in range(0, sizes[0], 2):
            at = outer * sizes[1] + inner
            sources.append((at // 2, (at + sizes[1]) // 2, at % 2))
    return pl.pallas_call(
        functools.partial(reorder_kernel, sources=sources),
        out_shape=jax.ShapeDtypeStruct(values.shape, dtype),
        compiler_params=pltpu.CompilerParams(vmem_limit_bytes=48 << 20),
        name="reorder",
    )(values)


def norm_stats(values):
    mean = jnp.mean(values, axis=-1, keepdims=True)
    center = values - mean
    return mean, lax.rsqrt(jnp.mean(center * center, axis=-1, keepdims=True) + EPSILON)


def spread_stats(plan, stats, count):
    mean, square = stats[0], stats[1]
    for step in bits(plan.nb):
        other = swap_over(jnp.stack([mean, square]), "batch", step, plan.nb)
        other = aligned(plan, other, step)
        gap = other[0] - mean
        mean = 0.5 * (mean + other[0])
        square = square + other[1] + gap * gap * (0.5 * count)
        count = 2 * count
    return jnp.stack([mean, lax.rsqrt(square / count + EPSILON)])


def spread_sums(plan, sums, count):
    for step in bits(plan.nb):
        sums = sums + aligned(plan, swap_over(sums, "batch", step, plan.nb), step)
    return sums / (count * plan.nb)


def norm_back(upstream, gain, unit, scale):
    scaled = upstream * gain
    first = jnp.mean(scaled, axis=-1, keepdims=True)
    second = jnp.mean(scaled * unit, axis=-1, keepdims=True)
    grad = scale * (scaled - first - unit * second)
    return grad, jnp.sum(upstream * unit, axis=0), jnp.sum(upstream, axis=0)


def xpos_tables(length):
    slot_pos = (jnp.arange(length, dtype=jnp.int32) - length // 2).astype(WIDE)
    lane = jnp.arange(128, dtype=jnp.int32)
    index = (lane % 32).astype(WIDE)
    angle = slot_pos[:, None] * jnp.exp(index * (-jnp.log(10000.0) / 32.0))[None, :]
    zeta = (index / 32.0 + 0.4) / 1.4
    growth = jnp.exp(slot_pos[:, None] * jnp.log(zeta)[None, :] / 512.0)
    cosine, sine = jnp.cos(angle), jnp.sin(angle)
    sine = jnp.where(lane % 64 < 32, -sine, sine)
    return cosine * growth, sine * growth, cosine / growth, sine / growth


def swap_halves(values):
    lane = lax.broadcasted_iota(jnp.int32, values.shape, 1)
    return jnp.where(lane % 64 < 32, pltpu.roll(values, 96, 1), pltpu.roll(values, 32, 1))


def matmul(a, b, contract):
    return lax.dot_general(a, b, ((contract[:1], contract[1:]), ((), ())), preferred_element_type=WIDE)


def as_column(row):
    return jnp.broadcast_to(row, (128, row.shape[1])).T[:, :1]


def as_row(column):
    return jnp.broadcast_to(column, (column.shape[0], 128)).T[:1]


def stat_rows(values):
    mean = jnp.mean(values, axis=-1, keepdims=True)
    center = values - mean
    square = jnp.sum(center * center, axis=-1, keepdims=True)
    return jnp.concatenate([as_row(mean), as_row(square)], axis=0)


def plain_end(acc, block, out):
    out[...] = acc


def gelu_end(acc, block, active_out, slope_out, stats_out):
    phi = 0.5 + 0.5 * lax.erf(acc * (0.5**0.5))
    active = acc * phi
    active_out[...] = active
    slope_out[...] = phi + acc * (jnp.exp(-0.5 * acc * acc) * ((2.0 * np.pi) ** -0.5))
    stats_out[...] = stat_rows(active)


def norm_back_end(acc, block, normal, stats, gain, bias, out, sums_out, vectors_out, low_out=None):
    out[...] = acc
    unit = (normal[...] - as_column(stats[0:1])) * as_column(stats[1:2])
    if low_out is not None:
        low_out[...] = (unit * gain[...] + bias[...]).astype(LOW)
    scaled = acc * gain[...]
    sums = [jnp.sum(scaled, axis=-1, keepdims=True), jnp.sum(scaled * unit, axis=-1, keepdims=True)]
    sums_out[...] = jnp.concatenate([as_row(sums[0]), as_row(sums[1])], axis=0)
    vectors = jnp.concatenate(
        [jnp.sum(acc * unit, axis=0, keepdims=True), jnp.sum(acc, axis=0, keepdims=True)], axis=0
    )

    @pl.when(block == 0)
    def _():
        vectors_out[...] = vectors

    @pl.when(block != 0)
    def _():
        vectors_out[...] += vectors


def pieces_kernel(*refs, moves, loads, step, n_arrays, n_weights, n_extra, keep, columns, end):
    arrays, weights = refs[:n_arrays], refs[n_arrays : n_arrays + n_weights]
    at = n_arrays + n_weights + n_extra
    extra = refs[n_arrays + n_weights : at]
    full, kept = refs[at], refs[at + 1] if keep else None
    outs = refs[at + 1 + keep : -6]
    rows, weight, arrived, left, loaded, stored = refs[-6:]
    block, count = pl.program_id(0), pl.num_programs(0)

    @pl.when(block == 0)
    def _():
        for index, column, row, n in loads:
            pltpu.make_async_copy(
                weights[index].at[:, pl.ds(column, weight.shape[1])],
                weight.at[pl.ds(row, n), :],
                loaded.at[0],
            ).start()
        for index, first, row, n in moves:
            pltpu.make_async_copy(
                arrays[index].at[pl.ds(first, n), :], rows.at[pl.ds(row, n), :], arrived.at[row // step]
            ).start()
        pltpu.make_async_copy(weight, weight, loaded.at[0]).wait()
        if keep:
            pltpu.make_async_copy(weight, kept, stored.at[0]).start()

    here = pl.ds(pl.multiple_of(block * step, step), step)
    pltpu.make_async_copy(rows.at[here], rows.at[here], arrived.at[block]).wait()
    pltpu.make_async_copy(rows.at[here], full.at[here], left.at[block]).start()
    acc = matmul(rows[here, :], weight[:, :columns], (1, 0))
    end(acc, block, *extra, *outs)

    @pl.when(block == count - 1)
    def _():
        for i in range(rows.shape[0] // step):
            part = pl.ds(i * step, step)
            pltpu.make_async_copy(rows.at[part], full.at[part], left.at[i]).wait()
        if keep:
            pltpu.make_async_copy(weight, kept, stored.at[0]).wait()


def moves_of(arrays, step):
    moves, total = [], 0
    for index, array in enumerate(arrays):
        for first in range(0, array.shape[0], step):
            n = min(step, array.shape[0] - first)
            moves.append((index, first, total, n))
            total += n
    return moves, total


def pieces_matmul(arrays, weights, columns, end, extra, outs, name):
    step = ROWS_AT_ONCE
    moves, total = moves_of(arrays, step)
    loads, inner = [], 0
    for index, weight in enumerate(weights):
        loads.append((index, columns[0], inner, weight.shape[0]))
        inner += weight.shape[0]
    keep = len(weights) > 1

    def spec(shape, kind):
        if kind == "rows":
            return pl.BlockSpec((step, shape[1]), lambda i: (i, 0))
        if kind == "lanes":
            return pl.BlockSpec((shape[0], step), lambda i: (0, i))
        return pl.BlockSpec(shape, lambda i: (0, 0))

    anywhere = pl.BlockSpec(memory_space=pl.ANY)
    kept = [jax.ShapeDtypeStruct((inner, columns[1]), LOW)] if keep else []
    return pl.pallas_call(
        functools.partial(
            pieces_kernel,
            moves=moves,
            loads=loads,
            step=step,
            n_arrays=len(arrays),
            n_weights=len(weights),
            n_extra=len(extra),
            keep=int(keep),
            columns=columns[2],
            end=end,
        ),
        grid=(total // step,),
        in_specs=[anywhere] * (len(arrays) + len(weights))
        + [spec(array.shape, kind) for array, kind in extra],
        out_specs=[anywhere] * (1 + keep) + [spec(*out[:2]) for out in outs],
        out_shape=[jax.ShapeDtypeStruct((total, inner), LOW)]
        + kept
        + [jax.ShapeDtypeStruct(out[0], out[2] if len(out) > 2 else WIDE) for out in outs],
        scratch_shapes=[
            pltpu.VMEM((total, inner), LOW),
            pltpu.VMEM((inner, columns[1]), LOW),
            pltpu.SemaphoreType.DMA((total // step,)),
            pltpu.SemaphoreType.DMA((total // step,)),
            pltpu.SemaphoreType.DMA((1,)),
            pltpu.SemaphoreType.DMA((1,)),
        ],
        compiler_params=pltpu.CompilerParams(vmem_limit_bytes=56 << 20),
        name=name,
    )(*arrays, *weights, *[array for array, _ in extra])


def mixed_left(values, stats, gain, bias):
    unit = (values[...] - as_column(stats[0:1])) * as_column(stats[1:2])
    return (unit * gain[...] + bias[...]).astype(LOW)


def hidden_left(grad, active, slope, stats, sums, gain):
    scale = as_column(stats[1:2])
    unit = (active[...] - as_column(stats[0:1])) * scale
    back = grad[...] * gain[...] - as_column(sums[0:1]) - unit * as_column(sums[1:2])
    return (scale * back * slope[...]).astype(LOW)


def plain_left(values):
    return values[...]


def part_kernel(*refs, n_in, make_left, keeps, ends):
    n_more = len(ends[1])
    left = make_left(*refs[:n_in])
    acc = matmul(left, refs[n_in][...], (1, 1))
    more, outs = refs[n_in + 1 : n_in + 1 + n_more], refs[n_in + 1 + n_more :]
    if keeps:
        outs[0 if ends[2] else 1][...] = left
        outs = outs[1:] if ends[2] else outs[2:]
    ends[0](acc, pl.program_id(0), *more, *outs)


def other_end(acc, block, *outs):
    if len(outs) == 1:
        outs[0][...] = acc.astype(LOW)
        return
    for i, out in enumerate(outs):

        @pl.when(block == i)
        def _(out=out):
            out[...] = acc.astype(LOW)


def own_x_end(acc, block, from_x, from_far, over_x, far_y, at_x):
    slots, half = at_x.shape

    @pl.when(block == 0)
    def _():
        total = acc + from_x[...].astype(WIDE)
        over_x[slots:] = total[:, :half].astype(LOW)
        at_x[...] = total[:, half:]

    @pl.when(block == 1)
    def _():
        total = acc + from_far[...].astype(WIDE)
        over_x[:slots] = total[:, :half].astype(LOW)
        far_y[...] = total[:, half:].astype(LOW)


def own_y_end(acc, block, from_near, from_y, over_y, near, at_y):
    half = at_y.shape[1]

    @pl.when(block == 0)
    def _():
        near[...] = acc + from_near[...].astype(WIDE)

    @pl.when(block == 1)
    def _():
        total = acc + from_y[...].astype(WIDE)
        over_y[...] = total[:, half:].astype(LOW)
        at_y[...] = total[:, :half]


def part_call(ins, weight, columns, make_left, kept, at, blocks, end, more, outs, name):
    step = ROWS_AT_ONCE
    total = next(array.shape[0] for array, kind in ins if kind == "rows")
    rows = weight.shape[0]

    def spec(array, kind):
        if kind == "rows":
            return pl.BlockSpec((step, array.shape[1]), lambda i: (at(i), 0))
        if kind == "lanes":
            return pl.BlockSpec((array.shape[0], step), lambda i: (0, at(i)))
        return pl.BlockSpec(array.shape, lambda i: (0, 0))

    once = pl.Buffered(1)
    in_specs = [spec(*item) for item in ins]
    in_specs.append(
        pl.BlockSpec((rows, columns[0]), lambda i: (0, columns[1]), pipeline_mode=once)
    )
    in_specs += [pl.BlockSpec(m.shape, lambda i: (0, 0), pipeline_mode=once) for m in more]
    operands = [array for array, _ in ins] + [weight, *more]
    out_specs, out_shape, aliases = [], [], {}
    if kept is not None:
        if kept:
            aliases[len(operands)] = 0
            in_specs.append(pl.BlockSpec(memory_space=pl.ANY))
            operands += kept
        out_specs.append(pl.BlockSpec((step, columns[0]), lambda i: (at(i), 0)))
        out_shape.append(jax.ShapeDtypeStruct((total, columns[0]), LOW))
    for shape, dtype, moves in outs:
        out_specs.append(pl.BlockSpec((step if moves else shape[0], shape[1]), lambda i, m=moves: (i if m else 0, 0)))
        out_shape.append(jax.ShapeDtypeStruct(shape, dtype))
    return pl.pallas_call(
        functools.partial(
            part_kernel,
            n_in=len(ins),
            make_left=make_left,
            keeps=kept is not None,
            ends=(end, more, not kept),
        ),
        grid=(blocks,),
        in_specs=in_specs,
        out_specs=out_specs,
        out_shape=out_shape,
        input_output_aliases=aliases,
        compiler_params=pltpu.CompilerParams(vmem_limit_bytes=56 << 20),
        name=name,
    )(*operands)


def block_parts(plan, ins, weight, columns, make_left, keeps, name):
    step, rows = ROWS_AT_ONCE, weight.shape[0]
    left = [] if keeps else None

    def call(at, blocks, end, more, outs, name):
        return part_call(ins, weight, columns, make_left, left, at, blocks, end, more, outs, name)

    if not plan.fast:
        total = next(array.shape[0] for array, kind in ins if kind == "rows")
        outs = [((total, rows), LOW, True)]
        return call(lambda i: i, total // step, other_end, [], outs, name)
    half = rows // 2
    outs = [((step, rows), LOW, False)] * 4
    outs = call(lambda i: 4 + i, 4, other_end, [], outs, name + "_other")
    if keeps:
        left = [outs[0]]
    near, at_x, at_y, far = outs[int(keeps) :]
    others = [swap_over(part, "batch", 1, 8) for part in (at_x, far, near, at_y)]
    outs = [((2 * step, half), LOW, False), ((step, half), LOW, False), ((step, half), WIDE, False)]
    outs = call(lambda i: 1 + 2 * i, 2, own_x_end, others[:2], outs, name + "_own_x")
    if keeps:
        left = [outs[0]]
    over_x, far_y, at_x = outs[int(keeps) :]
    outs = [((step, half), LOW, False), ((step, rows), WIDE, False), ((step, half), WIDE, False)]
    outs = call(lambda i: 2 * i, 2, own_y_end, others[2:], outs, name + "_own_y")
    if keeps:
        left = [outs[0]]
    over_y, near, at_y = outs[int(keeps) :]
    return *(left or []), (over_x, far_y, over_y, near, at_x, at_y)


def fill_bias(bias, valid, seg_row, seg_col, length):
    for i in range(length // STRIPE):
        low, high = i * STRIPE, (i + 1) * STRIPE
        shape = (STRIPE, high)
        query = lax.broadcasted_iota(jnp.int32, shape, 0) + low
        key = lax.broadcasted_iota(jnp.int32, shape, 1)
        same = seg_col[low:high] == seg_row[:, :high]
        allowed = (key == query) | (same & (key <= query) & (query < valid))
        bias[low:high, :high] = jnp.where(allowed, 0.0, -1e30)


def attend_kernel(
    info, proj, cos_q, sin_q, cos_k, sin_k, seg_row, seg_col, qkv, attended, log_total, stats, bias,
    *, ns, slots, hd
):
    row, head = pl.program_id(0), pl.program_id(1)
    length = ns * slots

    def place(quarter):
        return pl.multiple_of(info[row, quarter] * slots, slots)

    @pl.when(head == 0)
    def _():
        for q in range(ns):
            source, low, high = place(q), q * slots, (q + 1) * slots
            for part, (cosine, sine) in enumerate(((cos_q, sin_q), (cos_k, sin_k))):
                cosine, sine = cosine[low:high], sine[low:high]
                for pair in range(hd // 128):
                    at = part * hd + pair * 128
                    values = proj[pl.ds(source, slots), at : at + 128]
                    turned = values * cosine + swap_halves(values) * sine
                    qkv[low:high, at : at + 128] = turned.astype(LOW)
            qkv[low:high, 2 * hd :] = proj[pl.ds(source, slots), 2 * hd :].astype(LOW)
        fill_bias(bias, info[row, ns], seg_row[...], seg_col[...], length)
        log_total[...] = jnp.zeros_like(log_total)

    mine = lax.broadcasted_iota(jnp.int32, (STRIPE, hd), 1) // HEAD == head
    column = lax.broadcasted_iota(jnp.int32, (STRIPE, 128), 1) == head
    for i in range(length // STRIPE):
        low, high = i * STRIPE, (i + 1) * STRIPE
        queries = jnp.where(mine, qkv[low:high, :hd] * 0.125, jnp.zeros((), LOW))
        scores = matmul(queries, qkv[:high, hd : 2 * hd], (1, 1)) + bias[low:high, :high]
        top = jnp.max(scores, axis=-1, keepdims=True)
        weight = jnp.exp(scores - top)
        total = jnp.sum(weight, axis=-1, keepdims=True)
        summed = matmul(weight.astype(LOW), qkv[:high, 2 * hd :], (1, 0)) / total
        log_total[low:high] = jnp.where(column, top + jnp.log(total), log_total[low:high])
        for u in range(STRIPE // slots):
            to = place(i * (STRIPE // slots) + u)
            rows = slice(u * slots, (u + 1) * slots)
            attended[pl.ds(to, slots), :] = jnp.where(
                mine[rows], summed[rows], attended[pl.ds(to, slots), :]
            )

    @pl.when(head == pl.num_programs(1) - 1)
    def _():
        for q in range(ns):
            here = slice(q * slots, (q + 1) * slots)
            stats[:, here] = stat_rows(attended[here])


def attend_back_kernel(
    info, qkv, attended, grad, stats, sums, gain, log_total, cos_q, sin_q, cos_k, sin_k, seg_row, seg_col, out,
    bias, grad_low, product, grad_q, grad_k, grad_v, *, ns, slots, hd
):
    row, head = pl.program_id(0), pl.program_id(1)
    length = ns * slots

    def place(quarter):
        return pl.multiple_of(info[row, quarter] * slots, slots)

    @pl.when(head == 0)
    def _():
        for q in range(ns):
            to, low, high = place(q), q * slots, (q + 1) * slots
            values = attended[low:high]
            scale = as_column(stats[1:2, low:high])
            unit = (values - as_column(stats[0:1, low:high])) * scale
            back = grad[low:high] * gain[...] - as_column(sums[0:1, low:high])
            back = scale * (back - unit * as_column(sums[1:2, low:high]))
            grad_low[pl.ds(to, slots), :] = back.astype(LOW)
            product[pl.ds(to, slots), :] = back * values
        fill_bias(bias, info[row, ns], seg_row[...], seg_col[...], length)
        for total in (grad_q, grad_k, grad_v):
            total[...] = jnp.zeros_like(total)

    mine = lax.broadcasted_iota(jnp.int32, (STRIPE, hd), 1) // HEAD == head
    column = lax.broadcasted_iota(jnp.int32, (STRIPE, 128), 1) == head
    nothing = jnp.zeros((), LOW)
    mine_all = lax.broadcasted_iota(jnp.int32, (length, hd), 1) // HEAD == head
    keys_mine = jnp.where(mine_all, qkv[:, hd : 2 * hd], nothing)
    for i in range(length // STRIPE):
        low, high = i * STRIPE, (i + 1) * STRIPE
        queries = jnp.where(mine, qkv[low:high, :hd] * 0.125, nothing)
        upstream = jnp.where(mine, grad_low[low:high], nothing)
        delta = jnp.sum(jnp.where(mine, product[low:high], 0.0), axis=-1, keepdims=True)
        log_sum = jnp.sum(jnp.where(column, log_total[low:high], 0.0), axis=-1, keepdims=True)
        scores = matmul(queries, qkv[:high, hd : 2 * hd], (1, 1)) + bias[low:high, :high]
        prob = jnp.exp(scores - log_sum)
        grad_prob = matmul(upstream, qkv[:high, 2 * hd :], (1, 1))
        grad_s = (prob * (grad_prob - delta)).astype(LOW)
        grad_q[low:high] += matmul(grad_s, keys_mine[:high], (1, 0))
        grad_k[:high] += matmul(grad_s, queries, (0, 0))
        grad_v[:high] += matmul(prob.astype(LOW), upstream, (0, 0))

    @pl.when(head == pl.num_programs(1) - 1)
    def _():
        for q in range(ns):
            target, low, high = place(q), q * slots, (q + 1) * slots
            tables = (cos_q, sin_q, grad_q, 0.125), (cos_k, sin_k, grad_k, 1.0)
            for part, (cosine, sine, total, scale) in enumerate(tables):
                cosine, sine = cosine[low:high] * scale, sine[low:high] * scale
                for pair in range(hd // 128):
                    values = total[low:high, pair * 128 : pair * 128 + 128]
                    turned = values * cosine - swap_halves(values) * sine
                    at = part * hd + pair * 128
                    out[pl.ds(target, slots), at : at + 128] = turned.astype(LOW)
            out[pl.ds(target, slots), 2 * hd :] = grad_v[low:high].astype(LOW)


def row_block(length, width):
    return pl.BlockSpec((length, width), lambda r, h, info: (r, 0))


def shared_block(length, width):
    return pl.BlockSpec((length, width), lambda r, h, info: (0, 0))


def attend(plan, info, proj, tables, segments):
    count, width = proj.shape
    length, hd = count // plan.rows, width // 3
    slots = length // plan.ns
    return pl.pallas_call(
        functools.partial(attend_kernel, ns=plan.ns, slots=slots, hd=hd),
        grid_spec=pltpu.PrefetchScalarGridSpec(
            num_scalar_prefetch=1,
            grid=(plan.rows, hd // HEAD),
            in_specs=[
                row_block(length, width),
                *[shared_block(length, 128)] * 4,
                pl.BlockSpec((None, 1, length), lambda r, h, info: (r, 0, 0)),
                pl.BlockSpec((None, length, 1), lambda r, h, info: (r, 0, 0)),
            ],
            out_specs=[
                row_block(length, width),
                row_block(length, hd),
                row_block(length, 128),
                pl.BlockSpec((2, length), lambda r, h, info: (0, r)),
            ],
            scratch_shapes=[pltpu.VMEM((length, length), WIDE)],
        ),
        out_shape=[
            jax.ShapeDtypeStruct((count, width), LOW),
            jax.ShapeDtypeStruct((count, hd), WIDE),
            jax.ShapeDtypeStruct((count, 128), WIDE),
            jax.ShapeDtypeStruct((2, count), WIDE),
        ],
        compiler_params=pltpu.CompilerParams(vmem_limit_bytes=48 << 20),
        name="attend",
    )(info, proj, *tables, segments[:, None, :], segments[:, :, None])


def attend_back(plan, info, qkv, attended, grad, stats, sums, gain, log_total, tables, segments):
    count, width = qkv.shape
    length, hd = count // plan.rows, width // 3
    slots = length // plan.ns
    return pl.pallas_call(
        functools.partial(attend_back_kernel, ns=plan.ns, slots=slots, hd=hd),
        grid_spec=pltpu.PrefetchScalarGridSpec(
            num_scalar_prefetch=1,
            grid=(plan.rows, hd // HEAD),
            in_specs=[
                row_block(length, width),
                row_block(length, hd),
                row_block(length, hd),
                pl.BlockSpec((2, length), lambda r, h, info: (0, r)),
                pl.BlockSpec((2, length), lambda r, h, info: (0, r)),
                shared_block(1, hd),
                row_block(length, 128),
                *[shared_block(length, 128)] * 4,
                pl.BlockSpec((None, 1, length), lambda r, h, info: (r, 0, 0)),
                pl.BlockSpec((None, length, 1), lambda r, h, info: (r, 0, 0)),
            ],
            out_specs=row_block(length, width),
            scratch_shapes=[
                pltpu.VMEM((length, length), WIDE),
                pltpu.VMEM((length, hd), LOW),
                pltpu.VMEM((length, hd), WIDE),
                pltpu.VMEM((length, hd), WIDE),
                pltpu.VMEM((length, hd), WIDE),
                pltpu.VMEM((length, hd), WIDE),
            ],
        ),
        out_shape=jax.ShapeDtypeStruct((count, width), LOW),
        compiler_params=pltpu.CompilerParams(vmem_limit_bytes=48 << 20),
        name="attend_back",
    )(
        info, qkv, attended, grad, stats, sums, gain, log_total, *tables,
        segments[:, None, :], segments[:, :, None],
    )


def shards(
    plan,
    tokens,
    segments,
    valid_count,
    cotangent,
    w_qkv,
    w_out,
    w_up,
    w_down,
    gain_attn,
    bias_attn,
    gain_mix,
    bias_mix,
    gain_ffn,
    bias_ffn,
    gain_hidden,
    bias_hidden,
):
    nb, ns = plan.nb, plan.ns
    width, slots, length = tokens.shape[2], tokens.shape[1], segments.shape[1]
    hd, hidden_part = width // nb, w_up.shape[1] // nb
    batch_index, seq_index = lax.axis_index("batch"), lax.axis_index("seq")
    entry = lax.dynamic_index_in_dim(
        jnp.asarray(plan.table), batch_index * ns + seq_index, 0, keepdims=False
    )

    tokens_low = reorder(plan, tokens[0], False, LOW)
    group = w_qkv.reshape(w_qkv.shape[0], 3, nb, hd).transpose(2, 0, 1, 3)
    group = group.reshape(nb, -1, 3 * hd)
    attn_own = jnp.concatenate([group, split_columns(plan, w_out.T)], axis=2)
    tokens_low, attn_own = sync(tokens_low, attn_own)
    attn_own = exchange(attn_own)
    qkv_w = gather_layers(attn_own[:, :, : 3 * hd])
    tokens_low = lax.ppermute(tokens_low, BOTH, plan.there)

    own_params = (gain_attn, bias_attn, gain_mix, bias_mix, gain_ffn, bias_ffn, gain_hidden, bias_hidden)
    tokens_low, cotangent, attn_own, *own_params = sync(tokens_low, cotangent, attn_own, *own_params)
    params = gather_over(jnp.concatenate([p.astype(WIDE) for p in own_params]), "seq", ns)
    packed = jnp.concatenate(
        [params.reshape(-1), segments[0].astype(WIDE), valid_count.astype(WIDE)]
    )
    packed = gather_over(packed, "batch", nb)
    spread = packed[:, : params.size].reshape(nb, ns, -1)
    vectors, at = [], 0
    for index, p in enumerate(own_params):
        piece = spread[:, :, at : at + p.shape[0]]
        at += p.shape[0]
        if index in (0, 1, 4, 5):
            vectors.append(piece.transpose(1, 0, 2).reshape(1, -1))
        else:
            vectors.append(lax.dynamic_index_in_dim(piece, batch_index, 0, False).reshape(1, -1))
    ga, ba, gm, bm, gf, bf, gh, bh = vectors
    count = plan.rows * length
    resid = tokens_low.astype(WIDE)
    mean_attn, scale_attn = norm_stats(resid)
    unit_attn = (resid - mean_attn) * scale_attn
    normed_low = (unit_attn * ga + ba).astype(LOW)
    normed_low, packed, cotangent, w_up, w_down, gm, bm, gf, bf, gh, bh = sync(
        normed_low, packed, cotangent, w_up, w_down, gm, bm, gf, bf, gh, bh
    )

    near = gather_near(plan, normed_low)
    ffn_own = jnp.concatenate([split_columns(plan, w) for w in (w_up, w_down.T)], axis=2)
    slot = seq_index * slots + jnp.arange(slots, dtype=jnp.int32)
    living = (slot < valid_count[0])[:, None]
    grad_low = reorder(plan, jnp.where(living, cotangent[0], jnp.zeros((), LOW)), False, LOW)
    layer_rows = jnp.concatenate(
        [
            lax.dynamic_slice_in_dim(packed[:, params.size :], entry[r], 1, 0)
            for r in range(plan.rows)
        ]
    ).astype(jnp.int32)
    seg_rows = layer_rows[:, :length]
    info = jnp.concatenate(
        [entry[plan.rows :].reshape(plan.rows, ns), layer_rows[:, length:]], axis=1
    )
    out_own = attn_own[:, :, 3 * hd :]
    ffn_own, grad_low, seg_rows, info, out_own, near = sync(
        ffn_own, grad_low, seg_rows, info, out_own, near
    )
    out_wt = gather_layers(out_own)
    tables = xpos_tables(length)
    grad_low, ffn_own, tables, arrays = sync(grad_low, ffn_own, tables, gather_far(plan, near))
    ffn_own = exchange(ffn_own)
    grad_low = lax.ppermute(grad_low, BOTH, plan.there)
    normed, projected = pieces_matmul(
        arrays,
        [qkv_w],
        (0, 3 * hd, 3 * hd),
        plain_end,
        [],
        [((count, 3 * hd), "rows")],
        "project",
    )
    qkv, attended, log_total, stats_mix = attend(plan, info, projected, tables, seg_rows)
    stats_mix, grad_low, ffn_own = sync(stats_mix, grad_low, ffn_own)
    up_w = gather_layers(ffn_own[:, :, :hidden_part])
    down_wt = gather_layers(ffn_own[:, :, hidden_part:])
    stats_mix = spread_stats(plan, stats_mix, hd)
    mixed, kept = block_parts(
        plan,
        [(attended, "rows"), (stats_mix, "lanes"), (gm, "whole"), (bm, "whole")],
        out_wt,
        (hd, 0),
        mixed_left,
        True,
        "out",
    )
    state, _ = reduce_first(plan, kept)
    resid_mid = resid + reduce_last(plan, state)[0]

    mean_ffn, scale_ffn = norm_stats(resid_mid)
    unit_ffn = (resid_mid - mean_ffn) * scale_ffn
    near = sync(*gather_near(plan, (unit_ffn * gf + bf).astype(LOW)))
    grad_later, *arrays = sync(grad_low, *gather_far(plan, near))
    grad_near = gather_near(plan, grad_later)
    ffn_in, active, slope, stats_hid = pieces_matmul(
        arrays,
        [up_w],
        (0, hidden_part, hidden_part),
        gelu_end,
        [],
        [((count, hidden_part), "rows"), ((count, hidden_part), "rows"), ((2, count), "lanes")],
        "up",
    )
    stats_hid, *grad_near = sync(stats_hid, *grad_near)
    grad_arrays = gather_far(plan, grad_near)
    stats_hid = spread_stats(plan, stats_hid, hidden_part)

    grad_all, grad_hn, sums_hid, vectors_hid, hidden_low = pieces_matmul(
        grad_arrays,
        [down_wt],
        (0, hidden_part, hidden_part),
        norm_back_end,
        [(active, "rows"), (stats_hid, "lanes"), (gh, "whole"), (bh, "whole")],
        [
            ((count, hidden_part), "rows"),
            ((2, count), "lanes"),
            ((2, hidden_part), "whole"),
            ((count, hidden_part), "rows", LOW),
        ],
        "down_back",
    )
    grad_down = matmul(grad_all, hidden_low, (0, 0)).astype(LOW)
    sums_hid = spread_sums(plan, sums_hid, hidden_part)
    sums_hid, grad_down = sync(sums_hid, grad_down)
    grad_down = scatter_layers(plan, grad_down)
    grad_hidden, kept = block_parts(
        plan,
        [
            (grad_hn, "rows"), (active, "rows"), (slope, "rows"),
            (stats_hid, "lanes"), (sums_hid, "lanes"), (gh, "whole"),
        ],
        up_w,
        (hidden_part, 0),
        hidden_left,
        True,
        "up_back",
    )
    grad_up = matmul(ffn_in, grad_hidden, (0, 0)).astype(LOW)
    state, (grad_up, hidden_low) = reduce_first(plan, kept, grad_up, hidden_low)
    grad_up = scatter_layers(plan, grad_up)
    grad_ffn_in, _ = reduce_last(plan, state)
    grad_mid, gain_ffn_part, bias_ffn_part = norm_back(grad_ffn_in, gf, unit_ffn, scale_ffn)
    grad_mid = grad_mid + grad_low.astype(WIDE)
    (kept,) = block_parts(
        plan,
        [(hidden_low, "rows")],
        down_wt,
        (hidden_part, 0),
        plain_left,
        False,
        "down",
    )
    kept, near = sync(kept, gather_near(plan, grad_mid.astype(LOW)))
    arrays = sync(*gather_far(plan, near))
    grad_down, arrays = sync(grad_down, arrays)
    grad_down = exchange(grad_down)
    mid_all, grad_mixed, sums_mix, vectors_mix = pieces_matmul(
        arrays,
        [out_wt],
        (0, hd, hd),
        norm_back_end,
        [(attended, "rows"), (stats_mix, "lanes"), (gm, "whole"), (bm, "whole")],
        [((count, hd), "rows"), ((2, count), "lanes"), ((2, hd), "whole")],
        "out_back",
    )
    sums_mix, grad_down = sync(sums_mix, grad_down)
    grad_out = matmul(mid_all, mixed, (0, 0)).astype(LOW)
    sums_mix = spread_sums(plan, sums_mix, hd)
    sums_mix, grad_out, grad_up, kept = sync(sums_mix, grad_out, grad_up, kept)
    grad_out = scatter_layers(plan, grad_out)
    grad_proj = attend_back(
        plan, info, qkv, attended, grad_mixed, stats_mix, sums_mix, gm, log_total, tables, seg_rows
    )
    vectors = jnp.concatenate([vectors_mix, vectors_hid], axis=1)
    for step in bits(ns)[:1]:
        vectors = vectors + swap_over(vectors, "seq", step, ns)
    state, (grad_proj, vectors) = reduce_first(plan, kept, grad_proj, vectors)
    grad_proj, state = sync(grad_proj, state)
    grad_qkv = matmul(normed, grad_proj, (0, 0)).astype(LOW)
    total, (grad_proj, grad_qkv, grad_up, grad_out) = reduce_last(
        plan, state, grad_proj, grad_qkv, exchange(grad_up), grad_out
    )
    grad_qkv = scatter_layers(plan, grad_qkv)
    output = (resid_mid + total).astype(LOW)
    (kept,) = block_parts(
        plan, [(grad_proj, "rows")], qkv_w, (3 * hd, 0), plain_left, False, "project_back"
    )
    for step in bits(ns)[1:]:
        vectors = vectors + swap_over(vectors, "seq", step, ns)
    state, (output, vectors) = reduce_first(plan, kept, output, vectors)
    output = lax.ppermute(output, BOTH, plan.back)
    grad_normed, _ = reduce_last(plan, state)
    grad_resid, gain_attn_part, bias_attn_part = norm_back(
        grad_normed, ga, unit_attn, scale_attn
    )
    whole = jnp.stack([gain_ffn_part, bias_ffn_part, gain_attn_part, bias_attn_part])
    whole = sum_over(whole, "seq", ns)
    whole = whole.reshape(4, ns, nb, -1).transpose(2, 0, 1, 3).reshape(nb, 1, 4 * hd)
    grad_tokens, grad_qkv, whole = sync((grad_mid + grad_resid).astype(LOW), grad_qkv, whole)
    grad_tokens = lax.ppermute(grad_tokens, BOTH, plan.back)
    attn_grads = jnp.concatenate([grad_qkv, grad_out], axis=2)
    rows = attn_grads.shape[1]
    whole = jnp.broadcast_to(whole.astype(LOW), (nb, 16, 4 * hd))
    attn_grads = exchange(jnp.concatenate([attn_grads, whole], axis=1))
    own = jnp.sum(attn_grads[:, rows].astype(WIDE), axis=0).reshape(4, ns, -1)
    own = lax.dynamic_index_in_dim(own, seq_index, 1, False)
    grad_qkv, grad_out = attn_grads[:, :rows, : 3 * hd], attn_grads[:, :rows, 3 * hd :]
    mixes = lax.dynamic_index_in_dim(vectors[:, :hd].reshape(2, ns, -1), seq_index, 1, False)
    hiddens = lax.dynamic_index_in_dim(vectors[:, hd:].reshape(2, ns, -1), seq_index, 1, False)
    grad_qkv = grad_qkv.reshape(nb, -1, 3, hd).transpose(1, 2, 0, 3).reshape(w_qkv.shape)
    grad_qkv, grad_out = grad_qkv.astype(WIDE), join_columns(plan, grad_out).astype(WIDE).T
    grad_up = join_columns(plan, grad_up).astype(WIDE)
    grad_down = join_columns(plan, grad_down).astype(WIDE).T
    output = reorder(plan, output, True, LOW)
    grad_tokens, own, mixes, hiddens, grad_qkv, grad_out, grad_up, grad_down, output = sync(
        grad_tokens, own, mixes, hiddens, grad_qkv, grad_out, grad_up, grad_down, output
    )
    return (
        output[None],
        reorder(plan, grad_tokens, True, WIDE)[None],
        grad_qkv,
        grad_out,
        grad_up,
        grad_down,
        own[2],
        own[3],
        mixes[0],
        mixes[1],
        own[0],
        own[1],
        hiddens[0],
        hiddens[1],
    )


def solution(mesh):
    plan = Plan(mesh.shape["batch"], mesh.shape["seq"])
    rows = P("batch", "seq", None)
    over_rows, over_columns, vector = P(BOTH, None), P(None, BOTH), P(BOTH)
    return jax.shard_map(
        functools.partial(shards, plan),
        mesh=mesh,
        in_specs=(rows, P("batch", None), P("batch"), rows)
        + (over_rows, over_columns, over_rows, over_columns)
        + (vector,) * 8,
        out_specs=(rows, rows, over_rows, over_columns, over_rows, over_columns) + (vector,) * 8,
        check_vma=False,
    )
```

```python
import functools

import jax
import jax.numpy as jnp
import numpy as np
from jax import lax
from jax.experimental import pallas as pl
from jax.experimental.pallas import tpu as pltpu
from jax.sharding import PartitionSpec as P

EPSILON = 1e-05
HEAD = 64
STRIPE = 256
ROWS_AT_ONCE = 256
LOW = jnp.bfloat16
WIDE = jnp.float32
BOTH = ("batch", "seq")

LAYER = (3, 0, 1, 2, 2, 1, 0, 3)
PLACE = (0, 1, 1, 1, 0, 0, 0, 1)
TURN = ((3, 0), (2, 1), (1, 2), (3, 0))


class Plan:
    def __init__(self, nb, ns):
        self.nb, self.ns = nb, ns
        self.rows = nb // ns
        self.fast = nb == 8 and ns == 4
        if self.fast:
            layer, place, turn = LAYER, PLACE, TURN
        else:
            layer = [b // self.rows for b in range(nb)]
            place = [b % self.rows for b in range(nb)]
            turn = [[0] * self.rows for _ in range(ns)]
        self.there = []
        for b in range(nb):
            for s in range(ns):
                k, p = layer[b], place[b]
                target = ((s ^ turn[k][p]) * self.rows + p) * ns + k
                self.there.append((b * ns + s, target))
        self.back = [(d, s) for s, d in self.there]
        row_of = {(layer[b], place[b]): b for b in range(nb)}
        table = []
        for b in range(nb):
            for k in range(ns):
                c, t = b % self.rows, b // self.rows
                order = [c, 1 - c] if self.fast else list(range(self.rows))
                entry = [row_of[k, p] for p in order]
                for p in order:
                    for q in range(ns):
                        entry.append(q ^ t ^ turn[k][p] if self.fast else q ^ turn[k][p])
                table.append(entry)
        self.table = np.array(table, np.int32)


def swap_over(value, axis, step, size):
    return lax.ppermute(value, axis, [(i, i ^ step) for i in range(size)])


def bits(size):
    return [1 << i for i in range(size.bit_length() - 1)]


def sum_over(value, axis, size):
    for step in bits(size):
        value = value + swap_over(value, axis, step, size)
    return value


def aligned(plan, value, step):
    if not plan.fast:
        return value
    shape = value.shape
    axis = {1: 1, 4: 2, 2: 3}[step]
    return jnp.flip(value.reshape(shape[0], 2, 2, 2, shape[1] // 8), axis).reshape(shape)


def gather_over(value, axis, size):
    index = lax.axis_index(axis)
    value = value[None]
    for step in bits(size):
        other = swap_over(value, axis, step, size)
        upper = (index & step) != 0
        value = jnp.concatenate(
            [jnp.where(upper, other, value), jnp.where(upper, value, other)], axis=0
        )
    return value


def sync(*values):
    return lax.optimization_barrier(values)


def gather_near(plan, block):
    if not plan.fast:
        slots, width = block.shape
        full = lax.all_gather(block, "batch", axis=0, tiled=False)
        full = full.reshape(plan.nb // plan.rows, plan.rows, slots, width)
        return [full.transpose(1, 0, 2, 3).reshape(plan.nb * slots, width)]
    return [block, swap_over(block, "batch", 2, 8), swap_over(block, "batch", 4, 8)]


def gather_far(plan, near):
    if not plan.fast:
        return near
    block, from_x, from_y = near
    half = block.shape[0] // 2
    far = swap_over(from_x[:half], "batch", 4, 8), swap_over(from_y[half:], "batch", 2, 8)
    other = [swap_over(piece, "batch", 1, 8) for piece in near]
    *other, far_a, far_b = sync(*other, *far)
    return [*near, far_a, far_b, *other, swap_over(far_a, "batch", 1, 8), swap_over(far_b, "batch", 1, 8)]


def reduce_first(plan, kept, *others):
    if not plan.fast:
        count, width = kept.shape
        slots = count // plan.nb
        part = kept.reshape(plan.rows, plan.nb // plan.rows, slots, width).transpose(1, 0, 2, 3)
        total = lax.psum_scatter(
            part.reshape(count, width), "batch", scatter_dimension=0, tiled=True
        )
        total, *others = sync(total, *others)
        return total.astype(WIDE), others
    over_x, far_y, over_y, near, at_x, at_y = kept
    slots, half = at_x.shape
    over_x, far_y = swap_over(over_x, "batch", 2, 8), swap_over(far_y, "batch", 4, 8)
    over_y = swap_over(over_y, "batch", 4, 8)
    over_x, far_y, over_y, *others = sync(over_x, far_y, over_y, *others)
    to_x = (at_x + far_y.astype(WIDE)).astype(LOW)
    to_y = (at_y + over_x[:slots].astype(WIDE)).astype(LOW)
    first = near[:, :half] + over_x[slots:].astype(WIDE)
    second = near[:, half:] + over_y.astype(WIDE)
    return (first, second, to_x, to_y), others


def reduce_last(plan, state, *others):
    if not plan.fast:
        return state, others
    first, second, to_x, to_y = state
    from_x, from_y = swap_over(to_x, "batch", 2, 8), swap_over(to_y, "batch", 4, 8)
    from_x, from_y, *others = sync(from_x, from_y, *others)
    total = jnp.concatenate([first + from_y.astype(WIDE), second + from_x.astype(WIDE)], axis=1)
    return total, others


def split_columns(plan, shard):
    rows, width = shard.shape
    return shard.reshape(rows, plan.nb, width // plan.nb).transpose(1, 0, 2)


def join_columns(plan, pieces):
    nb, rows, part = pieces.shape
    return pieces.transpose(1, 0, 2).reshape(rows, nb * part)


def exchange(pieces):
    return lax.all_to_all(pieces, "batch", 0, 0, tiled=True)


def gather_layers(pieces):
    nb, rows, part = pieces.shape
    return lax.all_gather(pieces.reshape(nb * rows, part), "seq", axis=0, tiled=True)


def scatter_layers(plan, part):
    own = lax.psum_scatter(part, "seq", scatter_dimension=0, tiled=True)
    rows, width = own.shape
    return own.reshape(plan.nb, rows // plan.nb, width)


def reorder_kernel(values, out, *, sources):
    low = lax.broadcasted_iota(jnp.int32, (values.shape[0], 128), 1) < 64
    for at, (first, second, half) in enumerate(sources):
        a = values[:, first * 128 : first * 128 + 128].astype(WIDE)
        b = values[:, second * 128 : second * 128 + 128].astype(WIDE)
        if half:
            a = pltpu.roll(a, 64, 1)
        else:
            b = pltpu.roll(b, 64, 1)
        out[:, at * 128 : at * 128 + 128] = jnp.where(low, a, b).astype(out.dtype)


def reorder(plan, values, outward, dtype):
    count, width = values.shape
    sizes = (plan.ns, plan.nb) if outward else (plan.nb, plan.ns)
    if width != plan.nb * plan.ns * 64 or sizes[0] % 2 or sizes[1] % 2:
        values = values.reshape(count, *sizes, width // (plan.nb * plan.ns))
        return values.transpose(0, 2, 1, 3).reshape(count, width).astype(dtype)
    sources = []
    for inner in range(sizes[1]):
        for outer in range(0, sizes[0], 2):
            at = outer * sizes[1] + inner
            sources.append((at // 2, (at + sizes[1]) // 2, at % 2))
    return pl.pallas_call(
        functools.partial(reorder_kernel, sources=sources),
        out_shape=jax.ShapeDtypeStruct(values.shape, dtype),
        compiler_params=pltpu.CompilerParams(vmem_limit_bytes=48 << 20),
        name="reorder",
    )(values)


def norm_stats(values):
    mean = jnp.mean(values, axis=-1, keepdims=True)
    center = values - mean
    return mean, lax.rsqrt(jnp.mean(center * center, axis=-1, keepdims=True) + EPSILON)


def spread_stats(plan, stats, count):
    mean, square = stats[0], stats[1]
    for step in bits(plan.nb):
        other = swap_over(jnp.stack([mean, square]), "batch", step, plan.nb)
        other = aligned(plan, other, step)
        gap = other[0] - mean
        mean = 0.5 * (mean + other[0])
        square = square + other[1] + gap * gap * (0.5 * count)
        count = 2 * count
    return jnp.stack([mean, lax.rsqrt(square / count + EPSILON)])


def spread_sums(plan, sums, count):
    for step in bits(plan.nb):
        sums = sums + aligned(plan, swap_over(sums, "batch", step, plan.nb), step)
    return sums / (count * plan.nb)


def norm_back(upstream, gain, unit, scale):
    scaled = upstream * gain
    first = jnp.mean(scaled, axis=-1, keepdims=True)
    second = jnp.mean(scaled * unit, axis=-1, keepdims=True)
    grad = scale * (scaled - first - unit * second)
    return grad, jnp.sum(upstream * unit, axis=0), jnp.sum(upstream, axis=0)


def xpos_tables(length):
    slot_pos = (jnp.arange(length, dtype=jnp.int32) - length // 2).astype(WIDE)
    lane = jnp.arange(128, dtype=jnp.int32)
    index = (lane % 32).astype(WIDE)
    angle = slot_pos[:, None] * jnp.exp(index * (-jnp.log(10000.0) / 32.0))[None, :]
    zeta = (index / 32.0 + 0.4) / 1.4
    growth = jnp.exp(slot_pos[:, None] * jnp.log(zeta)[None, :] / 512.0)
    cosine, sine = jnp.cos(angle), jnp.sin(angle)
    sine = jnp.where(lane % 64 < 32, -sine, sine)
    return cosine * growth, sine * growth, cosine / growth, sine / growth


def swap_halves(values):
    lane = lax.broadcasted_iota(jnp.int32, values.shape, 1)
    return jnp.where(lane % 64 < 32, pltpu.roll(values, 96, 1), pltpu.roll(values, 32, 1))


def matmul(a, b, contract):
    return lax.dot_general(a, b, ((contract[:1], contract[1:]), ((), ())), preferred_element_type=WIDE)


def as_column(row):
    return jnp.broadcast_to(row, (128, row.shape[1])).T[:, :1]


def as_row(column):
    return jnp.broadcast_to(column, (column.shape[0], 128)).T[:1]


def stat_rows(values):
    mean = jnp.mean(values, axis=-1, keepdims=True)
    center = values - mean
    square = jnp.sum(center * center, axis=-1, keepdims=True)
    return jnp.concatenate([as_row(mean), as_row(square)], axis=0)


def plain_end(acc, block, out):
    out[...] = acc


def gelu_end(acc, block, active_out, slope_out, stats_out):
    phi = 0.5 + 0.5 * lax.erf(acc * (0.5**0.5))
    active = acc * phi
    active_out[...] = active
    slope_out[...] = phi + acc * (jnp.exp(-0.5 * acc * acc) * ((2.0 * np.pi) ** -0.5))
    stats_out[...] = stat_rows(active)


def norm_back_end(acc, block, normal, stats, gain, bias, out, sums_out, vectors_out, low_out=None):
    out[...] = acc
    unit = (normal[...] - as_column(stats[0:1])) * as_column(stats[1:2])
    if low_out is not None:
        low_out[...] = (unit * gain[...] + bias[...]).astype(LOW)
    scaled = acc * gain[...]
    sums = [jnp.sum(scaled, axis=-1, keepdims=True), jnp.sum(scaled * unit, axis=-1, keepdims=True)]
    sums_out[...] = jnp.concatenate([as_row(sums[0]), as_row(sums[1])], axis=0)
    vectors = jnp.concatenate(
        [jnp.sum(acc * unit, axis=0, keepdims=True), jnp.sum(acc, axis=0, keepdims=True)], axis=0
    )

    @pl.when(block == 0)
    def _():
        vectors_out[...] = vectors

    @pl.when(block != 0)
    def _():
        vectors_out[...] += vectors


def pieces_kernel(*refs, moves, loads, step, n_arrays, n_weights, n_extra, keep, columns, end):
    arrays, weights = refs[:n_arrays], refs[n_arrays : n_arrays + n_weights]
    at = n_arrays + n_weights + n_extra
    extra = refs[n_arrays + n_weights : at]
    full, kept = refs[at], refs[at + 1] if keep else None
    outs = refs[at + 1 + keep : -6]
    rows, weight, arrived, left, loaded, stored = refs[-6:]
    block, count = pl.program_id(0), pl.num_programs(0)

    @pl.when(block == 0)
    def _():
        for index, column, row, n in loads:
            pltpu.make_async_copy(
                weights[index].at[:, pl.ds(column, weight.shape[1])],
                weight.at[pl.ds(row, n), :],
                loaded.at[0],
            ).start()
        for index, first, row, n in moves:
            pltpu.make_async_copy(
                arrays[index].at[pl.ds(first, n), :], rows.at[pl.ds(row, n), :], arrived.at[row // step]
            ).start()
        pltpu.make_async_copy(weight, weight, loaded.at[0]).wait()
        if keep:
            pltpu.make_async_copy(weight, kept, stored.at[0]).start()

    here = pl.ds(pl.multiple_of(block * step, step), step)
    pltpu.make_async_copy(rows.at[here], rows.at[here], arrived.at[block]).wait()
    pltpu.make_async_copy(rows.at[here], full.at[here], left.at[block]).start()
    acc = matmul(rows[here, :], weight[:, :columns], (1, 0))
    end(acc, block, *extra, *outs)

    @pl.when(block == count - 1)
    def _():
        for i in range(rows.shape[0] // step):
            part = pl.ds(i * step, step)
            pltpu.make_async_copy(rows.at[part], full.at[part], left.at[i]).wait()
        if keep:
            pltpu.make_async_copy(weight, kept, stored.at[0]).wait()


def moves_of(arrays, step):
    moves, total = [], 0
    for index, array in enumerate(arrays):
        for first in range(0, array.shape[0], step):
            n = min(step, array.shape[0] - first)
            moves.append((index, first, total, n))
            total += n
    return moves, total


def pieces_matmul(arrays, weights, columns, end, extra, outs, name):
    step = ROWS_AT_ONCE
    moves, total = moves_of(arrays, step)
    loads, inner = [], 0
    for index, weight in enumerate(weights):
        loads.append((index, columns[0], inner, weight.shape[0]))
        inner += weight.shape[0]
    keep = len(weights) > 1

    def spec(shape, kind):
        if kind == "rows":
            return pl.BlockSpec((step, shape[1]), lambda i: (i, 0))
        if kind == "lanes":
            return pl.BlockSpec((shape[0], step), lambda i: (0, i))
        return pl.BlockSpec(shape, lambda i: (0, 0))

    anywhere = pl.BlockSpec(memory_space=pl.ANY)
    kept = [jax.ShapeDtypeStruct((inner, columns[1]), LOW)] if keep else []
    return pl.pallas_call(
        functools.partial(
            pieces_kernel,
            moves=moves,
            loads=loads,
            step=step,
            n_arrays=len(arrays),
            n_weights=len(weights),
            n_extra=len(extra),
            keep=int(keep),
            columns=columns[2],
            end=end,
        ),
        grid=(total // step,),
        in_specs=[anywhere] * (len(arrays) + len(weights))
        + [spec(array.shape, kind) for array, kind in extra],
        out_specs=[anywhere] * (1 + keep) + [spec(*out[:2]) for out in outs],
        out_shape=[jax.ShapeDtypeStruct((total, inner), LOW)]
        + kept
        + [jax.ShapeDtypeStruct(out[0], out[2] if len(out) > 2 else WIDE) for out in outs],
        scratch_shapes=[
            pltpu.VMEM((total, inner), LOW),
            pltpu.VMEM((inner, columns[1]), LOW),
            pltpu.SemaphoreType.DMA((total // step,)),
            pltpu.SemaphoreType.DMA((total // step,)),
            pltpu.SemaphoreType.DMA((1,)),
            pltpu.SemaphoreType.DMA((1,)),
        ],
        compiler_params=pltpu.CompilerParams(vmem_limit_bytes=56 << 20),
        name=name,
    )(*arrays, *weights, *[array for array, _ in extra])


def mixed_left(values, stats, gain, bias):
    unit = (values[...] - as_column(stats[0:1])) * as_column(stats[1:2])
    return (unit * gain[...] + bias[...]).astype(LOW)


def hidden_left(grad, active, slope, stats, sums, gain):
    scale = as_column(stats[1:2])
    unit = (active[...] - as_column(stats[0:1])) * scale
    back = grad[...] * gain[...] - as_column(sums[0:1]) - unit * as_column(sums[1:2])
    return (scale * back * slope[...]).astype(LOW)


def plain_left(values):
    return values[...]


def part_kernel(*refs, n_in, make_left, keeps, ends):
    n_more = len(ends[1])
    left = make_left(*refs[:n_in])
    acc = matmul(left, refs[n_in][...], (1, 1))
    more, outs = refs[n_in + 1 : n_in + 1 + n_more], refs[n_in + 1 + n_more :]
    if keeps:
        outs[0 if ends[2] else 1][...] = left
        outs = outs[1:] if ends[2] else outs[2:]
    ends[0](acc, pl.program_id(0), *more, *outs)


def other_end(acc, block, *outs):
    if len(outs) == 1:
        outs[0][...] = acc.astype(LOW)
        return
    for i, out in enumerate(outs):

        @pl.when(block == i)
        def _(out=out):
            out[...] = acc.astype(LOW)


def own_x_end(acc, block, from_x, from_far, over_x, far_y, at_x):
    slots, half = at_x.shape

    @pl.when(block == 0)
    def _():
        total = acc + from_x[...].astype(WIDE)
        over_x[slots:] = total[:, :half].astype(LOW)
        at_x[...] = total[:, half:]

    @pl.when(block == 1)
    def _():
        total = acc + from_far[...].astype(WIDE)
        over_x[:slots] = total[:, :half].astype(LOW)
        far_y[...] = total[:, half:].astype(LOW)


def own_y_end(acc, block, from_near, from_y, over_y, near, at_y):
    half = at_y.shape[1]

    @pl.when(block == 0)
    def _():
        near[...] = acc + from_near[...].astype(WIDE)

    @pl.when(block == 1)
    def _():
        total = acc + from_y[...].astype(WIDE)
        over_y[...] = total[:, half:].astype(LOW)
        at_y[...] = total[:, :half]


def part_call(ins, weight, columns, make_left, kept, at, blocks, end, more, outs, name):
    step = ROWS_AT_ONCE
    total = next(array.shape[0] for array, kind in ins if kind == "rows")
    rows = weight.shape[0]

    def spec(array, kind):
        if kind == "rows":
            return pl.BlockSpec((step, array.shape[1]), lambda i: (at(i), 0))
        if kind == "lanes":
            return pl.BlockSpec((array.shape[0], step), lambda i: (0, at(i)))
        return pl.BlockSpec(array.shape, lambda i: (0, 0))

    once = pl.Buffered(1)
    in_specs = [spec(*item) for item in ins]
    in_specs.append(
        pl.BlockSpec((rows, columns[0]), lambda i: (0, columns[1]), pipeline_mode=once)
    )
    in_specs += [pl.BlockSpec(m.shape, lambda i: (0, 0), pipeline_mode=once) for m in more]
    operands = [array for array, _ in ins] + [weight, *more]
    out_specs, out_shape, aliases = [], [], {}
    if kept is not None:
        if kept:
            aliases[len(operands)] = 0
            in_specs.append(pl.BlockSpec(memory_space=pl.ANY))
            operands += kept
        out_specs.append(pl.BlockSpec((step, columns[0]), lambda i: (at(i), 0)))
        out_shape.append(jax.ShapeDtypeStruct((total, columns[0]), LOW))
    for shape, dtype, moves in outs:
        out_specs.append(pl.BlockSpec((step if moves else shape[0], shape[1]), lambda i, m=moves: (i if m else 0, 0)))
        out_shape.append(jax.ShapeDtypeStruct(shape, dtype))
    return pl.pallas_call(
        functools.partial(
            part_kernel,
            n_in=len(ins),
            make_left=make_left,
            keeps=kept is not None,
            ends=(end, more, not kept),
        ),
        grid=(blocks,),
        in_specs=in_specs,
        out_specs=out_specs,
        out_shape=out_shape,
        input_output_aliases=aliases,
        compiler_params=pltpu.CompilerParams(vmem_limit_bytes=56 << 20),
        name=name,
    )(*operands)


def block_parts(plan, ins, weight, columns, make_left, keeps, name):
    step, rows = ROWS_AT_ONCE, weight.shape[0]
    left = [] if keeps else None

    def call(at, blocks, end, more, outs, name):
        return part_call(ins, weight, columns, make_left, left, at, blocks, end, more, outs, name)

    if not plan.fast:
        total = next(array.shape[0] for array, kind in ins if kind == "rows")
        outs = [((total, rows), LOW, True)]
        return call(lambda i: i, total // step, other_end, [], outs, name)
    half = rows // 2
    outs = [((step, rows), LOW, False)] * 4
    outs = call(lambda i: 4 + i, 4, other_end, [], outs, name + "_other")
    if keeps:
        left = [outs[0]]
    near, at_x, at_y, far = outs[int(keeps) :]
    others = [swap_over(part, "batch", 1, 8) for part in (at_x, far, near, at_y)]
    outs = [((2 * step, half), LOW, False), ((step, half), LOW, False), ((step, half), WIDE, False)]
    outs = call(lambda i: 1 + 2 * i, 2, own_x_end, others[:2], outs, name + "_own_x")
    if keeps:
        left = [outs[0]]
    over_x, far_y, at_x = outs[int(keeps) :]
    outs = [((step, half), LOW, False), ((step, rows), WIDE, False), ((step, half), WIDE, False)]
    outs = call(lambda i: 2 * i, 2, own_y_end, others[2:], outs, name + "_own_y")
    if keeps:
        left = [outs[0]]
    over_y, near, at_y = outs[int(keeps) :]
    return *(left or []), (over_x, far_y, over_y, near, at_x, at_y)


def fill_bias(bias, valid, seg_row, seg_col, length):
    for i in range(length // STRIPE):
        low, high = i * STRIPE, (i + 1) * STRIPE
        shape = (STRIPE, high)
        query = lax.broadcasted_iota(jnp.int32, shape, 0) + low
        key = lax.broadcasted_iota(jnp.int32, shape, 1)
        same = seg_col[low:high] == seg_row[:, :high]
        allowed = (key == query) | (same & (key <= query) & (query < valid))
        bias[low:high, :high] = jnp.where(allowed, 0.0, -1e30)


def attend_kernel(
    info, proj, cos_q, sin_q, cos_k, sin_k, seg_row, seg_col, qkv, attended, log_total, stats, bias,
    *, ns, slots, hd
):
    row, head = pl.program_id(0), pl.program_id(1)
    length = ns * slots

    def place(quarter):
        return pl.multiple_of(info[row, quarter] * slots, slots)

    @pl.when(head == 0)
    def _():
        for q in range(ns):
            source, low, high = place(q), q * slots, (q + 1) * slots
            for part, (cosine, sine) in enumerate(((cos_q, sin_q), (cos_k, sin_k))):
                cosine, sine = cosine[low:high], sine[low:high]
                for pair in range(hd // 128):
                    at = part * hd + pair * 128
                    values = proj[pl.ds(source, slots), at : at + 128]
                    turned = values * cosine + swap_halves(values) * sine
                    qkv[low:high, at : at + 128] = turned.astype(LOW)
            qkv[low:high, 2 * hd :] = proj[pl.ds(source, slots), 2 * hd :].astype(LOW)
        fill_bias(bias, info[row, ns], seg_row[...], seg_col[...], length)
        log_total[...] = jnp.zeros_like(log_total)

    mine = lax.broadcasted_iota(jnp.int32, (STRIPE, hd), 1) // HEAD == head
    column = lax.broadcasted_iota(jnp.int32, (STRIPE, 128), 1) == head
    for i in range(length // STRIPE):
        low, high = i * STRIPE, (i + 1) * STRIPE
        queries = jnp.where(mine, qkv[low:high, :hd] * 0.125, jnp.zeros((), LOW))
        scores = matmul(queries, qkv[:high, hd : 2 * hd], (1, 1)) + bias[low:high, :high]
        top = jnp.max(scores, axis=-1, keepdims=True)
        weight = jnp.exp(scores - top)
        total = jnp.sum(weight, axis=-1, keepdims=True)
        summed = matmul(weight.astype(LOW), qkv[:high, 2 * hd :], (1, 0)) / total
        log_total[low:high] = jnp.where(column, top + jnp.log(total), log_total[low:high])
        for u in range(STRIPE // slots):
            to = place(i * (STRIPE // slots) + u)
            rows = slice(u * slots, (u + 1) * slots)
            attended[pl.ds(to, slots), :] = jnp.where(
                mine[rows], summed[rows], attended[pl.ds(to, slots), :]
            )

    @pl.when(head == pl.num_programs(1) - 1)
    def _():
        for q in range(ns):
            here = slice(q * slots, (q + 1) * slots)
            stats[:, here] = stat_rows(attended[here])


def attend_back_kernel(
    info, qkv, attended, grad, stats, sums, gain, log_total, cos_q, sin_q, cos_k, sin_k, seg_row, seg_col, out,
    bias, grad_low, product, grad_q, grad_k, grad_v, *, ns, slots, hd
):
    row, head = pl.program_id(0), pl.program_id(1)
    length = ns * slots

    def place(quarter):
        return pl.multiple_of(info[row, quarter] * slots, slots)

    @pl.when(head == 0)
    def _():
        for q in range(ns):
            to, low, high = place(q), q * slots, (q + 1) * slots
            values = attended[low:high]
            scale = as_column(stats[1:2, low:high])
            unit = (values - as_column(stats[0:1, low:high])) * scale
            back = grad[low:high] * gain[...] - as_column(sums[0:1, low:high])
            back = scale * (back - unit * as_column(sums[1:2, low:high]))
            grad_low[pl.ds(to, slots), :] = back.astype(LOW)
            product[pl.ds(to, slots), :] = back * values
        fill_bias(bias, info[row, ns], seg_row[...], seg_col[...], length)
        for total in (grad_q, grad_k, grad_v):
            total[...] = jnp.zeros_like(total)

    mine = lax.broadcasted_iota(jnp.int32, (STRIPE, hd), 1) // HEAD == head
    column = lax.broadcasted_iota(jnp.int32, (STRIPE, 128), 1) == head
    nothing = jnp.zeros((), LOW)
    mine_all = lax.broadcasted_iota(jnp.int32, (length, hd), 1) // HEAD == head
    keys_mine = jnp.where(mine_all, qkv[:, hd : 2 * hd], nothing)
    for i in range(length // STRIPE):
        low, high = i * STRIPE, (i + 1) * STRIPE
        queries = jnp.where(mine, qkv[low:high, :hd] * 0.125, nothing)
        upstream = jnp.where(mine, grad_low[low:high], nothing)
        delta = jnp.sum(jnp.where(mine, product[low:high], 0.0), axis=-1, keepdims=True)
        log_sum = jnp.sum(jnp.where(column, log_total[low:high], 0.0), axis=-1, keepdims=True)
        scores = matmul(queries, qkv[:high, hd : 2 * hd], (1, 1)) + bias[low:high, :high]
        prob = jnp.exp(scores - log_sum)
        grad_prob = matmul(upstream, qkv[:high, 2 * hd :], (1, 1))
        grad_s = (prob * (grad_prob - delta)).astype(LOW)
        grad_q[low:high] += matmul(grad_s, keys_mine[:high], (1, 0))
        grad_k[:high] += matmul(grad_s, queries, (0, 0))
        grad_v[:high] += matmul(prob.astype(LOW), upstream, (0, 0))

    @pl.when(head == pl.num_programs(1) - 1)
    def _():
        for q in range(ns):
            target, low, high = place(q), q * slots, (q + 1) * slots
            tables = (cos_q, sin_q, grad_q, 0.125), (cos_k, sin_k, grad_k, 1.0)
            for part, (cosine, sine, total, scale) in enumerate(tables):
                cosine, sine = cosine[low:high] * scale, sine[low:high] * scale
                for pair in range(hd // 128):
                    values = total[low:high, pair * 128 : pair * 128 + 128]
                    turned = values * cosine - swap_halves(values) * sine
                    at = part * hd + pair * 128
                    out[pl.ds(target, slots), at : at + 128] = turned.astype(LOW)
            out[pl.ds(target, slots), 2 * hd :] = grad_v[low:high].astype(LOW)


def row_block(length, width):
    return pl.BlockSpec((length, width), lambda r, h, info: (r, 0))


def shared_block(length, width):
    return pl.BlockSpec((length, width), lambda r, h, info: (0, 0))


def attend(plan, info, proj, tables, segments):
    count, width = proj.shape
    length, hd = count // plan.rows, width // 3
    slots = length // plan.ns
    return pl.pallas_call(
        functools.partial(attend_kernel, ns=plan.ns, slots=slots, hd=hd),
        grid_spec=pltpu.PrefetchScalarGridSpec(
            num_scalar_prefetch=1,
            grid=(plan.rows, hd // HEAD),
            in_specs=[
                row_block(length, width),
                *[shared_block(length, 128)] * 4,
                pl.BlockSpec((None, 1, length), lambda r, h, info: (r, 0, 0)),
                pl.BlockSpec((None, length, 1), lambda r, h, info: (r, 0, 0)),
            ],
            out_specs=[
                row_block(length, width),
                row_block(length, hd),
                row_block(length, 128),
                pl.BlockSpec((2, length), lambda r, h, info: (0, r)),
            ],
            scratch_shapes=[pltpu.VMEM((length, length), WIDE)],
        ),
        out_shape=[
            jax.ShapeDtypeStruct((count, width), LOW),
            jax.ShapeDtypeStruct((count, hd), WIDE),
            jax.ShapeDtypeStruct((count, 128), WIDE),
            jax.ShapeDtypeStruct((2, count), WIDE),
        ],
        compiler_params=pltpu.CompilerParams(vmem_limit_bytes=48 << 20),
        name="attend",
    )(info, proj, *tables, segments[:, None, :], segments[:, :, None])


def attend_back(plan, info, qkv, attended, grad, stats, sums, gain, log_total, tables, segments):
    count, width = qkv.shape
    length, hd = count // plan.rows, width // 3
    slots = length // plan.ns
    return pl.pallas_call(
        functools.partial(attend_back_kernel, ns=plan.ns, slots=slots, hd=hd),
        grid_spec=pltpu.PrefetchScalarGridSpec(
            num_scalar_prefetch=1,
            grid=(plan.rows, hd // HEAD),
            in_specs=[
                row_block(length, width),
                row_block(length, hd),
                row_block(length, hd),
                pl.BlockSpec((2, length), lambda r, h, info: (0, r)),
                pl.BlockSpec((2, length), lambda r, h, info: (0, r)),
                shared_block(1, hd),
                row_block(length, 128),
                *[shared_block(length, 128)] * 4,
                pl.BlockSpec((None, 1, length), lambda r, h, info: (r, 0, 0)),
                pl.BlockSpec((None, length, 1), lambda r, h, info: (r, 0, 0)),
            ],
            out_specs=row_block(length, width),
            scratch_shapes=[
                pltpu.VMEM((length, length), WIDE),
                pltpu.VMEM((length, hd), LOW),
                pltpu.VMEM((length, hd), WIDE),
                pltpu.VMEM((length, hd), WIDE),
                pltpu.VMEM((length, hd), WIDE),
                pltpu.VMEM((length, hd), WIDE),
            ],
        ),
        out_shape=jax.ShapeDtypeStruct((count, width), LOW),
        compiler_params=pltpu.CompilerParams(vmem_limit_bytes=48 << 20),
        name="attend_back",
    )(
        info, qkv, attended, grad, stats, sums, gain, log_total, *tables,
        segments[:, None, :], segments[:, :, None],
    )


def shards(
    plan,
    tokens,
    segments,
    valid_count,
    cotangent,
    w_qkv,
    w_out,
    w_up,
    w_down,
    gain_attn,
    bias_attn,
    gain_mix,
    bias_mix,
    gain_ffn,
    bias_ffn,
    gain_hidden,
    bias_hidden,
):
    nb, ns = plan.nb, plan.ns
    width, slots, length = tokens.shape[2], tokens.shape[1], segments.shape[1]
    hd, hidden_part = width // nb, w_up.shape[1] // nb
    batch_index, seq_index = lax.axis_index("batch"), lax.axis_index("seq")
    entry = lax.dynamic_index_in_dim(
        jnp.asarray(plan.table), batch_index * ns + seq_index, 0, keepdims=False
    )

    tokens_low = reorder(plan, tokens[0], False, LOW)
    group = w_qkv.reshape(w_qkv.shape[0], 3, nb, hd).transpose(2, 0, 1, 3)
    group = group.reshape(nb, -1, 3 * hd)
    attn_own = jnp.concatenate([group, split_columns(plan, w_out.T)], axis=2)
    tokens_low, attn_own = sync(tokens_low, attn_own)
    attn_own = exchange(attn_own)
    qkv_w = gather_layers(attn_own[:, :, : 3 * hd])
    tokens_low = lax.ppermute(tokens_low, BOTH, plan.there)

    own_params = (gain_attn, bias_attn, gain_mix, bias_mix, gain_ffn, bias_ffn, gain_hidden, bias_hidden)
    tokens_low, cotangent, attn_own, *own_params = sync(tokens_low, cotangent, attn_own, *own_params)
    params = gather_over(jnp.concatenate([p.astype(WIDE) for p in own_params]), "seq", ns)
    packed = jnp.concatenate(
        [params.reshape(-1), segments[0].astype(WIDE), valid_count.astype(WIDE)]
    )
    packed = gather_over(packed, "batch", nb)
    spread = packed[:, : params.size].reshape(nb, ns, -1)
    vectors, at = [], 0
    for index, p in enumerate(own_params):
        piece = spread[:, :, at : at + p.shape[0]]
        at += p.shape[0]
        if index in (0, 1, 4, 5):
            vectors.append(piece.transpose(1, 0, 2).reshape(1, -1))
        else:
            vectors.append(lax.dynamic_index_in_dim(piece, batch_index, 0, False).reshape(1, -1))
    ga, ba, gm, bm, gf, bf, gh, bh = vectors
    count = plan.rows * length
    resid = tokens_low.astype(WIDE)
    mean_attn, scale_attn = norm_stats(resid)
    unit_attn = (resid - mean_attn) * scale_attn
    normed_low = (unit_attn * ga + ba).astype(LOW)
    normed_low, packed, cotangent, w_up, w_down, gm, bm, gf, bf, gh, bh = sync(
        normed_low, packed, cotangent, w_up, w_down, gm, bm, gf, bf, gh, bh
    )

    near = gather_near(plan, normed_low)
    ffn_own = jnp.concatenate([split_columns(plan, w) for w in (w_up, w_down.T)], axis=2)
    slot = seq_index * slots + jnp.arange(slots, dtype=jnp.int32)
    living = (slot < valid_count[0])[:, None]
    grad_low = reorder(plan, jnp.where(living, cotangent[0], jnp.zeros((), LOW)), False, LOW)
    layer_rows = jnp.concatenate(
        [
            lax.dynamic_slice_in_dim(packed[:, params.size :], entry[r], 1, 0)
            for r in range(plan.rows)
        ]
    ).astype(jnp.int32)
    seg_rows = layer_rows[:, :length]
    info = jnp.concatenate(
        [entry[plan.rows :].reshape(plan.rows, ns), layer_rows[:, length:]], axis=1
    )
    out_own = attn_own[:, :, 3 * hd :]
    ffn_own, grad_low, seg_rows, info, out_own, near = sync(
        ffn_own, grad_low, seg_rows, info, out_own, near
    )
    out_wt = gather_layers(out_own)
    tables = xpos_tables(length)
    grad_low, ffn_own, tables, arrays = sync(grad_low, ffn_own, tables, gather_far(plan, near))
    ffn_own = exchange(ffn_own)
    grad_low = lax.ppermute(grad_low, BOTH, plan.there)
    normed, projected = pieces_matmul(
        arrays,
        [qkv_w],
        (0, 3 * hd, 3 * hd),
        plain_end,
        [],
        [((count, 3 * hd), "rows")],
        "project",
    )
    qkv, attended, log_total, stats_mix = attend(plan, info, projected, tables, seg_rows)
    stats_mix, grad_low, ffn_own = sync(stats_mix, grad_low, ffn_own)
    up_w = gather_layers(ffn_own[:, :, :hidden_part])
    down_wt = gather_layers(ffn_own[:, :, hidden_part:])
    stats_mix = spread_stats(plan, stats_mix, hd)
    mixed, kept = block_parts(
        plan,
        [(attended, "rows"), (stats_mix, "lanes"), (gm, "whole"), (bm, "whole")],
        out_wt,
        (hd, 0),
        mixed_left,
        True,
        "out",
    )
    state, _ = reduce_first(plan, kept)
    resid_mid = resid + reduce_last(plan, state)[0]

    mean_ffn, scale_ffn = norm_stats(resid_mid)
    unit_ffn = (resid_mid - mean_ffn) * scale_ffn
    near = sync(*gather_near(plan, (unit_ffn * gf + bf).astype(LOW)))
    grad_later, *arrays = sync(grad_low, *gather_far(plan, near))
    grad_near = gather_near(plan, grad_later)
    ffn_in, active, slope, stats_hid = pieces_matmul(
        arrays,
        [up_w],
        (0, hidden_part, hidden_part),
        gelu_end,
        [],
        [((count, hidden_part), "rows"), ((count, hidden_part), "rows"), ((2, count), "lanes")],
        "up",
    )
    stats_hid, *grad_near = sync(stats_hid, *grad_near)
    grad_arrays = gather_far(plan, grad_near)
    stats_hid = spread_stats(plan, stats_hid, hidden_part)

    grad_all, grad_hn, sums_hid, vectors_hid, hidden_low = pieces_matmul(
        grad_arrays,
        [down_wt],
        (0, hidden_part, hidden_part),
        norm_back_end,
        [(active, "rows"), (stats_hid, "lanes"), (gh, "whole"), (bh, "whole")],
        [
            ((count, hidden_part), "rows"),
            ((2, count), "lanes"),
            ((2, hidden_part), "whole"),
            ((count, hidden_part), "rows", LOW),
        ],
        "down_back",
    )
    grad_down = matmul(grad_all, hidden_low, (0, 0)).astype(LOW)
    sums_hid = spread_sums(plan, sums_hid, hidden_part)
    sums_hid, grad_down = sync(sums_hid, grad_down)
    grad_down = scatter_layers(plan, grad_down)
    grad_hidden, kept = block_parts(
        plan,
        [
            (grad_hn, "rows"), (active, "rows"), (slope, "rows"),
            (stats_hid, "lanes"), (sums_hid, "lanes"), (gh, "whole"),
        ],
        up_w,
        (hidden_part, 0),
        hidden_left,
        True,
        "up_back",
    )
    grad_up = matmul(ffn_in, grad_hidden, (0, 0)).astype(LOW)
    state, (grad_up, hidden_low) = reduce_first(plan, kept, grad_up, hidden_low)
    grad_up = scatter_layers(plan, grad_up)
    grad_ffn_in, _ = reduce_last(plan, state)
    grad_mid, gain_ffn_part, bias_ffn_part = norm_back(grad_ffn_in, gf, unit_ffn, scale_ffn)
    grad_mid = grad_mid + grad_low.astype(WIDE)
    (kept,) = block_parts(
        plan,
        [(hidden_low, "rows")],
        down_wt,
        (hidden_part, 0),
        plain_left,
        False,
        "down",
    )
    kept, near = sync(kept, gather_near(plan, grad_mid.astype(LOW)))
    arrays = sync(*gather_far(plan, near))
    grad_down, arrays = sync(grad_down, arrays)
    grad_down = exchange(grad_down)
    mid_all, grad_mixed, sums_mix, vectors_mix = pieces_matmul(
        arrays,
        [out_wt],
        (0, hd, hd),
        norm_back_end,
        [(attended, "rows"), (stats_mix, "lanes"), (gm, "whole"), (bm, "whole")],
        [((count, hd), "rows"), ((2, count), "lanes"), ((2, hd), "whole")],
        "out_back",
    )
    sums_mix, grad_down = sync(sums_mix, grad_down)
    grad_out = matmul(mid_all, mixed, (0, 0)).astype(LOW)
    sums_mix = spread_sums(plan, sums_mix, hd)
    sums_mix, grad_out, grad_up, kept = sync(sums_mix, grad_out, grad_up, kept)
    grad_out = scatter_layers(plan, grad_out)
    grad_proj = attend_back(
        plan, info, qkv, attended, grad_mixed, stats_mix, sums_mix, gm, log_total, tables, seg_rows
    )
    vectors = jnp.concatenate([vectors_mix, vectors_hid], axis=1)
    for step in bits(ns)[:1]:
        vectors = vectors + swap_over(vectors, "seq", step, ns)
    state, (grad_proj, vectors) = reduce_first(plan, kept, grad_proj, vectors)
    grad_qkv = matmul(normed, grad_proj, (0, 0)).astype(LOW)
    grad_proj, grad_qkv, grad_up, grad_out = sync(grad_proj, grad_qkv, exchange(grad_up), grad_out)
    grad_qkv = scatter_layers(plan, grad_qkv)
    output = (resid_mid + reduce_last(plan, state)[0]).astype(LOW)
    (kept,) = block_parts(
        plan, [(grad_proj, "rows")], qkv_w, (3 * hd, 0), plain_left, False, "project_back"
    )
    state, (output, vectors) = reduce_first(plan, kept, output, vectors)
    output = lax.ppermute(output, BOTH, plan.back)
    for step in bits(ns)[1:]:
        vectors = vectors + swap_over(vectors, "seq", step, ns)
    grad_normed, (vectors,) = reduce_last(plan, state, vectors)
    grad_resid, gain_attn_part, bias_attn_part = norm_back(
        grad_normed, ga, unit_attn, scale_attn
    )
    whole = jnp.stack([gain_ffn_part, bias_ffn_part, gain_attn_part, bias_attn_part])
    whole = sum_over(whole, "seq", ns)
    whole = whole.reshape(4, ns, nb, -1).transpose(2, 0, 1, 3).reshape(nb, 1, 4 * hd)
    grad_tokens, grad_qkv, whole = sync((grad_mid + grad_resid).astype(LOW), grad_qkv, whole)
    grad_tokens = lax.ppermute(grad_tokens, BOTH, plan.back)
    attn_grads = jnp.concatenate([grad_qkv, grad_out], axis=2)
    rows = attn_grads.shape[1]
    whole = jnp.broadcast_to(whole.astype(LOW), (nb, 16, 4 * hd))
    attn_grads = exchange(jnp.concatenate([attn_grads, whole], axis=1))
    own = jnp.sum(attn_grads[:, rows].astype(WIDE), axis=0).reshape(4, ns, -1)
    own = lax.dynamic_index_in_dim(own, seq_index, 1, False)
    grad_qkv, grad_out = attn_grads[:, :rows, : 3 * hd], attn_grads[:, :rows, 3 * hd :]
    mixes = lax.dynamic_index_in_dim(vectors[:, :hd].reshape(2, ns, -1), seq_index, 1, False)
    hiddens = lax.dynamic_index_in_dim(vectors[:, hd:].reshape(2, ns, -1), seq_index, 1, False)
    grad_qkv = grad_qkv.reshape(nb, -1, 3, hd).transpose(1, 2, 0, 3).reshape(w_qkv.shape)
    grad_qkv, grad_out = grad_qkv.astype(WIDE), join_columns(plan, grad_out).astype(WIDE).T
    grad_up = join_columns(plan, grad_up).astype(WIDE)
    grad_down = join_columns(plan, grad_down).astype(WIDE).T
    output = reorder(plan, output, True, LOW)
    grad_tokens, own, mixes, hiddens, grad_qkv, grad_out, grad_up, grad_down, output = sync(
        grad_tokens, own, mixes, hiddens, grad_qkv, grad_out, grad_up, grad_down, output
    )
    return (
        output[None],
        reorder(plan, grad_tokens, True, WIDE)[None],
        grad_qkv,
        grad_out,
        grad_up,
        grad_down,
        own[2],
        own[3],
        mixes[0],
        mixes[1],
        own[0],
        own[1],
        hiddens[0],
        hiddens[1],
    )


def solution(mesh):
    plan = Plan(mesh.shape["batch"], mesh.shape["seq"])
    rows = P("batch", "seq", None)
    over_rows, over_columns, vector = P(BOTH, None), P(None, BOTH), P(BOTH)
    return jax.shard_map(
        functools.partial(shards, plan),
        mesh=mesh,
        in_specs=(rows, P("batch", None), P("batch"), rows)
        + (over_rows, over_columns, over_rows, over_columns)
        + (vector,) * 8,
        out_specs=(rows, rows, over_rows, over_columns, over_rows, over_columns) + (vector,) * 8,
        check_vma=False,
    )
```

```python
import functools

import jax
import jax.numpy as jnp
import numpy as np
from jax import lax
from jax.experimental import pallas as pl
from jax.experimental.pallas import tpu as pltpu
from jax.sharding import PartitionSpec as P

EPSILON = 1e-05
HEAD = 64
STRIPE = 256
ROWS_AT_ONCE = 256
LOW = jnp.bfloat16
WIDE = jnp.float32
BOTH = ("batch", "seq")

LAYER = (3, 0, 1, 2, 2, 1, 0, 3)
PLACE = (0, 1, 1, 1, 0, 0, 0, 1)
TURN = ((3, 0), (2, 1), (1, 2), (3, 0))


class Plan:
    def __init__(self, nb, ns):
        self.nb, self.ns = nb, ns
        self.rows = nb // ns
        self.fast = nb == 8 and ns == 4
        if self.fast:
            layer, place, turn = LAYER, PLACE, TURN
        else:
            layer = [b // self.rows for b in range(nb)]
            place = [b % self.rows for b in range(nb)]
            turn = [[0] * self.rows for _ in range(ns)]
        self.there = []
        for b in range(nb):
            for s in range(ns):
                k, p = layer[b], place[b]
                target = ((s ^ turn[k][p]) * self.rows + p) * ns + k
                self.there.append((b * ns + s, target))
        self.back = [(d, s) for s, d in self.there]
        row_of = {(layer[b], place[b]): b for b in range(nb)}
        table = []
        for b in range(nb):
            for k in range(ns):
                c, t = b % self.rows, b // self.rows
                order = [c, 1 - c] if self.fast else list(range(self.rows))
                entry = [row_of[k, p] for p in order]
                for p in order:
                    for q in range(ns):
                        entry.append(q ^ t ^ turn[k][p] if self.fast else q ^ turn[k][p])
                table.append(entry)
        self.table = np.array(table, np.int32)


def swap_over(value, axis, step, size):
    return lax.ppermute(value, axis, [(i, i ^ step) for i in range(size)])


def bits(size):
    return [1 << i for i in range(size.bit_length() - 1)]


def sum_over(value, axis, size):
    for step in bits(size):
        value = value + swap_over(value, axis, step, size)
    return value


def aligned(plan, value, step):
    if not plan.fast:
        return value
    shape = value.shape
    axis = {1: 1, 4: 2, 2: 3}[step]
    return jnp.flip(value.reshape(shape[0], 2, 2, 2, shape[1] // 8), axis).reshape(shape)


def gather_over(value, axis, size):
    index = lax.axis_index(axis)
    value = value[None]
    for step in bits(size):
        other = swap_over(value, axis, step, size)
        upper = (index & step) != 0
        value = jnp.concatenate(
            [jnp.where(upper, other, value), jnp.where(upper, value, other)], axis=0
        )
    return value


def sync(*values):
    return lax.optimization_barrier(values)


def gather_near(plan, block):
    if not plan.fast:
        slots, width = block.shape
        full = lax.all_gather(block, "batch", axis=0, tiled=False)
        full = full.reshape(plan.nb // plan.rows, plan.rows, slots, width)
        return [full.transpose(1, 0, 2, 3).reshape(plan.nb * slots, width)]
    return [block, swap_over(block, "batch", 2, 8), swap_over(block, "batch", 4, 8)]


def gather_far(plan, near):
    if not plan.fast:
        return near
    block, from_x, from_y = near
    half = block.shape[0] // 2
    far = swap_over(from_x[:half], "batch", 4, 8), swap_over(from_y[half:], "batch", 2, 8)
    other = [swap_over(piece, "batch", 1, 8) for piece in near]
    *other, far_a, far_b = sync(*other, *far)
    return [*near, far_a, far_b, *other, swap_over(far_a, "batch", 1, 8), swap_over(far_b, "batch", 1, 8)]


def reduce_first(plan, kept, *others):
    if not plan.fast:
        count, width = kept.shape
        slots = count // plan.nb
        part = kept.reshape(plan.rows, plan.nb // plan.rows, slots, width).transpose(1, 0, 2, 3)
        total = lax.psum_scatter(
            part.reshape(count, width), "batch", scatter_dimension=0, tiled=True
        )
        total, *others = sync(total, *others)
        return total.astype(WIDE), others
    over_x, far_y, over_y, near, at_x, at_y = kept
    slots, half = at_x.shape
    over_x, far_y = swap_over(over_x, "batch", 2, 8), swap_over(far_y, "batch", 4, 8)
    over_y = swap_over(over_y, "batch", 4, 8)
    over_x, far_y, over_y, *others = sync(over_x, far_y, over_y, *others)
    to_x = (at_x + far_y.astype(WIDE)).astype(LOW)
    to_y = (at_y + over_x[:slots].astype(WIDE)).astype(LOW)
    first = near[:, :half] + over_x[slots:].astype(WIDE)
    second = near[:, half:] + over_y.astype(WIDE)
    return (first, second, to_x, to_y), others


def reduce_last(plan, state):
    if not plan.fast:
        return state
    first, second, to_x, to_y = state
    from_x, from_y = swap_over(to_x, "batch", 2, 8), swap_over(to_y, "batch", 4, 8)
    from_x, from_y = sync(from_x, from_y)
    return jnp.concatenate([first + from_y.astype(WIDE), second + from_x.astype(WIDE)], axis=1)


def split_columns(plan, shard):
    rows, width = shard.shape
    return shard.reshape(rows, plan.nb, width // plan.nb).transpose(1, 0, 2)


def join_columns(plan, pieces):
    nb, rows, part = pieces.shape
    return pieces.transpose(1, 0, 2).reshape(rows, nb * part)


def exchange(pieces):
    return lax.all_to_all(pieces, "batch", 0, 0, tiled=True)


def gather_layers(pieces):
    nb, rows, part = pieces.shape
    return lax.all_gather(pieces.reshape(nb * rows, part), "seq", axis=0, tiled=True)


def scatter_layers(plan, part):
    own = lax.psum_scatter(part, "seq", scatter_dimension=0, tiled=True)
    rows, width = own.shape
    return own.reshape(plan.nb, rows // plan.nb, width)


def reorder_kernel(values, out, *, sources):
    low = lax.broadcasted_iota(jnp.int32, (values.shape[0], 128), 1) < 64
    for at, (first, second, half) in enumerate(sources):
        a = values[:, first * 128 : first * 128 + 128].astype(WIDE)
        b = values[:, second * 128 : second * 128 + 128].astype(WIDE)
        if half:
            a = pltpu.roll(a, 64, 1)
        else:
            b = pltpu.roll(b, 64, 1)
        out[:, at * 128 : at * 128 + 128] = jnp.where(low, a, b).astype(out.dtype)


def reorder(plan, values, outward, dtype):
    count, width = values.shape
    sizes = (plan.ns, plan.nb) if outward else (plan.nb, plan.ns)
    if width != plan.nb * plan.ns * 64 or sizes[0] % 2 or sizes[1] % 2:
        values = values.reshape(count, *sizes, width // (plan.nb * plan.ns))
        return values.transpose(0, 2, 1, 3).reshape(count, width).astype(dtype)
    sources = []
    for inner in range(sizes[1]):
        for outer in range(0, sizes[0], 2):
            at = outer * sizes[1] + inner
            sources.append((at // 2, (at + sizes[1]) // 2, at % 2))
    return pl.pallas_call(
        functools.partial(reorder_kernel, sources=sources),
        out_shape=jax.ShapeDtypeStruct(values.shape, dtype),
        compiler_params=pltpu.CompilerParams(vmem_limit_bytes=48 << 20),
        name="reorder",
    )(values)


def norm_stats(values):
    mean = jnp.mean(values, axis=-1, keepdims=True)
    center = values - mean
    return mean, lax.rsqrt(jnp.mean(center * center, axis=-1, keepdims=True) + EPSILON)


def spread_stats(plan, stats, count):
    mean, square = stats[0], stats[1]
    for step in bits(plan.nb):
        other = swap_over(jnp.stack([mean, square]), "batch", step, plan.nb)
        other = aligned(plan, other, step)
        gap = other[0] - mean
        mean = 0.5 * (mean + other[0])
        square = square + other[1] + gap * gap * (0.5 * count)
        count = 2 * count
    return jnp.stack([mean, lax.rsqrt(square / count + EPSILON)])


def spread_sums(plan, sums, count):
    for step in bits(plan.nb):
        sums = sums + aligned(plan, swap_over(sums, "batch", step, plan.nb), step)
    return sums / (count * plan.nb)


def norm_back(upstream, gain, unit, scale):
    scaled = upstream * gain
    first = jnp.mean(scaled, axis=-1, keepdims=True)
    second = jnp.mean(scaled * unit, axis=-1, keepdims=True)
    grad = scale * (scaled - first - unit * second)
    return grad, jnp.sum(upstream * unit, axis=0), jnp.sum(upstream, axis=0)


def xpos_tables(length):
    slot_pos = (jnp.arange(length, dtype=jnp.int32) - length // 2).astype(WIDE)
    lane = jnp.arange(128, dtype=jnp.int32)
    index = (lane % 32).astype(WIDE)
    angle = slot_pos[:, None] * jnp.exp(index * (-jnp.log(10000.0) / 32.0))[None, :]
    zeta = (index / 32.0 + 0.4) / 1.4
    growth = jnp.exp(slot_pos[:, None] * jnp.log(zeta)[None, :] / 512.0)
    cosine, sine = jnp.cos(angle), jnp.sin(angle)
    sine = jnp.where(lane % 64 < 32, -sine, sine)
    return cosine * growth, sine * growth, cosine / growth, sine / growth


def swap_halves(values):
    lane = lax.broadcasted_iota(jnp.int32, values.shape, 1)
    return jnp.where(lane % 64 < 32, pltpu.roll(values, 96, 1), pltpu.roll(values, 32, 1))


def matmul(a, b, contract):
    return lax.dot_general(a, b, ((contract[:1], contract[1:]), ((), ())), preferred_element_type=WIDE)


def as_column(row):
    return jnp.broadcast_to(row, (128, row.shape[1])).T[:, :1]


def as_row(column):
    return jnp.broadcast_to(column, (column.shape[0], 128)).T[:1]


def stat_rows(values):
    mean = jnp.mean(values, axis=-1, keepdims=True)
    center = values - mean
    square = jnp.sum(center * center, axis=-1, keepdims=True)
    return jnp.concatenate([as_row(mean), as_row(square)], axis=0)


def plain_end(acc, block, out):
    out[...] = acc


def gelu_end(acc, block, active_out, slope_out, stats_out):
    phi = 0.5 + 0.5 * lax.erf(acc * (0.5**0.5))
    active = acc * phi
    active_out[...] = active
    slope_out[...] = phi + acc * (jnp.exp(-0.5 * acc * acc) * ((2.0 * np.pi) ** -0.5))
    stats_out[...] = stat_rows(active)


def norm_back_end(acc, block, normal, stats, gain, bias, out, sums_out, vectors_out, low_out=None):
    out[...] = acc
    unit = (normal[...] - as_column(stats[0:1])) * as_column(stats[1:2])
    if low_out is not None:
        low_out[...] = (unit * gain[...] + bias[...]).astype(LOW)
    scaled = acc * gain[...]
    sums = [jnp.sum(scaled, axis=-1, keepdims=True), jnp.sum(scaled * unit, axis=-1, keepdims=True)]
    sums_out[...] = jnp.concatenate([as_row(sums[0]), as_row(sums[1])], axis=0)
    vectors = jnp.concatenate(
        [jnp.sum(acc * unit, axis=0, keepdims=True), jnp.sum(acc, axis=0, keepdims=True)], axis=0
    )

    @pl.when(block == 0)
    def _():
        vectors_out[...] = vectors

    @pl.when(block != 0)
    def _():
        vectors_out[...] += vectors


def pieces_kernel(*refs, moves, loads, step, n_arrays, n_weights, n_extra, keep, columns, end):
    arrays, weights = refs[:n_arrays], refs[n_arrays : n_arrays + n_weights]
    at = n_arrays + n_weights + n_extra
    extra = refs[n_arrays + n_weights : at]
    full, kept = refs[at], refs[at + 1] if keep else None
    outs = refs[at + 1 + keep : -6]
    rows, weight, arrived, left, loaded, stored = refs[-6:]
    block, count = pl.program_id(0), pl.num_programs(0)

    @pl.when(block == 0)
    def _():
        for index, column, row, n in loads:
            pltpu.make_async_copy(
                weights[index].at[:, pl.ds(column, weight.shape[1])],
                weight.at[pl.ds(row, n), :],
                loaded.at[0],
            ).start()
        for index, first, row, n in moves:
            pltpu.make_async_copy(
                arrays[index].at[pl.ds(first, n), :], rows.at[pl.ds(row, n), :], arrived.at[row // step]
            ).start()
        pltpu.make_async_copy(weight, weight, loaded.at[0]).wait()
        if keep:
            pltpu.make_async_copy(weight, kept, stored.at[0]).start()

    here = pl.ds(pl.multiple_of(block * step, step), step)
    pltpu.make_async_copy(rows.at[here], rows.at[here], arrived.at[block]).wait()
    pltpu.make_async_copy(rows.at[here], full.at[here], left.at[block]).start()
    acc = matmul(rows[here, :], weight[:, :columns], (1, 0))
    end(acc, block, *extra, *outs)

    @pl.when(block == count - 1)
    def _():
        for i in range(rows.shape[0] // step):
            part = pl.ds(i * step, step)
            pltpu.make_async_copy(rows.at[part], full.at[part], left.at[i]).wait()
        if keep:
            pltpu.make_async_copy(weight, kept, stored.at[0]).wait()


def moves_of(arrays, step):
    moves, total = [], 0
    for index, array in enumerate(arrays):
        for first in range(0, array.shape[0], step):
            n = min(step, array.shape[0] - first)
            moves.append((index, first, total, n))
            total += n
    return moves, total


def pieces_matmul(arrays, weights, columns, end, extra, outs, name):
    step = 2 * ROWS_AT_ONCE
    moves, total = moves_of(arrays, step)
    loads, inner = [], 0
    for index, weight in enumerate(weights):
        loads.append((index, columns[0], inner, weight.shape[0]))
        inner += weight.shape[0]
    keep = len(weights) > 1

    def spec(shape, kind):
        if kind == "rows":
            return pl.BlockSpec((step, shape[1]), lambda i: (i, 0))
        if kind == "lanes":
            return pl.BlockSpec((shape[0], step), lambda i: (0, i))
        return pl.BlockSpec(shape, lambda i: (0, 0))

    anywhere = pl.BlockSpec(memory_space=pl.ANY)
    kept = [jax.ShapeDtypeStruct((inner, columns[1]), LOW)] if keep else []
    return pl.pallas_call(
        functools.partial(
            pieces_kernel,
            moves=moves,
            loads=loads,
            step=step,
            n_arrays=len(arrays),
            n_weights=len(weights),
            n_extra=len(extra),
            keep=int(keep),
            columns=columns[2],
            end=end,
        ),
        grid=(total // step,),
        in_specs=[anywhere] * (len(arrays) + len(weights))
        + [spec(array.shape, kind) for array, kind in extra],
        out_specs=[anywhere] * (1 + keep) + [spec(*out[:2]) for out in outs],
        out_shape=[jax.ShapeDtypeStruct((total, inner), LOW)]
        + kept
        + [jax.ShapeDtypeStruct(out[0], out[2] if len(out) > 2 else WIDE) for out in outs],
        scratch_shapes=[
            pltpu.VMEM((total, inner), LOW),
            pltpu.VMEM((inner, columns[1]), LOW),
            pltpu.SemaphoreType.DMA((total // step,)),
            pltpu.SemaphoreType.DMA((total // step,)),
            pltpu.SemaphoreType.DMA((1,)),
            pltpu.SemaphoreType.DMA((1,)),
        ],
        compiler_params=pltpu.CompilerParams(vmem_limit_bytes=56 << 20),
        name=name,
    )(*arrays, *weights, *[array for array, _ in extra])


def mixed_left(values, stats, gain, bias):
    unit = (values[...] - as_column(stats[0:1])) * as_column(stats[1:2])
    return (unit * gain[...] + bias[...]).astype(LOW)


def hidden_left(grad, active, slope, stats, sums, gain):
    scale = as_column(stats[1:2])
    unit = (active[...] - as_column(stats[0:1])) * scale
    back = grad[...] * gain[...] - as_column(sums[0:1]) - unit * as_column(sums[1:2])
    return (scale * back * slope[...]).astype(LOW)


def plain_left(values):
    return values[...]


def part_kernel(*refs, n_in, make_left, keeps, ends):
    n_more = len(ends[1])
    left = make_left(*refs[:n_in])
    acc = matmul(left, refs[n_in][...], (1, 1))
    more, outs = refs[n_in + 1 : n_in + 1 + n_more], refs[n_in + 1 + n_more :]
    if keeps:
        outs[0 if ends[2] else 1][...] = left
        outs = outs[1:] if ends[2] else outs[2:]
    ends[0](acc, pl.program_id(0), *more, *outs)


def other_end(acc, block, *outs):
    if len(outs) == 1:
        outs[0][...] = acc.astype(LOW)
        return
    for i, out in enumerate(outs):

        @pl.when(block == i)
        def _(out=out):
            out[...] = acc.astype(LOW)


def own_x_end(acc, block, from_x, from_far, over_x, far_y, at_x):
    slots, half = at_x.shape

    @pl.when(block == 0)
    def _():
        total = acc + from_x[...].astype(WIDE)
        over_x[slots:] = total[:, :half].astype(LOW)
        at_x[...] = total[:, half:]

    @pl.when(block == 1)
    def _():
        total = acc + from_far[...].astype(WIDE)
        over_x[:slots] = total[:, :half].astype(LOW)
        far_y[...] = total[:, half:].astype(LOW)


def own_y_end(acc, block, from_near, from_y, over_y, near, at_y):
    half = at_y.shape[1]

    @pl.when(block == 0)
    def _():
        near[...] = acc + from_near[...].astype(WIDE)

    @pl.when(block == 1)
    def _():
        total = acc + from_y[...].astype(WIDE)
        over_y[...] = total[:, half:].astype(LOW)
        at_y[...] = total[:, :half]


def part_call(ins, weight, columns, make_left, kept, at, blocks, end, more, outs, name):
    step = ROWS_AT_ONCE
    total = next(array.shape[0] for array, kind in ins if kind == "rows")
    rows = weight.shape[0]

    def spec(array, kind):
        if kind == "rows":
            return pl.BlockSpec((step, array.shape[1]), lambda i: (at(i), 0))
        if kind == "lanes":
            return pl.BlockSpec((array.shape[0], step), lambda i: (0, at(i)))
        return pl.BlockSpec(array.shape, lambda i: (0, 0))

    once = pl.Buffered(1)
    in_specs = [spec(*item) for item in ins]
    in_specs.append(
        pl.BlockSpec((rows, columns[0]), lambda i: (0, columns[1]), pipeline_mode=once)
    )
    in_specs += [pl.BlockSpec(m.shape, lambda i: (0, 0), pipeline_mode=once) for m in more]
    operands = [array for array, _ in ins] + [weight, *more]
    out_specs, out_shape, aliases = [], [], {}
    if kept is not None:
        if kept:
            aliases[len(operands)] = 0
            in_specs.append(pl.BlockSpec(memory_space=pl.ANY))
            operands += kept
        out_specs.append(pl.BlockSpec((step, columns[0]), lambda i: (at(i), 0)))
        out_shape.append(jax.ShapeDtypeStruct((total, columns[0]), LOW))
    for shape, dtype, moves in outs:
        out_specs.append(pl.BlockSpec((step if moves else shape[0], shape[1]), lambda i, m=moves: (i if m else 0, 0)))
        out_shape.append(jax.ShapeDtypeStruct(shape, dtype))
    return pl.pallas_call(
        functools.partial(
            part_kernel,
            n_in=len(ins),
            make_left=make_left,
            keeps=kept is not None,
            ends=(end, more, not kept),
        ),
        grid=(blocks,),
        in_specs=in_specs,
        out_specs=out_specs,
        out_shape=out_shape,
        input_output_aliases=aliases,
        compiler_params=pltpu.CompilerParams(vmem_limit_bytes=56 << 20),
        name=name,
    )(*operands)


def block_parts(plan, ins, weight, columns, make_left, keeps, name):
    step, rows = ROWS_AT_ONCE, weight.shape[0]
    left = [] if keeps else None

    def call(at, blocks, end, more, outs, name):
        return part_call(ins, weight, columns, make_left, left, at, blocks, end, more, outs, name)

    if not plan.fast:
        total = next(array.shape[0] for array, kind in ins if kind == "rows")
        outs = [((total, rows), LOW, True)]
        return call(lambda i: i, total // step, other_end, [], outs, name)
    half = rows // 2
    outs = [((step, rows), LOW, False)] * 4
    outs = call(lambda i: 4 + i, 4, other_end, [], outs, name + "_other")
    if keeps:
        left = [outs[0]]
    near, at_x, at_y, far = outs[int(keeps) :]
    others = [swap_over(part, "batch", 1, 8) for part in (at_x, far, near, at_y)]
    outs = [((2 * step, half), LOW, False), ((step, half), LOW, False), ((step, half), WIDE, False)]
    outs = call(lambda i: 1 + 2 * i, 2, own_x_end, others[:2], outs, name + "_own_x")
    if keeps:
        left = [outs[0]]
    over_x, far_y, at_x = outs[int(keeps) :]
    outs = [((step, half), LOW, False), ((step, rows), WIDE, False), ((step, half), WIDE, False)]
    outs = call(lambda i: 2 * i, 2, own_y_end, others[2:], outs, name + "_own_y")
    if keeps:
        left = [outs[0]]
    over_y, near, at_y = outs[int(keeps) :]
    return *(left or []), (over_x, far_y, over_y, near, at_x, at_y)


def fill_bias(bias, valid, seg_row, seg_col, length):
    for i in range(length // STRIPE):
        low, high = i * STRIPE, (i + 1) * STRIPE
        shape = (STRIPE, high)
        query = lax.broadcasted_iota(jnp.int32, shape, 0) + low
        key = lax.broadcasted_iota(jnp.int32, shape, 1)
        same = seg_col[low:high] == seg_row[:, :high]
        allowed = (key == query) | (same & (key <= query) & (query < valid))
        bias[low:high, :high] = jnp.where(allowed, 0.0, -1e30)


def attend_kernel(
    info, proj, cos_q, sin_q, cos_k, sin_k, seg_row, seg_col, qkv, attended, log_total, stats, bias,
    *, ns, slots, hd
):
    row, head = pl.program_id(0), pl.program_id(1)
    length = ns * slots

    def place(quarter):
        return pl.multiple_of(info[row, quarter] * slots, slots)

    @pl.when(head == 0)
    def _():
        for q in range(ns):
            source, low, high = place(q), q * slots, (q + 1) * slots
            for part, (cosine, sine) in enumerate(((cos_q, sin_q), (cos_k, sin_k))):
                cosine, sine = cosine[low:high], sine[low:high]
                for pair in range(hd // 128):
                    at = part * hd + pair * 128
                    values = proj[pl.ds(source, slots), at : at + 128]
                    turned = values * cosine + swap_halves(values) * sine
                    qkv[low:high, at : at + 128] = turned.astype(LOW)
            qkv[low:high, 2 * hd :] = proj[pl.ds(source, slots), 2 * hd :].astype(LOW)
        fill_bias(bias, info[row, ns], seg_row[...], seg_col[...], length)
        log_total[...] = jnp.zeros_like(log_total)

    mine = lax.broadcasted_iota(jnp.int32, (STRIPE, hd), 1) // HEAD == head
    column = lax.broadcasted_iota(jnp.int32, (STRIPE, 128), 1) == head
    for i in range(length // STRIPE):
        low, high = i * STRIPE, (i + 1) * STRIPE
        queries = jnp.where(mine, qkv[low:high, :hd] * 0.125, jnp.zeros((), LOW))
        scores = matmul(queries, qkv[:high, hd : 2 * hd], (1, 1)) + bias[low:high, :high]
        top = jnp.max(scores, axis=-1, keepdims=True)
        weight = jnp.exp(scores - top)
        total = jnp.sum(weight, axis=-1, keepdims=True)
        summed = matmul(weight.astype(LOW), qkv[:high, 2 * hd :], (1, 0)) / total
        log_total[low:high] = jnp.where(column, top + jnp.log(total), log_total[low:high])
        for u in range(STRIPE // slots):
            to = place(i * (STRIPE // slots) + u)
            rows = slice(u * slots, (u + 1) * slots)
            attended[pl.ds(to, slots), :] = jnp.where(
                mine[rows], summed[rows], attended[pl.ds(to, slots), :]
            )

    @pl.when(head == pl.num_programs(1) - 1)
    def _():
        for q in range(ns):
            here = slice(q * slots, (q + 1) * slots)
            stats[:, here] = stat_rows(attended[here])


def attend_back_kernel(
    info, qkv, attended, grad, stats, sums, gain, log_total, cos_q, sin_q, cos_k, sin_k, seg_row, seg_col, out,
    bias, grad_low, product, grad_q, grad_k, grad_v, *, ns, slots, hd
):
    row, head = pl.program_id(0), pl.program_id(1)
    length = ns * slots

    def place(quarter):
        return pl.multiple_of(info[row, quarter] * slots, slots)

    @pl.when(head == 0)
    def _():
        for q in range(ns):
            to, low, high = place(q), q * slots, (q + 1) * slots
            values = attended[low:high]
            scale = as_column(stats[1:2, low:high])
            unit = (values - as_column(stats[0:1, low:high])) * scale
            back = grad[low:high] * gain[...] - as_column(sums[0:1, low:high])
            back = scale * (back - unit * as_column(sums[1:2, low:high]))
            grad_low[pl.ds(to, slots), :] = back.astype(LOW)
            product[pl.ds(to, slots), :] = back * values
        fill_bias(bias, info[row, ns], seg_row[...], seg_col[...], length)
        for total in (grad_q, grad_k, grad_v):
            total[...] = jnp.zeros_like(total)

    mine = lax.broadcasted_iota(jnp.int32, (STRIPE, hd), 1) // HEAD == head
    column = lax.broadcasted_iota(jnp.int32, (STRIPE, 128), 1) == head
    nothing = jnp.zeros((), LOW)
    mine_all = lax.broadcasted_iota(jnp.int32, (length, hd), 1) // HEAD == head
    keys_mine = jnp.where(mine_all, qkv[:, hd : 2 * hd], nothing)
    for i in range(length // STRIPE):
        low, high = i * STRIPE, (i + 1) * STRIPE
        queries = jnp.where(mine, qkv[low:high, :hd] * 0.125, nothing)
        upstream = jnp.where(mine, grad_low[low:high], nothing)
        delta = jnp.sum(jnp.where(mine, product[low:high], 0.0), axis=-1, keepdims=True)
        log_sum = jnp.sum(jnp.where(column, log_total[low:high], 0.0), axis=-1, keepdims=True)
        scores = matmul(queries, qkv[:high, hd : 2 * hd], (1, 1)) + bias[low:high, :high]
        prob = jnp.exp(scores - log_sum)
        grad_prob = matmul(upstream, qkv[:high, 2 * hd :], (1, 1))
        grad_s = (prob * (grad_prob - delta)).astype(LOW)
        grad_q[low:high] += matmul(grad_s, keys_mine[:high], (1, 0))
        grad_k[:high] += matmul(grad_s, queries, (0, 0))
        grad_v[:high] += matmul(prob.astype(LOW), upstream, (0, 0))

    @pl.when(head == pl.num_programs(1) - 1)
    def _():
        for q in range(ns):
            target, low, high = place(q), q * slots, (q + 1) * slots
            tables = (cos_q, sin_q, grad_q, 0.125), (cos_k, sin_k, grad_k, 1.0)
            for part, (cosine, sine, total, scale) in enumerate(tables):
                cosine, sine = cosine[low:high] * scale, sine[low:high] * scale
                for pair in range(hd // 128):
                    values = total[low:high, pair * 128 : pair * 128 + 128]
                    turned = values * cosine - swap_halves(values) * sine
                    at = part * hd + pair * 128
                    out[pl.ds(target, slots), at : at + 128] = turned.astype(LOW)
            out[pl.ds(target, slots), 2 * hd :] = grad_v[low:high].astype(LOW)


def row_block(length, width):
    return pl.BlockSpec((length, width), lambda r, h, info: (r, 0))


def shared_block(length, width):
    return pl.BlockSpec((length, width), lambda r, h, info: (0, 0))


def attend(plan, info, proj, tables, segments):
    count, width = proj.shape
    length, hd = count // plan.rows, width // 3
    slots = length // plan.ns
    return pl.pallas_call(
        functools.partial(attend_kernel, ns=plan.ns, slots=slots, hd=hd),
        grid_spec=pltpu.PrefetchScalarGridSpec(
            num_scalar_prefetch=1,
            grid=(plan.rows, hd // HEAD),
            in_specs=[
                row_block(length, width),
                *[shared_block(length, 128)] * 4,
                pl.BlockSpec((None, 1, length), lambda r, h, info: (r, 0, 0)),
                pl.BlockSpec((None, length, 1), lambda r, h, info: (r, 0, 0)),
            ],
            out_specs=[
                row_block(length, width),
                row_block(length, hd),
                row_block(length, 128),
                pl.BlockSpec((2, length), lambda r, h, info: (0, r)),
            ],
            scratch_shapes=[pltpu.VMEM((length, length), WIDE)],
        ),
        out_shape=[
            jax.ShapeDtypeStruct((count, width), LOW),
            jax.ShapeDtypeStruct((count, hd), WIDE),
            jax.ShapeDtypeStruct((count, 128), WIDE),
            jax.ShapeDtypeStruct((2, count), WIDE),
        ],
        compiler_params=pltpu.CompilerParams(vmem_limit_bytes=48 << 20),
        name="attend",
    )(info, proj, *tables, segments[:, None, :], segments[:, :, None])


def attend_back(plan, info, qkv, attended, grad, stats, sums, gain, log_total, tables, segments):
    count, width = qkv.shape
    length, hd = count // plan.rows, width // 3
    slots = length // plan.ns
    return pl.pallas_call(
        functools.partial(attend_back_kernel, ns=plan.ns, slots=slots, hd=hd),
        grid_spec=pltpu.PrefetchScalarGridSpec(
            num_scalar_prefetch=1,
            grid=(plan.rows, hd // HEAD),
            in_specs=[
                row_block(length, width),
                row_block(length, hd),
                row_block(length, hd),
                pl.BlockSpec((2, length), lambda r, h, info: (0, r)),
                pl.BlockSpec((2, length), lambda r, h, info: (0, r)),
                shared_block(1, hd),
                row_block(length, 128),
                *[shared_block(length, 128)] * 4,
                pl.BlockSpec((None, 1, length), lambda r, h, info: (r, 0, 0)),
                pl.BlockSpec((None, length, 1), lambda r, h, info: (r, 0, 0)),
            ],
            out_specs=row_block(length, width),
            scratch_shapes=[
                pltpu.VMEM((length, length), WIDE),
                pltpu.VMEM((length, hd), LOW),
                pltpu.VMEM((length, hd), WIDE),
                pltpu.VMEM((length, hd), WIDE),
                pltpu.VMEM((length, hd), WIDE),
                pltpu.VMEM((length, hd), WIDE),
            ],
        ),
        out_shape=jax.ShapeDtypeStruct((count, width), LOW),
        compiler_params=pltpu.CompilerParams(vmem_limit_bytes=48 << 20),
        name="attend_back",
    )(
        info, qkv, attended, grad, stats, sums, gain, log_total, *tables,
        segments[:, None, :], segments[:, :, None],
    )


def shards(
    plan,
    tokens,
    segments,
    valid_count,
    cotangent,
    w_qkv,
    w_out,
    w_up,
    w_down,
    gain_attn,
    bias_attn,
    gain_mix,
    bias_mix,
    gain_ffn,
    bias_ffn,
    gain_hidden,
    bias_hidden,
):
    nb, ns = plan.nb, plan.ns
    width, slots, length = tokens.shape[2], tokens.shape[1], segments.shape[1]
    hd, hidden_part = width // nb, w_up.shape[1] // nb
    batch_index, seq_index = lax.axis_index("batch"), lax.axis_index("seq")
    entry = lax.dynamic_index_in_dim(
        jnp.asarray(plan.table), batch_index * ns + seq_index, 0, keepdims=False
    )

    tokens_low = reorder(plan, tokens[0], False, LOW)
    group = w_qkv.reshape(w_qkv.shape[0], 3, nb, hd).transpose(2, 0, 1, 3)
    group = group.reshape(nb, -1, 3 * hd)
    attn_own = jnp.concatenate([group, split_columns(plan, w_out.T)], axis=2)
    tokens_low, attn_own = sync(tokens_low, attn_own)
    attn_own = exchange(attn_own)
    qkv_w = gather_layers(attn_own[:, :, : 3 * hd])
    tokens_low = lax.ppermute(tokens_low, BOTH, plan.there)

    own_params = (gain_attn, bias_attn, gain_mix, bias_mix, gain_ffn, bias_ffn, gain_hidden, bias_hidden)
    tokens_low, cotangent, attn_own, *own_params = sync(tokens_low, cotangent, attn_own, *own_params)
    params = gather_over(jnp.concatenate([p.astype(WIDE) for p in own_params]), "seq", ns)
    packed = jnp.concatenate(
        [params.reshape(-1), segments[0].astype(WIDE), valid_count.astype(WIDE)]
    )
    packed = gather_over(packed, "batch", nb)
    spread = packed[:, : params.size].reshape(nb, ns, -1)
    vectors, at = [], 0
    for index, p in enumerate(own_params):
        piece = spread[:, :, at : at + p.shape[0]]
        at += p.shape[0]
        if index in (0, 1, 4, 5):
            vectors.append(piece.transpose(1, 0, 2).reshape(1, -1))
        else:
            vectors.append(lax.dynamic_index_in_dim(piece, batch_index, 0, False).reshape(1, -1))
    ga, ba, gm, bm, gf, bf, gh, bh = vectors
    count = plan.rows * length
    resid = tokens_low.astype(WIDE)
    mean_attn, scale_attn = norm_stats(resid)
    unit_attn = (resid - mean_attn) * scale_attn
    normed_low = (unit_attn * ga + ba).astype(LOW)
    normed_low, packed, cotangent, w_up, w_down, gm, bm, gf, bf, gh, bh = sync(
        normed_low, packed, cotangent, w_up, w_down, gm, bm, gf, bf, gh, bh
    )

    near = gather_near(plan, normed_low)
    ffn_own = jnp.concatenate([split_columns(plan, w) for w in (w_up, w_down.T)], axis=2)
    slot = seq_index * slots + jnp.arange(slots, dtype=jnp.int32)
    living = (slot < valid_count[0])[:, None]
    grad_low = reorder(plan, jnp.where(living, cotangent[0], jnp.zeros((), LOW)), False, LOW)
    layer_rows = jnp.concatenate(
        [
            lax.dynamic_slice_in_dim(packed[:, params.size :], entry[r], 1, 0)
            for r in range(plan.rows)
        ]
    ).astype(jnp.int32)
    seg_rows = layer_rows[:, :length]
    info = jnp.concatenate(
        [entry[plan.rows :].reshape(plan.rows, ns), layer_rows[:, length:]], axis=1
    )
    out_own = attn_own[:, :, 3 * hd :]
    ffn_own, grad_low, seg_rows, info, out_own, near = sync(
        ffn_own, grad_low, seg_rows, info, out_own, near
    )
    out_wt = gather_layers(out_own)
    tables = xpos_tables(length)
    grad_low, ffn_own, tables, arrays = sync(grad_low, ffn_own, tables, gather_far(plan, near))
    ffn_own = exchange(ffn_own)
    grad_low = lax.ppermute(grad_low, BOTH, plan.there)
    normed, projected = pieces_matmul(
        arrays,
        [qkv_w],
        (0, 3 * hd, 3 * hd),
        plain_end,
        [],
        [((count, 3 * hd), "rows")],
        "project",
    )
    qkv, attended, log_total, stats_mix = attend(plan, info, projected, tables, seg_rows)
    stats_mix, grad_low, ffn_own = sync(stats_mix, grad_low, ffn_own)
    up_w = gather_layers(ffn_own[:, :, :hidden_part])
    down_wt = gather_layers(ffn_own[:, :, hidden_part:])
    stats_mix = spread_stats(plan, stats_mix, hd)
    mixed, kept = block_parts(
        plan,
        [(attended, "rows"), (stats_mix, "lanes"), (gm, "whole"), (bm, "whole")],
        out_wt,
        (hd, 0),
        mixed_left,
        True,
        "out",
    )
    state, _ = reduce_first(plan, kept)
    resid_mid = resid + reduce_last(plan, state)

    mean_ffn, scale_ffn = norm_stats(resid_mid)
    unit_ffn = (resid_mid - mean_ffn) * scale_ffn
    near = sync(*gather_near(plan, (unit_ffn * gf + bf).astype(LOW)))
    grad_later, *arrays = sync(grad_low, *gather_far(plan, near))
    grad_near = gather_near(plan, grad_later)
    ffn_in, active, slope, stats_hid = pieces_matmul(
        arrays,
        [up_w],
        (0, hidden_part, hidden_part),
        gelu_end,
        [],
        [((count, hidden_part), "rows"), ((count, hidden_part), "rows"), ((2, count), "lanes")],
        "up",
    )
    stats_hid, *grad_near = sync(stats_hid, *grad_near)
    grad_arrays = gather_far(plan, grad_near)
    stats_hid = spread_stats(plan, stats_hid, hidden_part)

    grad_all, grad_hn, sums_hid, vectors_hid, hidden_low = pieces_matmul(
        grad_arrays,
        [down_wt],
        (0, hidden_part, hidden_part),
        norm_back_end,
        [(active, "rows"), (stats_hid, "lanes"), (gh, "whole"), (bh, "whole")],
        [
            ((count, hidden_part), "rows"),
            ((2, count), "lanes"),
            ((2, hidden_part), "whole"),
            ((count, hidden_part), "rows", LOW),
        ],
        "down_back",
    )
    grad_down = matmul(grad_all, hidden_low, (0, 0)).astype(LOW)
    sums_hid = spread_sums(plan, sums_hid, hidden_part)
    sums_hid, grad_down = sync(sums_hid, grad_down)
    grad_down = scatter_layers(plan, grad_down)
    grad_hidden, kept = block_parts(
        plan,
        [
            (grad_hn, "rows"), (active, "rows"), (slope, "rows"),
            (stats_hid, "lanes"), (sums_hid, "lanes"), (gh, "whole"),
        ],
        up_w,
        (hidden_part, 0),
        hidden_left,
        True,
        "up_back",
    )
    grad_up = matmul(ffn_in, grad_hidden, (0, 0)).astype(LOW)
    state, (grad_up, hidden_low) = reduce_first(plan, kept, grad_up, hidden_low)
    grad_up = scatter_layers(plan, grad_up)
    grad_ffn_in = reduce_last(plan, state)
    grad_mid, gain_ffn_part, bias_ffn_part = norm_back(grad_ffn_in, gf, unit_ffn, scale_ffn)
    grad_mid = grad_mid + grad_low.astype(WIDE)
    (kept,) = block_parts(
        plan,
        [(hidden_low, "rows")],
        down_wt,
        (hidden_part, 0),
        plain_left,
        False,
        "down",
    )
    kept, near = sync(kept, gather_near(plan, grad_mid.astype(LOW)))
    arrays = sync(*gather_far(plan, near))
    grad_down, arrays = sync(grad_down, arrays)
    grad_down = exchange(grad_down)
    mid_all, grad_mixed, sums_mix, vectors_mix = pieces_matmul(
        arrays,
        [out_wt],
        (0, hd, hd),
        norm_back_end,
        [(attended, "rows"), (stats_mix, "lanes"), (gm, "whole"), (bm, "whole")],
        [((count, hd), "rows"), ((2, count), "lanes"), ((2, hd), "whole")],
        "out_back",
    )
    sums_mix, grad_down = sync(sums_mix, grad_down)
    grad_out = matmul(mid_all, mixed, (0, 0)).astype(LOW)
    sums_mix = spread_sums(plan, sums_mix, hd)
    sums_mix, grad_out, grad_up, kept = sync(sums_mix, grad_out, grad_up, kept)
    grad_out = scatter_layers(plan, grad_out)
    grad_proj = attend_back(
        plan, info, qkv, attended, grad_mixed, stats_mix, sums_mix, gm, log_total, tables, seg_rows
    )
    vectors = jnp.concatenate([vectors_mix, vectors_hid], axis=1)
    for step in bits(ns)[:1]:
        vectors = vectors + swap_over(vectors, "seq", step, ns)
    state, (grad_proj, vectors) = reduce_first(plan, kept, grad_proj, vectors)
    grad_qkv = matmul(normed, grad_proj, (0, 0)).astype(LOW)
    grad_proj, grad_qkv, grad_up, grad_out = sync(grad_proj, grad_qkv, exchange(grad_up), grad_out)
    grad_qkv = scatter_layers(plan, grad_qkv)
    output = (resid_mid + reduce_last(plan, state)).astype(LOW)
    (kept,) = block_parts(
        plan, [(grad_proj, "rows")], qkv_w, (3 * hd, 0), plain_left, False, "project_back"
    )
    for step in bits(ns)[1:]:
        vectors = vectors + swap_over(vectors, "seq", step, ns)
    state, (output, vectors) = reduce_first(plan, kept, output, vectors)
    output = lax.ppermute(output, BOTH, plan.back)
    grad_normed = reduce_last(plan, state)
    grad_resid, gain_attn_part, bias_attn_part = norm_back(
        grad_normed, ga, unit_attn, scale_attn
    )
    whole = jnp.stack([gain_ffn_part, bias_ffn_part, gain_attn_part, bias_attn_part])
    whole = sum_over(whole, "seq", ns)
    whole = whole.reshape(4, ns, nb, -1).transpose(2, 0, 1, 3).reshape(nb, 1, 4 * hd)
    grad_tokens, grad_qkv, whole = sync((grad_mid + grad_resid).astype(LOW), grad_qkv, whole)
    grad_tokens = lax.ppermute(grad_tokens, BOTH, plan.back)
    attn_grads = jnp.concatenate([grad_qkv, grad_out], axis=2)
    rows = attn_grads.shape[1]
    whole = jnp.broadcast_to(whole.astype(LOW), (nb, 16, 4 * hd))
    attn_grads = exchange(jnp.concatenate([attn_grads, whole], axis=1))
    own = jnp.sum(attn_grads[:, rows].astype(WIDE), axis=0).reshape(4, ns, -1)
    own = lax.dynamic_index_in_dim(own, seq_index, 1, False)
    grad_qkv, grad_out = attn_grads[:, :rows, : 3 * hd], attn_grads[:, :rows, 3 * hd :]
    mixes = lax.dynamic_index_in_dim(vectors[:, :hd].reshape(2, ns, -1), seq_index, 1, False)
    hiddens = lax.dynamic_index_in_dim(vectors[:, hd:].reshape(2, ns, -1), seq_index, 1, False)
    grad_qkv = grad_qkv.reshape(nb, -1, 3, hd).transpose(1, 2, 0, 3).reshape(w_qkv.shape)
    grad_qkv, grad_out = grad_qkv.astype(WIDE), join_columns(plan, grad_out).astype(WIDE).T
    grad_up = join_columns(plan, grad_up).astype(WIDE)
    grad_down = join_columns(plan, grad_down).astype(WIDE).T
    output = reorder(plan, output, True, LOW)
    grad_tokens, own, mixes, hiddens, grad_qkv, grad_out, grad_up, grad_down, output = sync(
        grad_tokens, own, mixes, hiddens, grad_qkv, grad_out, grad_up, grad_down, output
    )
    return (
        output[None],
        reorder(plan, grad_tokens, True, WIDE)[None],
        grad_qkv,
        grad_out,
        grad_up,
        grad_down,
        own[2],
        own[3],
        mixes[0],
        mixes[1],
        own[0],
        own[1],
        hiddens[0],
        hiddens[1],
    )


def solution(mesh):
    plan = Plan(mesh.shape["batch"], mesh.shape["seq"])
    rows = P("batch", "seq", None)
    over_rows, over_columns, vector = P(BOTH, None), P(None, BOTH), P(BOTH)
    return jax.shard_map(
        functools.partial(shards, plan),
        mesh=mesh,
        in_specs=(rows, P("batch", None), P("batch"), rows)
        + (over_rows, over_columns, over_rows, over_columns)
        + (vector,) * 8,
        out_specs=(rows, rows, over_rows, over_columns, over_rows, over_columns) + (vector,) * 8,
        check_vma=False,
    )
```
